128 devices in a mesh: req: 8 (over x, core), exp: 16 (over y, z).
Axes of the slice: x: 4, y: 4, z: 4, core: 2. Of those that a mesh axis runs over, the one named last changes fastest.
Arguments:
- queries: bfloat16 [8192, 2048], P('req', 'exp'), may hold values from -6 to 6
- keys: bfloat16 [8192, 2048], P('req', 'exp'), may hold values from -15 to 15
- values: bfloat16 [8192, 2048], P('req', 'exp'), may hold values from -6 to 6
- prefix_keys: bfloat16 [4, 4096, 2048], P(None, 'req', 'exp'), may hold values from -15 to 15
- prefix_values: bfloat16 [4, 4096, 2048], P(None, 'req', 'exp'), may hold values from -6 to 6
- lengths: int32 [8, 8], P('req'), may hold values from 1 to 512, 1024 in all within a row
- groups: int32 [8, 8], P('req'), may hold values from 0 to 3
- residual: bfloat16 [8192, 2048], P(('req', 'exp')), may hold values from -6 to 6
- out_proj: bfloat16 [2048, 2048], P('exp'), may hold values from -0.125 to 0.125
- norm_gain: bfloat16 [2048], replicated, may hold values from 0.099609375 to 1.8984375
- expert_ids: int32 [8192, 4], P(('req', 'exp')), may hold values from 0 to 31, all different within a row; in each aligned block of 64 rows (0 to 63, 64 to 127, ...) at most 16 rows name the same one
- expert_gates: bfloat16 [8192, 4], P(('req', 'exp')), may hold values from 0.049804688 to 0.5
- w_gate: bfloat16 [32, 2048, 704], P('exp'), may hold values from -0.125 to 0.125
- w_up: bfloat16 [32, 2048, 704], P('exp'), may hold values from -0.125 to 0.125
- w_down: bfloat16 [32, 704, 2048], P('exp'), may hold values from -0.21875 to 0.21875
Outputs:
- layer_out: bfloat16 [8192, 2048], P(('req', 'exp'))
The draws below stay inside these ranges and needn't reach their ends.
Inputs may be any that keep to these rules, and one draw needn't show every extreme that they name: The 8 lengths of a row sum to 1024; the longest request of each row has half of 1024 tokens. `expert_ids`: each row names 4 different experts. Among the 64 tokens of one device, no expert is named more than 16 times; on some device some expert is named exactly 16 times.
All inputs are finite; a program needn't handle non-finite values.
Results may differ from the reference program's by a relative error of at most 0.02.
Values may be sent and summed in bfloat16 or wider, within the bound.
A program may use at most 256 MiB of HBM per device.

```python
import math
import jax
import jax.numpy as jnp
import numpy as np
from jax import lax

D = 2048
HEADS = 16
HEAD = 128
TOPK = 4
EXPERTS = 32
FE = 704
G = 4
RQ = 8
PREF = 4096
ROW_TOK = 1024
TOKENS = 8192
TOK_DEV = 64
CAP = 16
N_REQ = 8


def draw_queries(key, part):
    drawn = jnp.clip(jax.random.normal(jax.random.fold_in(key, 11), (TOKENS, D), jnp.float32), -5.5, 5.5)
    return drawn.astype(jnp.bfloat16)


def draw_prefix_keys(key, part):
    drawn = jnp.clip(2.5 * jax.random.normal(jax.random.fold_in(key, 23), (G, PREF, D), jnp.float32), -15.0, 15.0)
    return drawn.astype(jnp.bfloat16)


def set_ends(result, own_key, smallest, largest):
    longest = result.shape.index(max(result.shape))
    spots = []
    for shift in (0, 1):
        where = [jax.random.randint(jax.random.fold_in(own_key, axis), (), 0, length) for axis, length in enumerate(result.shape)]
        where[longest] = (where[longest] + shift) % result.shape[longest]
        spots.append(tuple(where))
    return result.at[spots[0]].set(smallest).at[spots[1]].set(largest)


def shard_levels(key, dims, pieces, smallest, high):
    factor_of, own = 1.0, jax.random.fold_in(key, 6)
    for dim, blocks in pieces:
        steps = jnp.exp(jax.random.uniform(jax.random.fold_in(own, dim), (blocks,), jnp.float32, smallest / len(pieces), high / len(pieces)))
        factor_of = factor_of * jnp.repeat(steps, dims[dim] // blocks).reshape([-1 if axis == dim else 1 for axis in range(len(dims))])
    return factor_of


def split_up(amount, total, reach, skew):
    weights = [(1 << 20) // math.isqrt(standing ** skew) + 1 for standing in range(2, amount + 1)]
    rest, given = total - reach - (amount - 1), [1] * (amount - 1)
    while rest > 0:
        candidates = [i for i in range(amount - 1) if given[i] < reach]
        pool, budget = sum([weights[i] for i in candidates]), rest
        for i in candidates:
            extra = min(reach - given[i], max(1, budget * weights[i] // pool), rest)
            given[i] = given[i] + extra
            rest = rest - extra
    return np.array([reach] + given)


def ragged_sizes(rng, amount, total, bound, lean):
    if amount == 2:
        one = jax.random.randint(rng, (), max(1, total - bound), min(bound, total - 1) + 1)
        return jnp.stack([one, total - one])
    tallies = jnp.asarray(split_up(amount, total, bound, lean), jnp.int32)
    couples = (amount - 1) // 2
    giver, taker = tallies[1:1 + 2 * couples:2], tallies[2:2 + 2 * couples:2]
    slack = jnp.minimum(giver - 1, bound - taker)
    shifted = jax.random.randint(jax.random.fold_in(rng, 1), (couples,), 0, 1 << 20) % (slack + 1)
    tallies = tallies.at[1:1 + 2 * couples:2].set(giver - shifted).at[2:2 + 2 * couples:2].set(taker + shifted)
    return tallies[jax.random.permutation(jax.random.fold_in(rng, 2), amount)]


def shared_out(rng, own, number, rows, number_of, top, limit, slope):
    order = jax.random.permutation(rng, number_of)
    heavy_load, usual = load_shares(number_of, rows * top, limit, slope, True), load_shares(number_of, rows * top, limit, slope, False)
    places = jnp.arange(number_of)

    def named(sizes, rotation):
        used = int((sizes > 0).sum())
        fixed = max(1, used // 4)
        moved = fixed + (places - fixed + rotation * (used - fixed)) % max(1, number_of - fixed)
        return jnp.zeros((number_of,), jnp.int32).at[order[jnp.where(places < fixed, places, moved)]].set(jnp.asarray(sizes, jnp.int32))

    sizes = jnp.where(number % 4 == 0, named(heavy_load, number // 4), named(usual, number - number // 4 - 1))
    mixed = jax.random.permutation(jax.random.fold_in(own, 3), number_of)
    donor, taker = mixed[0:number_of // 2 * 2:2], mixed[1:number_of // 2 * 2:2]
    margin = jnp.minimum(sizes[donor] - 1, limit - sizes[taker]) // 2
    margin = jnp.where((donor == order[0]) | (taker == order[0]) | (sizes[taker] == 0), 0, jnp.maximum(margin, 0))
    moved = jax.random.randint(jax.random.fold_in(own, 4), (number_of // 2,), 0, 1 << 20) % (margin + 1)
    sizes = sizes.at[donor].add(-moved).at[taker].add(moved)
    members = jnp.searchsorted(jnp.cumsum(sizes), jnp.arange(rows * top), side="right").astype(jnp.int32)
    table = members.reshape(top, rows).T
    table = table[jax.random.permutation(jax.random.fold_in(own, 1), rows)]
    rotation = jax.random.randint(jax.random.fold_in(own, 2), (rows, 1), 0, top)
    return jnp.take_along_axis(table, (jnp.arange(top)[None, :] + rotation) % top, axis=1)


def load_shares(number_of, total, bound, slope, full):
    portions = [(1 << 20) // math.isqrt(grade ** slope) + 1 for grade in range(1, number_of + 1)]
    largest = bound if full else min(bound, max(-(-total // number_of), total * portions[0] // sum(portions)))
    least = 1 if total - largest >= number_of - 1 else 0
    holding, spare = [largest] + [least] * (number_of - 1), total - largest - least * (number_of - 1)
    while spare > 0:
        movable = [i for i in range(1, number_of) if holding[i] < largest] or [i for i in range(1, number_of) if holding[i] < bound]
        whole, left = sum([portions[i] for i in movable]), spare
        for i in movable:
            more = min(bound - holding[i], max(1, left * portions[i] // whole), spare)
            holding[i] = holding[i] + more
            spare = spare - more
    return np.array(holding)


def noise(stream_key, dims, spread, reach, cuts=(), kind=jnp.bfloat16):
    loudness = shard_levels(stream_key, dims, cuts, -0.22, 0.18) if cuts else 1.0
    values = jax.random.normal(stream_key, dims, jnp.float32) * spread * loudness
    return jnp.minimum(jnp.maximum(values, -reach), reach).astype(kind)


def setup_inputs(seed: int = 0) -> dict:
    key_list = jax.random.split(jax.random.key(seed), 16)
    queries = draw_queries(jax.random.fold_in(key_list[15], 71), 0)
    keys = noise(key_list[1], (TOKENS, D), 2.5, 15.0, ((0, 8), (1, 16)))
    values = noise(key_list[2], (TOKENS, D), 1.0, 6.0, ((0, 8), (1, 16)))
    prefix_keys = draw_prefix_keys(jax.random.fold_in(key_list[15], 71), 0)
    prefix_values = noise(key_list[4], (G, PREF, D), 1.0, 6.0, ((1, 8), (2, 16)))
    lengths = jax.vmap(lambda own: ragged_sizes(own, RQ, ROW_TOK, ROW_TOK // 2, 2))(jax.random.split(key_list[5], N_REQ)).reshape((N_REQ, RQ)).astype(jnp.int32)
    groups = set_ends(jax.random.randint(key_list[6], (N_REQ, RQ), 0, G), jax.random.fold_in(key_list[6], 1), 0, G - 1).astype(jnp.int32)
    residual = noise(key_list[7], (TOKENS, D), 1.0, 6.0, ((0, 128),))
    out_proj = noise(key_list[8], (D, D), D ** -0.5, 0.125, ((0, 16),))
    norm_gain = jnp.clip(1.0 + 0.18 * jax.random.normal(key_list[9], (D,), jnp.float32), 0.099609375, 1.8984375).astype(jnp.bfloat16)
    expert_ids_keys = jax.random.split(jax.random.fold_in(key_list[10], 1), TOKENS // TOK_DEV)
    expert_ids_turns = jax.random.permutation(jax.random.fold_in(key_list[10], 3), TOKENS // TOK_DEV)
    expert_ids = jax.vmap(lambda own, number: shared_out(jax.random.fold_in(key_list[10], 2), own, number, TOK_DEV, EXPERTS, TOPK, CAP, 2))(expert_ids_keys, expert_ids_turns).reshape((TOKENS, TOPK))
    expert_gates = jnp.clip(0.049804688 + 0.4501953 * jax.random.uniform(key_list[11], (TOKENS, TOPK), jnp.float32) ** shard_levels(key_list[11], (TOKENS, TOPK), ((0, 128),), -0.2, 0.2), 0.049804688, 0.5).astype(jnp.bfloat16)
    w_gate = noise(key_list[12], (EXPERTS, D, FE), D ** -0.5, 0.125, ((0, 16),))
    w_up = noise(key_list[13], (EXPERTS, D, FE), D ** -0.5, 0.125, ((0, 16),))
    w_down = noise(key_list[14], (EXPERTS, FE, D), FE ** -0.5, 0.21875, ((0, 16),))
    return dict(queries=queries, keys=keys, values=values, prefix_keys=prefix_keys, prefix_values=prefix_values, lengths=lengths, groups=groups, residual=residual, out_proj=out_proj, norm_gain=norm_gain, expert_ids=expert_ids, expert_gates=expert_gates, w_gate=w_gate, w_up=w_up, w_down=w_down)


NEG = -1e+30

def token_layout(lengths, groups):
    req_ends = jnp.cumsum(lengths, axis=-1)
    starts = req_ends - lengths
    position = jnp.arange(ROW_TOK, dtype=jnp.int32)
    request = lax.optimization_barrier(jnp.sum((position[None, :, None] >= req_ends[:, None, :]).astype(jnp.int32), axis=-1))
    onehot = request[:, :, None] == jnp.arange(RQ, dtype=jnp.int32)[None, None, :]
    first_tok = lax.optimization_barrier(jnp.sum(jnp.where(onehot, starts[:, None, :], 0), axis=-1))
    tok_group = lax.optimization_barrier(jnp.sum(jnp.where(onehot, groups[:, None, :], 0), axis=-1))
    return (request, position[None, :] - first_tok, tok_group)

def reference(queries, keys, values, prefix_keys, prefix_values, lengths, groups, residual, out_proj, norm_gain, expert_ids, expert_gates, w_gate, w_up, w_down):
    request, position, tok_group = token_layout(lengths, groups)
    scaling = 1.0 / math.sqrt(HEAD)
    block_len = min(128, ROW_TOK)
    per_row = ROW_TOK // block_len
    key_grid = prefix_keys.astype(jnp.float32).reshape(G, PREF, HEADS, HEAD)
    val_grid = prefix_values.astype(jnp.float32).reshape(G, PREF, HEADS, HEAD)

    def per_block(block_id):
        row_id = block_id // per_row
        offset = block_id % per_row * block_len
        query_grid = lax.dynamic_slice_in_dim(queries, block_id * block_len, block_len, 0).astype(jnp.float32).reshape(block_len, HEADS, HEAD)
        row_keys = lax.dynamic_slice_in_dim(keys, row_id * ROW_TOK, ROW_TOK, 0).astype(jnp.float32).reshape(ROW_TOK, HEADS, HEAD)
        row_vals = lax.dynamic_slice_in_dim(values, row_id * ROW_TOK, ROW_TOK, 0).astype(jnp.float32).reshape(ROW_TOK, HEADS, HEAD)
        row_req = lax.dynamic_index_in_dim(request, row_id, 0, keepdims=False)
        row_pos = lax.dynamic_index_in_dim(position, row_id, 0, keepdims=False)
        row_grp = lax.dynamic_index_in_dim(tok_group, row_id, 0, keepdims=False)
        query_req = lax.dynamic_slice_in_dim(row_req, offset, block_len, 0)
        query_pos = lax.dynamic_slice_in_dim(row_pos, offset, block_len, 0)
        query_grp = lax.dynamic_slice_in_dim(row_grp, offset, block_len, 0)
        pre_scores = jnp.einsum('qhd,gkhd->qhgk', query_grid, key_grid) * scaling
        member = query_grp[:, None] == jnp.arange(G, dtype=jnp.int32)[None, :]
        pre_scores = jnp.where(member[:, None, :, None], pre_scores, NEG)
        suf_scores = jnp.einsum('qhd,khd->qhk', query_grid, row_keys) * scaling
        allowed = (row_req[None, :] == query_req[:, None]) & (row_pos[None, :] <= query_pos[:, None])
        suf_scores = jnp.where(allowed[:, None, :], suf_scores, NEG)
        maxima = jnp.maximum(lax.optimization_barrier(jnp.max(pre_scores, axis=(2, 3))), lax.optimization_barrier(jnp.max(suf_scores, axis=2)))
        pre_exp = jnp.exp(pre_scores - maxima[:, :, None, None])
        suf_exp = jnp.exp(suf_scores - maxima[:, :, None])
        totals = lax.optimization_barrier(jnp.sum(pre_exp, axis=(2, 3))) + lax.optimization_barrier(jnp.sum(suf_exp, axis=2))
        pre_probs = lax.optimization_barrier(pre_exp.astype(jnp.bfloat16)).astype(jnp.float32)
        suf_probs = lax.optimization_barrier(suf_exp.astype(jnp.bfloat16)).astype(jnp.float32)
        weighted = jnp.einsum('qhgk,gkhd->qhd', pre_probs, val_grid) + jnp.einsum('qhk,khd->qhd', suf_probs, row_vals)
        return (weighted / totals[:, :, None]).astype(jnp.bfloat16).reshape(block_len, D)
    attended = lax.map(per_block, jnp.arange(TOKENS // block_len, dtype=jnp.int32)).reshape(TOKENS, D)
    stream = residual.astype(jnp.float32) + jnp.dot(attended, out_proj, preferred_element_type=jnp.float32)
    meansq = lax.optimization_barrier(jnp.mean(stream * stream, axis=-1, keepdims=True))
    normed = (stream * lax.rsqrt(meansq + 1e-06) * norm_gain.astype(jnp.float32)).astype(jnp.bfloat16)
    flat_ids = expert_ids.reshape(-1)
    flat_gate = expert_gates.reshape(-1).astype(jnp.float32)
    most_rows = TOKENS // TOK_DEV * CAP

    def per_expert(summed, expert):
        chosen = flat_ids == expert
        where_rows = jnp.nonzero(chosen, size=most_rows, fill_value=0)[0]
        is_live = jnp.arange(most_rows) < jnp.sum(chosen.astype(jnp.int32))
        tok_rows = where_rows // TOPK
        inputs = normed[tok_rows]
        gate_h = jnp.dot(inputs, w_gate[expert], preferred_element_type=jnp.float32)
        up_h = jnp.dot(inputs, w_up[expert], preferred_element_type=jnp.float32)
        hidden = (jax.nn.silu(gate_h) * up_h).astype(jnp.bfloat16)
        expert_out = jnp.dot(hidden, w_down[expert], preferred_element_type=jnp.float32)
        weight = jnp.where(is_live, flat_gate[where_rows], 0.0)
        return (summed.at[tok_rows].add(expert_out * weight[:, None]), None)
    summed, unused = lax.scan(per_expert, jnp.zeros((TOKENS, D), jnp.float32), jnp.arange(EXPERTS, dtype=jnp.int32))
    return (stream + summed).astype(jnp.bfloat16)
```

```python
import math

import jax
import jax.numpy as jnp
from jax import lax
from jax.sharding import PartitionSpec as P

HEAD = 128
TOPK = 4
EXPERTS = 32
G = 4
RQ = 8
ROW_TOK = 1024


NEG = -1e30


def token_layout(lengths, groups):
    req_ends = jnp.cumsum(lengths, axis=-1)
    starts = req_ends - lengths
    position = jnp.arange(ROW_TOK, dtype=jnp.int32)
    request = jnp.sum((position[None, :, None] >= req_ends[:, None, :]).astype(jnp.int32), axis=-1)
    onehot = request[:, :, None] == jnp.arange(RQ, dtype=jnp.int32)[None, None, :]
    first_tok = jnp.sum(jnp.where(onehot, starts[:, None, :], 0), axis=-1)
    tok_group = jnp.sum(jnp.where(onehot, groups[:, None, :], 0), axis=-1)
    return (request, position[None, :] - first_tok, tok_group)


def split_blocks(row_count):
    if row_count % 1024 == 0 and row_count > 1024:
        return row_count // 1024
    return 1


def pack_parts(parts):
    return jnp.concatenate([parts[0], parts[1], parts[2]], axis=1)


def unpack_parts(packed, head_count):
    columns = head_count * HEAD
    return (
        packed[:, :columns],
        packed[:, columns : columns + head_count],
        packed[:, columns + head_count :],
    )


def attend_prefix(query_rows, query_group, prefix_k, prefix_v):
    row_count, columns = query_rows.shape
    head_count = columns // HEAD
    span = prefix_k.shape[1]
    key_grid = prefix_k.reshape(G, span, head_count, HEAD)
    val_grid = prefix_v.reshape(G, span, head_count, HEAD)
    blocks = split_blocks(row_count)
    block_len = row_count // blocks
    scaling = 1.0 / math.sqrt(HEAD)

    def per_block(pieces):
        block_q, block_g = pieces
        query_grid = block_q.reshape(block_len, head_count, HEAD)
        scores = (
            jnp.einsum("qhd,gkhd->hqgk", query_grid, key_grid, preferred_element_type=jnp.float32)
            * scaling
        )
        member = block_g[:, None] == jnp.arange(G, dtype=jnp.int32)[None, :]
        scores = jnp.where(member[None, :, :, None], scores, NEG)
        maxima = jnp.max(scores, axis=(2, 3))
        exp_terms = jnp.exp(scores - maxima[:, :, None, None])
        totals = jnp.sum(exp_terms, axis=(2, 3))
        weighted = jnp.einsum(
            "hqgk,gkhd->qhd",
            exp_terms.astype(jnp.bfloat16),
            val_grid,
            preferred_element_type=jnp.float32,
        )
        return (weighted.reshape(block_len, columns), maxima.T, totals.T)

    weighted, maxima, totals = lax.map(
        per_block,
        (query_rows.reshape(blocks, block_len, columns), query_group.reshape(blocks, block_len)),
    )
    return (
        weighted.reshape(row_count, columns),
        maxima.reshape(row_count, head_count),
        totals.reshape(row_count, head_count),
    )


def attend_suffix(queries, keys, values, request, position):
    row_count, columns = queries.shape
    head_count = columns // HEAD
    blocks = split_blocks(row_count)
    block_len = row_count // blocks
    scaling = 1.0 / math.sqrt(HEAD)
    key_grid = keys.reshape(row_count, head_count, HEAD)
    val_grid = values.reshape(row_count, head_count, HEAD)

    def per_block(pieces):
        block_q, block_req, block_pos = pieces
        query_grid = block_q.reshape(block_len, head_count, HEAD)
        scores = (
            jnp.einsum("qhd,khd->hqk", query_grid, key_grid, preferred_element_type=jnp.float32)
            * scaling
        )
        allowed = (request[None, :] == block_req[:, None]) & (
            position[None, :] <= block_pos[:, None]
        )
        scores = jnp.where(allowed[None, :, :], scores, NEG)
        maxima = jnp.max(scores, axis=2)
        exp_terms = jnp.exp(scores - maxima[:, :, None])
        totals = jnp.sum(exp_terms, axis=2)
        weighted = jnp.einsum(
            "hqk,khd->qhd",
            exp_terms.astype(jnp.bfloat16),
            val_grid,
            preferred_element_type=jnp.float32,
        )
        return (weighted.reshape(block_len, columns), maxima.T, totals.T)

    weighted, maxima, totals = lax.map(
        per_block,
        (
            queries.reshape(blocks, block_len, columns),
            request.reshape(blocks, block_len),
            position.reshape(blocks, block_len),
        ),
    )
    return (
        weighted.reshape(row_count, columns),
        maxima.reshape(row_count, head_count),
        totals.reshape(row_count, head_count),
    )


def combine(former, latter):
    weighted_a, maxima_a, totals_a = former
    weighted_b, maxima_b, totals_b = latter
    row_count, head_count = maxima_a.shape
    maxima = jnp.maximum(maxima_a, maxima_b)
    factor_a = jnp.exp(maxima_a - maxima)
    factor_b = jnp.exp(maxima_b - maxima)
    weighted = (
        weighted_a.reshape(row_count, head_count, HEAD) * factor_a[:, :, None]
        + weighted_b.reshape(row_count, head_count, HEAD) * factor_b[:, :, None]
    )
    return (
        weighted.reshape(row_count, head_count * HEAD),
        maxima,
        totals_a * factor_a + totals_b * factor_b,
    )


def per_device(
    queries,
    keys,
    values,
    prefix_keys,
    prefix_values,
    lengths,
    groups,
    residual,
    out_proj,
    norm_gain,
    expert_ids,
    expert_gates,
    w_gate,
    w_up,
    w_down,
):
    row_tok, columns = queries.shape
    head_count = columns // HEAD
    tok_dev = residual.shape[0]
    request, position, tok_group = token_layout(lengths, groups)
    request, position, tok_group = (request[0], position[0], tok_group[0])
    all_groups = lax.all_gather(tok_group, "req", axis=0, tiled=True)
    partial_value = pack_parts(
        attend_prefix(
            lax.all_gather(queries, "req", axis=0, tiled=True),
            all_groups,
            prefix_keys,
            prefix_values,
        )
    )
    returned = lax.all_to_all(partial_value, "req", split_axis=0, concat_axis=0, tiled=True)
    owners = returned.shape[0] // row_tok
    back_w, back_m, back_t = unpack_parts(returned, head_count)
    all_weighted = back_w.reshape(owners, row_tok, head_count, HEAD)
    all_maxima = back_m.reshape(owners, row_tok, head_count)
    all_totals = back_t.reshape(owners, row_tok, head_count)
    maxima = jnp.max(all_maxima, axis=0)
    factor = jnp.exp(all_maxima - maxima[None])
    weighted = jnp.sum(all_weighted * factor[..., None], axis=0).reshape(row_tok, columns)
    prefix_part = (weighted, maxima, jnp.sum(all_totals * factor, axis=0))
    suffix_part = attend_suffix(queries, keys, values, request, position)
    weighted, maxima, totals = combine(prefix_part, suffix_part)
    attended = (
        (weighted.reshape(row_tok, head_count, HEAD) / totals[:, :, None])
        .reshape(row_tok, columns)
        .astype(jnp.bfloat16)
    )
    exp_count = lax.axis_size("exp")
    full_proj = lax.all_gather(out_proj, "exp", axis=0, tiled=True)
    token_rows = lax.all_to_all(attended, "exp", split_axis=0, concat_axis=1, tiled=True)
    projected = jnp.dot(token_rows, full_proj, preferred_element_type=jnp.float32)
    stream = residual.astype(jnp.float32) + projected
    meansq = jnp.mean(stream * stream, axis=-1, keepdims=True)
    normed = (stream * lax.rsqrt(meansq + 1e-06) * norm_gain.astype(jnp.float32)).astype(
        jnp.bfloat16
    )
    capacity = max(2, tok_dev // 4)
    slot_count = EXPERTS * capacity
    flat_ids = expert_ids.reshape(-1)
    onehot = (flat_ids[:, None] == jnp.arange(EXPERTS, dtype=jnp.int32)[None, :]).astype(jnp.int32)
    slot_of = jnp.sum(onehot * (jnp.cumsum(onehot, axis=0) - 1), axis=1)
    dest = flat_ids * capacity + slot_of
    dest_hot = dest[:, None] == jnp.arange(slot_count, dtype=jnp.int32)[None, :]
    select = jnp.sum(dest_hot.reshape(tok_dev, TOPK, slot_count).astype(jnp.float32), axis=1)
    buffer = jnp.dot(
        select.T.astype(jnp.bfloat16), normed, preferred_element_type=jnp.float32
    ).astype(jnp.bfloat16).reshape(EXPERTS, capacity, normed.shape[1])
    exp_dev = w_gate.shape[0]
    received = lax.all_to_all(buffer, "exp", split_axis=0, concat_axis=0, tiled=True)
    slots = received.shape[1]
    grid_in = received.reshape(exp_count, exp_dev, slots, received.shape[2])
    gate_h = jnp.einsum("secd,edf->secf", grid_in, w_gate, preferred_element_type=jnp.float32)
    up_h = jnp.einsum("secd,edf->secf", grid_in, w_up, preferred_element_type=jnp.float32)
    hidden = (jax.nn.silu(gate_h) * up_h).astype(jnp.bfloat16)
    expert_out = jnp.einsum("secf,efd->secd", hidden, w_down, preferred_element_type=jnp.float32)
    returned = lax.all_to_all(
        expert_out.astype(jnp.bfloat16).reshape(EXPERTS, slots, received.shape[2]),
        "exp",
        split_axis=0,
        concat_axis=0,
        tiled=True,
    )
    gates = expert_gates.astype(jnp.float32).reshape(tok_dev, TOPK, 1)
    weights = jnp.sum(dest_hot.reshape(tok_dev, TOPK, slot_count).astype(jnp.float32) * gates, axis=1)
    mixture = jnp.dot(
        weights.astype(jnp.bfloat16),
        returned.reshape(slot_count, received.shape[2]),
        preferred_element_type=jnp.float32,
    )
    return (stream + mixture).astype(jnp.bfloat16)


def solution(mesh):
    in_specs = (
        P("req", "exp"),
        P("req", "exp"),
        P("req", "exp"),
        P(None, "req", "exp"),
        P(None, "req", "exp"),
        P("req", None),
        P("req", None),
        P(("req", "exp"), None),
        P("exp", None),
        P(),
        P(("req", "exp"), None),
        P(("req", "exp"), None),
        P("exp", None, None),
        P("exp", None, None),
        P("exp", None, None),
    )
    out_specs = P(("req", "exp"), None)
    return jax.shard_map(
        per_device, mesh=mesh, in_specs=in_specs, out_specs=out_specs, check_vma=False
    )
```

```python
import math

import jax
import jax.numpy as jnp
from jax import lax
from jax.experimental import pallas as pl
from jax.experimental.pallas import tpu as pltpu
from jax.sharding import PartitionSpec as P

HEAD = 128
TOPK = 4
EXPERTS = 32
G = 4
RQ = 8
ROW_TOK = 1024


NEG = -1e30


def token_layout(lengths, groups):
    req_ends = jnp.cumsum(lengths, axis=-1)
    starts = req_ends - lengths
    position = jnp.arange(ROW_TOK, dtype=jnp.int32)
    request = jnp.sum((position[None, :, None] >= req_ends[:, None, :]).astype(jnp.int32), axis=-1)
    onehot = request[:, :, None] == jnp.arange(RQ, dtype=jnp.int32)[None, None, :]
    first_tok = jnp.sum(jnp.where(onehot, starts[:, None, :], 0), axis=-1)
    tok_group = jnp.sum(jnp.where(onehot, groups[:, None, :], 0), axis=-1)
    return (request, position[None, :] - first_tok, tok_group)


def split_blocks(row_count):
    if row_count % 1024 == 0 and row_count > 1024:
        return row_count // 1024
    return 1


def pack_parts(parts):
    return jnp.concatenate([parts[0], parts[1], parts[2]], axis=1)


def unpack_parts(packed, head_count):
    columns = head_count * HEAD
    return (
        packed[:, :columns],
        packed[:, columns : columns + head_count],
        packed[:, columns + head_count :],
    )


def attend_prefix(query_rows, query_group, prefix_k, prefix_v):
    row_count, columns = query_rows.shape
    head_count = columns // HEAD
    span = prefix_k.shape[1]
    key_grid = prefix_k.reshape(G, span, head_count, HEAD)
    val_grid = prefix_v.reshape(G, span, head_count, HEAD)
    blocks = split_blocks(row_count)
    block_len = row_count // blocks
    scaling = 1.0 / math.sqrt(HEAD)

    def per_block(pieces):
        block_q, block_g = pieces
        query_grid = block_q.reshape(block_len, head_count, HEAD)
        scores = (
            jnp.einsum("qhd,gkhd->hqgk", query_grid, key_grid, preferred_element_type=jnp.float32)
            * scaling
        )
        member = block_g[:, None] == jnp.arange(G, dtype=jnp.int32)[None, :]
        scores = jnp.where(member[None, :, :, None], scores, NEG)
        maxima = jnp.max(scores, axis=(2, 3))
        exp_terms = jnp.exp(scores - maxima[:, :, None, None])
        totals = jnp.sum(exp_terms, axis=(2, 3))
        weighted = jnp.einsum(
            "hqgk,gkhd->qhd",
            exp_terms.astype(jnp.bfloat16),
            val_grid,
            preferred_element_type=jnp.float32,
        )
        return (weighted.reshape(block_len, columns), maxima.T, totals.T)

    weighted, maxima, totals = lax.map(
        per_block,
        (query_rows.reshape(blocks, block_len, columns), query_group.reshape(blocks, block_len)),
    )
    return (
        weighted.reshape(row_count, columns),
        maxima.reshape(row_count, head_count),
        totals.reshape(row_count, head_count),
    )


QUERY_BLOCK = 128
KEY_BLOCK = 1024


def prefix_kernel(present_ref, q_ref, grp_ref, k_ref, v_ref, acc_ref, m_ref, l_ref):
    g = pl.program_id(0)
    kb = pl.program_id(1)
    scaling = 1.0 / math.sqrt(HEAD)

    @pl.when((g == 0) & (kb == 0))
    def _():
        acc_ref[...] = jnp.zeros_like(acc_ref)
        m_ref[...] = jnp.full_like(m_ref, NEG)
        l_ref[...] = jnp.zeros_like(l_ref)

    k = k_ref[0]
    v = v_ref[0]
    block_count = q_ref.shape[0] // QUERY_BLOCK

    def body(qb, carry):
        @pl.when(present_ref[qb * G + g] > 0)
        def _():
            rows = pl.ds(pl.multiple_of(qb * QUERY_BLOCK, QUERY_BLOCK), QUERY_BLOCK)
            s = lax.dot_general(
                q_ref[rows, :], k, (((1,), (1,)), ((), ())), preferred_element_type=jnp.float32
            ) * scaling
            mask = grp_ref[rows, :][:, :1] == g
            s = jnp.where(mask, s, NEG)
            m_prev = m_ref[rows, :]
            m_new = jnp.maximum(m_prev, jnp.max(s, axis=1, keepdims=True))
            alpha = jnp.exp(m_prev - m_new)
            p = jnp.where(mask, jnp.exp(s - m_new[:, :1]), 0.0)
            l_ref[rows, :] = alpha * l_ref[rows, :] + jnp.sum(p, axis=1, keepdims=True)
            acc_ref[rows, :] = alpha * acc_ref[rows, :] + jnp.dot(
                p.astype(jnp.bfloat16), v, preferred_element_type=jnp.float32
            )
            m_ref[rows, :] = m_new

        return carry

    lax.fori_loop(0, block_count, body, 0)


def attend_prefix_local(query_rows, query_group, prefix_k, prefix_v):
    row_count = query_rows.shape[0]
    span = prefix_k.shape[1]
    block_count = row_count // QUERY_BLOCK
    present = jnp.any(
        query_group.reshape(block_count, QUERY_BLOCK, 1)
        == jnp.arange(G, dtype=jnp.int32)[None, None, :],
        axis=1,
    ).astype(jnp.int32).reshape(-1)
    grp = jnp.broadcast_to(query_group[:, None], (row_count, HEAD))
    full = lambda g, kb, pr: (0, 0)
    kv_spec = pl.BlockSpec((1, KEY_BLOCK, HEAD), lambda g, kb, pr: (g, kb, 0))
    out_shape = jax.ShapeDtypeStruct((row_count, HEAD), jnp.float32)
    acc, maxima, totals = pl.pallas_call(
        prefix_kernel,
        grid_spec=pltpu.PrefetchScalarGridSpec(
            num_scalar_prefetch=1,
            grid=(G, span // KEY_BLOCK),
            in_specs=[
                pl.BlockSpec((row_count, HEAD), full),
                pl.BlockSpec((row_count, HEAD), full),
                kv_spec,
                kv_spec,
            ],
            out_specs=[pl.BlockSpec((row_count, HEAD), full)] * 3,
        ),
        out_shape=[out_shape] * 3,
        compiler_params=pltpu.CompilerParams(dimension_semantics=("arbitrary", "arbitrary")),
        cost_estimate=pl.CostEstimate(
            flops=4 * row_count * span * HEAD * 2,
            transcendentals=row_count * span * 2,
            bytes_accessed=2 * G * span * HEAD * 2 + row_count * HEAD * 14,
        ),
    )(present, query_rows, grp, prefix_k, prefix_v)
    return (acc, maxima[:, :1], totals[:, :1])


def attend_suffix(queries, keys, values, request, position):
    row_count, columns = queries.shape
    head_count = columns // HEAD
    blocks = split_blocks(row_count)
    block_len = row_count // blocks
    scaling = 1.0 / math.sqrt(HEAD)
    key_grid = keys.reshape(row_count, head_count, HEAD)
    val_grid = values.reshape(row_count, head_count, HEAD)

    def per_block(pieces):
        block_q, block_req, block_pos = pieces
        query_grid = block_q.reshape(block_len, head_count, HEAD)
        scores = (
            jnp.einsum("qhd,khd->hqk", query_grid, key_grid, preferred_element_type=jnp.float32)
            * scaling
        )
        allowed = (request[None, :] == block_req[:, None]) & (
            position[None, :] <= block_pos[:, None]
        )
        scores = jnp.where(allowed[None, :, :], scores, NEG)
        maxima = jnp.max(scores, axis=2)
        exp_terms = jnp.exp(scores - maxima[:, :, None])
        totals = jnp.sum(exp_terms, axis=2)
        weighted = jnp.einsum(
            "hqk,khd->qhd",
            exp_terms.astype(jnp.bfloat16),
            val_grid,
            preferred_element_type=jnp.float32,
        )
        return (weighted.reshape(block_len, columns), maxima.T, totals.T)

    weighted, maxima, totals = lax.map(
        per_block,
        (
            queries.reshape(blocks, block_len, columns),
            request.reshape(blocks, block_len),
            position.reshape(blocks, block_len),
        ),
    )
    return (
        weighted.reshape(row_count, columns),
        maxima.reshape(row_count, head_count),
        totals.reshape(row_count, head_count),
    )


def combine(former, latter):
    weighted_a, maxima_a, totals_a = former
    weighted_b, maxima_b, totals_b = latter
    row_count, head_count = maxima_a.shape
    maxima = jnp.maximum(maxima_a, maxima_b)
    factor_a = jnp.exp(maxima_a - maxima)
    factor_b = jnp.exp(maxima_b - maxima)
    weighted = (
        weighted_a.reshape(row_count, head_count, HEAD) * factor_a[:, :, None]
        + weighted_b.reshape(row_count, head_count, HEAD) * factor_b[:, :, None]
    )
    return (
        weighted.reshape(row_count, head_count * HEAD),
        maxima,
        totals_a * factor_a + totals_b * factor_b,
    )


def per_device(
    queries,
    keys,
    values,
    prefix_keys,
    prefix_values,
    lengths,
    groups,
    residual,
    out_proj,
    norm_gain,
    expert_ids,
    expert_gates,
    w_gate,
    w_up,
    w_down,
):
    row_tok, columns = queries.shape
    head_count = columns // HEAD
    tok_dev = residual.shape[0]
    request, position, tok_group = token_layout(lengths, groups)
    request, position, tok_group = (request[0], position[0], tok_group[0])
    prefix_part = attend_prefix_local(
        queries,
        tok_group,
        lax.all_gather(prefix_keys, "req", axis=1, tiled=True),
        lax.all_gather(prefix_values, "req", axis=1, tiled=True),
    )
    suffix_part = attend_suffix(queries, keys, values, request, position)
    weighted, maxima, totals = combine(prefix_part, suffix_part)
    attended = (
        (weighted.reshape(row_tok, head_count, HEAD) / totals[:, :, None])
        .reshape(row_tok, columns)
        .astype(jnp.bfloat16)
    )
    exp_count = lax.axis_size("exp")
    full_proj = lax.all_gather(out_proj, "exp", axis=0, tiled=True)
    token_rows = lax.all_to_all(attended, "exp", split_axis=0, concat_axis=1, tiled=True)
    projected = jnp.dot(token_rows, full_proj, preferred_element_type=jnp.float32)
    stream = residual.astype(jnp.float32) + projected
    meansq = jnp.mean(stream * stream, axis=-1, keepdims=True)
    normed = (stream * lax.rsqrt(meansq + 1e-06) * norm_gain.astype(jnp.float32)).astype(
        jnp.bfloat16
    )
    capacity = max(2, tok_dev // 4)
    slot_count = EXPERTS * capacity
    flat_ids = expert_ids.reshape(-1)
    onehot = (flat_ids[:, None] == jnp.arange(EXPERTS, dtype=jnp.int32)[None, :]).astype(jnp.int32)
    slot_of = jnp.sum(onehot * (jnp.cumsum(onehot, axis=0) - 1), axis=1)
    dest = flat_ids * capacity + slot_of
    dest_hot = dest[:, None] == jnp.arange(slot_count, dtype=jnp.int32)[None, :]
    select = jnp.sum(dest_hot.reshape(tok_dev, TOPK, slot_count).astype(jnp.float32), axis=1)
    buffer = jnp.dot(
        select.T.astype(jnp.bfloat16), normed, preferred_element_type=jnp.float32
    ).astype(jnp.bfloat16).reshape(EXPERTS, capacity, normed.shape[1])
    exp_dev = w_gate.shape[0]
    received = lax.all_to_all(buffer, "exp", split_axis=0, concat_axis=0, tiled=True)
    slots = received.shape[1]
    grid_in = received.reshape(exp_count, exp_dev, slots, received.shape[2])
    gate_h = jnp.einsum("secd,edf->secf", grid_in, w_gate, preferred_element_type=jnp.float32)
    up_h = jnp.einsum("secd,edf->secf", grid_in, w_up, preferred_element_type=jnp.float32)
    hidden = (jax.nn.silu(gate_h) * up_h).astype(jnp.bfloat16)
    expert_out = jnp.einsum("secf,efd->secd", hidden, w_down, preferred_element_type=jnp.float32)
    returned = lax.all_to_all(
        expert_out.astype(jnp.bfloat16).reshape(EXPERTS, slots, received.shape[2]),
        "exp",
        split_axis=0,
        concat_axis=0,
        tiled=True,
    )
    gates = expert_gates.astype(jnp.float32).reshape(tok_dev, TOPK, 1)
    weights = jnp.sum(dest_hot.reshape(tok_dev, TOPK, slot_count).astype(jnp.float32) * gates, axis=1)
    mixture = jnp.dot(
        weights.astype(jnp.bfloat16),
        returned.reshape(slot_count, received.shape[2]),
        preferred_element_type=jnp.float32,
    )
    return (stream + mixture).astype(jnp.bfloat16)


def solution(mesh):
    in_specs = (
        P("req", "exp"),
        P("req", "exp"),
        P("req", "exp"),
        P(None, "req", "exp"),
        P(None, "req", "exp"),
        P("req", None),
        P("req", None),
        P(("req", "exp"), None),
        P("exp", None),
        P(),
        P(("req", "exp"), None),
        P(("req", "exp"), None),
        P("exp", None, None),
        P("exp", None, None),
        P("exp", None, None),
    )
    out_specs = P(("req", "exp"), None)
    return jax.shard_map(
        per_device, mesh=mesh, in_specs=in_specs, out_specs=out_specs, check_vma=False
    )
```

```python
import math

import jax
import jax.numpy as jnp
from jax import lax
from jax.experimental import pallas as pl
from jax.experimental.pallas import tpu as pltpu
from jax.sharding import PartitionSpec as P

HEAD = 128
TOPK = 4
EXPERTS = 32
G = 4
RQ = 8
ROW_TOK = 1024


NEG = -1e30


def token_layout(lengths, groups):
    req_ends = jnp.cumsum(lengths, axis=-1)
    starts = req_ends - lengths
    position = jnp.arange(ROW_TOK, dtype=jnp.int32)
    request = jnp.sum((position[None, :, None] >= req_ends[:, None, :]).astype(jnp.int32), axis=-1)
    onehot = request[:, :, None] == jnp.arange(RQ, dtype=jnp.int32)[None, None, :]
    first_tok = jnp.sum(jnp.where(onehot, starts[:, None, :], 0), axis=-1)
    tok_group = jnp.sum(jnp.where(onehot, groups[:, None, :], 0), axis=-1)
    return (request, position[None, :] - first_tok, tok_group)


def split_blocks(row_count):
    if row_count % 1024 == 0 and row_count > 1024:
        return row_count // 1024
    return 1


def pack_parts(parts):
    return jnp.concatenate([parts[0], parts[1], parts[2]], axis=1)


def unpack_parts(packed, head_count):
    columns = head_count * HEAD
    return (
        packed[:, :columns],
        packed[:, columns : columns + head_count],
        packed[:, columns + head_count :],
    )


def attend_prefix(query_rows, query_group, prefix_k, prefix_v):
    row_count, columns = query_rows.shape
    head_count = columns // HEAD
    span = prefix_k.shape[1]
    key_grid = prefix_k.reshape(G, span, head_count, HEAD)
    val_grid = prefix_v.reshape(G, span, head_count, HEAD)
    blocks = split_blocks(row_count)
    block_len = row_count // blocks
    scaling = 1.0 / math.sqrt(HEAD)

    def per_block(pieces):
        block_q, block_g = pieces
        query_grid = block_q.reshape(block_len, head_count, HEAD)
        scores = (
            jnp.einsum("qhd,gkhd->hqgk", query_grid, key_grid, preferred_element_type=jnp.float32)
            * scaling
        )
        member = block_g[:, None] == jnp.arange(G, dtype=jnp.int32)[None, :]
        scores = jnp.where(member[None, :, :, None], scores, NEG)
        maxima = jnp.max(scores, axis=(2, 3))
        exp_terms = jnp.exp(scores - maxima[:, :, None, None])
        totals = jnp.sum(exp_terms, axis=(2, 3))
        weighted = jnp.einsum(
            "hqgk,gkhd->qhd",
            exp_terms.astype(jnp.bfloat16),
            val_grid,
            preferred_element_type=jnp.float32,
        )
        return (weighted.reshape(block_len, columns), maxima.T, totals.T)

    weighted, maxima, totals = lax.map(
        per_block,
        (query_rows.reshape(blocks, block_len, columns), query_group.reshape(blocks, block_len)),
    )
    return (
        weighted.reshape(row_count, columns),
        maxima.reshape(row_count, head_count),
        totals.reshape(row_count, head_count),
    )


QUERY_BLOCK = 128
KEY_BLOCK = 512


def prefix_kernel(present_ref, q_ref, grp_ref, k_ref, v_ref, acc_ref, m_ref, l_ref):
    g = pl.program_id(0)
    kb = pl.program_id(1)
    scaling = 1.0 / math.sqrt(HEAD)

    @pl.when((g == 0) & (kb == 0))
    def _():
        acc_ref[...] = jnp.zeros_like(acc_ref)
        m_ref[...] = jnp.full_like(m_ref, NEG)
        l_ref[...] = jnp.zeros_like(l_ref)

    k = k_ref[0]
    v = v_ref[0]
    block_count = q_ref.shape[0] // QUERY_BLOCK

    def body(qb, carry):
        @pl.when(present_ref[qb * G + g] > 0)
        def _():
            rows = pl.ds(pl.multiple_of(qb * QUERY_BLOCK, QUERY_BLOCK), QUERY_BLOCK)
            s = jnp.dot(q_ref[rows, :], k, preferred_element_type=jnp.float32) * scaling
            mask = grp_ref[rows, :][:, :1] == g
            s = jnp.where(mask, s, NEG)
            m_prev = m_ref[rows, :]
            m_new = jnp.maximum(m_prev, jnp.max(s, axis=1, keepdims=True))
            alpha = jnp.exp(m_prev - m_new)
            p = jnp.where(mask, jnp.exp(s - m_new[:, :1]), 0.0)
            l_ref[rows, :] = alpha * l_ref[rows, :] + jnp.sum(p, axis=1, keepdims=True)
            acc_ref[rows, :] = alpha * acc_ref[rows, :] + jnp.dot(
                p.astype(jnp.bfloat16), v, preferred_element_type=jnp.float32
            )
            m_ref[rows, :] = m_new

        return carry

    lax.fori_loop(0, block_count, body, 0)


def attend_prefix_local(query_rows, query_group, prefix_k, prefix_v):
    row_count = query_rows.shape[0]
    span = prefix_k.shape[1]
    prefix_kt = jnp.swapaxes(prefix_k, 1, 2)
    block_count = row_count // QUERY_BLOCK
    present = jnp.any(
        query_group.reshape(block_count, QUERY_BLOCK, 1)
        == jnp.arange(G, dtype=jnp.int32)[None, None, :],
        axis=1,
    ).astype(jnp.int32).reshape(-1)
    grp = jnp.broadcast_to(query_group[:, None], (row_count, HEAD))
    full = lambda g, kb, pr: (0, 0)
    kt_spec = pl.BlockSpec((1, HEAD, KEY_BLOCK), lambda g, kb, pr: (g, 0, kb))
    kv_spec = pl.BlockSpec((1, KEY_BLOCK, HEAD), lambda g, kb, pr: (g, kb, 0))
    out_shape = jax.ShapeDtypeStruct((row_count, HEAD), jnp.float32)
    acc, maxima, totals = pl.pallas_call(
        prefix_kernel,
        grid_spec=pltpu.PrefetchScalarGridSpec(
            num_scalar_prefetch=1,
            grid=(G, span // KEY_BLOCK),
            in_specs=[
                pl.BlockSpec((row_count, HEAD), full),
                pl.BlockSpec((row_count, HEAD), full),
                kt_spec,
                kv_spec,
            ],
            out_specs=[pl.BlockSpec((row_count, HEAD), full)] * 3,
        ),
        out_shape=[out_shape] * 3,
        compiler_params=pltpu.CompilerParams(dimension_semantics=("arbitrary", "arbitrary")),
        cost_estimate=pl.CostEstimate(
            flops=4 * row_count * span * HEAD * 2,
            transcendentals=row_count * span * 2,
            bytes_accessed=2 * G * span * HEAD * 2 + row_count * HEAD * 14,
        ),
    )(present, query_rows, grp, prefix_kt, prefix_v)
    return (acc, maxima[:, :1], totals[:, :1])


def attend_suffix(queries, keys, values, request, position):
    row_count, columns = queries.shape
    head_count = columns // HEAD
    blocks = split_blocks(row_count)
    block_len = row_count // blocks
    scaling = 1.0 / math.sqrt(HEAD)
    key_grid = keys.reshape(row_count, head_count, HEAD)
    val_grid = values.reshape(row_count, head_count, HEAD)

    def per_block(pieces):
        block_q, block_req, block_pos = pieces
        query_grid = block_q.reshape(block_len, head_count, HEAD)
        scores = (
            jnp.einsum("qhd,khd->hqk", query_grid, key_grid, preferred_element_type=jnp.float32)
            * scaling
        )
        allowed = (request[None, :] == block_req[:, None]) & (
            position[None, :] <= block_pos[:, None]
        )
        scores = jnp.where(allowed[None, :, :], scores, NEG)
        maxima = jnp.max(scores, axis=2)
        exp_terms = jnp.exp(scores - maxima[:, :, None])
        totals = jnp.sum(exp_terms, axis=2)
        weighted = jnp.einsum(
            "hqk,khd->qhd",
            exp_terms.astype(jnp.bfloat16),
            val_grid,
            preferred_element_type=jnp.float32,
        )
        return (weighted.reshape(block_len, columns), maxima.T, totals.T)

    weighted, maxima, totals = lax.map(
        per_block,
        (
            queries.reshape(blocks, block_len, columns),
            request.reshape(blocks, block_len),
            position.reshape(blocks, block_len),
        ),
    )
    return (
        weighted.reshape(row_count, columns),
        maxima.reshape(row_count, head_count),
        totals.reshape(row_count, head_count),
    )


def combine(former, latter):
    weighted_a, maxima_a, totals_a = former
    weighted_b, maxima_b, totals_b = latter
    row_count, head_count = maxima_a.shape
    maxima = jnp.maximum(maxima_a, maxima_b)
    factor_a = jnp.exp(maxima_a - maxima)
    factor_b = jnp.exp(maxima_b - maxima)
    weighted = (
        weighted_a.reshape(row_count, head_count, HEAD) * factor_a[:, :, None]
        + weighted_b.reshape(row_count, head_count, HEAD) * factor_b[:, :, None]
    )
    return (
        weighted.reshape(row_count, head_count * HEAD),
        maxima,
        totals_a * factor_a + totals_b * factor_b,
    )


def per_device(
    queries,
    keys,
    values,
    prefix_keys,
    prefix_values,
    lengths,
    groups,
    residual,
    out_proj,
    norm_gain,
    expert_ids,
    expert_gates,
    w_gate,
    w_up,
    w_down,
):
    row_tok, columns = queries.shape
    head_count = columns // HEAD
    tok_dev = residual.shape[0]
    request, position, tok_group = token_layout(lengths, groups)
    request, position, tok_group = (request[0], position[0], tok_group[0])
    req_count = lax.axis_size("req")
    local_kv = jnp.stack([prefix_keys, prefix_values])
    partner = [(i, i ^ 1) for i in range(req_count)]
    partner_kv = lax.ppermute(local_kv, "req", partner)
    ring_kv = jnp.concatenate(
        [
            lax.ppermute(local_kv, "req", [(i, (i + 2 * s) % req_count) for i in range(req_count)])
            for s in range(1, req_count // 2)
        ],
        axis=2,
    )
    forwarded_kv = lax.ppermute(ring_kv, "req", partner)
    prefix_part = None
    for chunk in (jnp.concatenate([local_kv, partner_kv], axis=2), ring_kv, forwarded_kv):
        part = attend_prefix_local(queries, tok_group, chunk[0], chunk[1])
        prefix_part = part if prefix_part is None else combine(prefix_part, part)
    suffix_part = attend_suffix(queries, keys, values, request, position)
    weighted, maxima, totals = combine(prefix_part, suffix_part)
    attended = (
        (weighted.reshape(row_tok, head_count, HEAD) / totals[:, :, None])
        .reshape(row_tok, columns)
        .astype(jnp.bfloat16)
    )
    exp_count = lax.axis_size("exp")
    full_proj = lax.all_gather(out_proj, "exp", axis=0, tiled=True)
    token_rows = lax.all_to_all(attended, "exp", split_axis=0, concat_axis=1, tiled=True)
    projected = jnp.dot(token_rows, full_proj, preferred_element_type=jnp.float32)
    stream = residual.astype(jnp.float32) + projected
    meansq = jnp.mean(stream * stream, axis=-1, keepdims=True)
    normed = (stream * lax.rsqrt(meansq + 1e-06) * norm_gain.astype(jnp.float32)).astype(
        jnp.bfloat16
    )
    capacity = max(2, tok_dev // 4)
    slot_count = EXPERTS * capacity
    flat_ids = expert_ids.reshape(-1)
    onehot = (flat_ids[:, None] == jnp.arange(EXPERTS, dtype=jnp.int32)[None, :]).astype(jnp.int32)
    slot_of = jnp.sum(onehot * (jnp.cumsum(onehot, axis=0) - 1), axis=1)
    dest = flat_ids * capacity + slot_of
    dest_hot = dest[:, None] == jnp.arange(slot_count, dtype=jnp.int32)[None, :]
    select = jnp.sum(dest_hot.reshape(tok_dev, TOPK, slot_count).astype(jnp.float32), axis=1)
    buffer = jnp.dot(
        select.T.astype(jnp.bfloat16), normed, preferred_element_type=jnp.float32
    ).astype(jnp.bfloat16).reshape(EXPERTS, capacity, normed.shape[1])
    exp_dev = w_gate.shape[0]
    received = lax.all_to_all(buffer, "exp", split_axis=0, concat_axis=0, tiled=True)
    slots = received.shape[1]
    grid_in = received.reshape(exp_count, exp_dev, slots, received.shape[2])
    gate_h = jnp.einsum("secd,edf->secf", grid_in, w_gate, preferred_element_type=jnp.float32)
    up_h = jnp.einsum("secd,edf->secf", grid_in, w_up, preferred_element_type=jnp.float32)
    hidden = (jax.nn.silu(gate_h) * up_h).astype(jnp.bfloat16)
    expert_out = jnp.einsum("secf,efd->secd", hidden, w_down, preferred_element_type=jnp.float32)
    returned = lax.all_to_all(
        expert_out.astype(jnp.bfloat16).reshape(EXPERTS, slots, received.shape[2]),
        "exp",
        split_axis=0,
        concat_axis=0,
        tiled=True,
    )
    gates = expert_gates.astype(jnp.float32).reshape(tok_dev, TOPK, 1)
    weights = jnp.sum(dest_hot.reshape(tok_dev, TOPK, slot_count).astype(jnp.float32) * gates, axis=1)
    mixture = jnp.dot(
        weights.astype(jnp.bfloat16),
        returned.reshape(slot_count, received.shape[2]),
        preferred_element_type=jnp.float32,
    )
    return (stream + mixture).astype(jnp.bfloat16)


def solution(mesh):
    in_specs = (
        P("req", "exp"),
        P("req", "exp"),
        P("req", "exp"),
        P(None, "req", "exp"),
        P(None, "req", "exp"),
        P("req", None),
        P("req", None),
        P(("req", "exp"), None),
        P("exp", None),
        P(),
        P(("req", "exp"), None),
        P(("req", "exp"), None),
        P("exp", None, None),
        P("exp", None, None),
        P("exp", None, None),
    )
    out_specs = P(("req", "exp"), None)
    return jax.shard_map(
        per_device, mesh=mesh, in_specs=in_specs, out_specs=out_specs, check_vma=False
    )
```

```python
import math

import jax
import jax.numpy as jnp
from jax import lax
from jax.experimental import pallas as pl
from jax.experimental.pallas import tpu as pltpu
from jax.sharding import PartitionSpec as P

HEAD = 128
TOPK = 4
EXPERTS = 32
G = 4
RQ = 8
ROW_TOK = 1024


NEG = -1e30


def token_layout(lengths, groups):
    req_ends = jnp.cumsum(lengths, axis=-1)
    starts = req_ends - lengths
    position = jnp.arange(ROW_TOK, dtype=jnp.int32)
    request = jnp.sum((position[None, :, None] >= req_ends[:, None, :]).astype(jnp.int32), axis=-1)
    onehot = request[:, :, None] == jnp.arange(RQ, dtype=jnp.int32)[None, None, :]
    first_tok = jnp.sum(jnp.where(onehot, starts[:, None, :], 0), axis=-1)
    tok_group = jnp.sum(jnp.where(onehot, groups[:, None, :], 0), axis=-1)
    return (request, position[None, :] - first_tok, tok_group)


def split_blocks(row_count):
    if row_count % 1024 == 0 and row_count > 1024:
        return row_count // 1024
    return 1


def pack_parts(parts):
    return jnp.concatenate([parts[0], parts[1], parts[2]], axis=1)


def unpack_parts(packed, head_count):
    columns = head_count * HEAD
    return (
        packed[:, :columns],
        packed[:, columns : columns + head_count],
        packed[:, columns + head_count :],
    )


def attend_prefix(query_rows, query_group, prefix_k, prefix_v):
    row_count, columns = query_rows.shape
    head_count = columns // HEAD
    span = prefix_k.shape[1]
    key_grid = prefix_k.reshape(G, span, head_count, HEAD)
    val_grid = prefix_v.reshape(G, span, head_count, HEAD)
    blocks = split_blocks(row_count)
    block_len = row_count // blocks
    scaling = 1.0 / math.sqrt(HEAD)

    def per_block(pieces):
        block_q, block_g = pieces
        query_grid = block_q.reshape(block_len, head_count, HEAD)
        scores = (
            jnp.einsum("qhd,gkhd->hqgk", query_grid, key_grid, preferred_element_type=jnp.float32)
            * scaling
        )
        member = block_g[:, None] == jnp.arange(G, dtype=jnp.int32)[None, :]
        scores = jnp.where(member[None, :, :, None], scores, NEG)
        maxima = jnp.max(scores, axis=(2, 3))
        exp_terms = jnp.exp(scores - maxima[:, :, None, None])
        totals = jnp.sum(exp_terms, axis=(2, 3))
        weighted = jnp.einsum(
            "hqgk,gkhd->qhd",
            exp_terms.astype(jnp.bfloat16),
            val_grid,
            preferred_element_type=jnp.float32,
        )
        return (weighted.reshape(block_len, columns), maxima.T, totals.T)

    weighted, maxima, totals = lax.map(
        per_block,
        (query_rows.reshape(blocks, block_len, columns), query_group.reshape(blocks, block_len)),
    )
    return (
        weighted.reshape(row_count, columns),
        maxima.reshape(row_count, head_count),
        totals.reshape(row_count, head_count),
    )


QUERY_BLOCK = 128
KEY_BLOCK = 2048


def prefix_kernel(present_ref, q_ref, grp_ref, k_ref, v_ref, acc_ref, m_ref, l_ref):
    g = pl.program_id(0)
    kb = pl.program_id(1)
    scaling = 1.0 / math.sqrt(HEAD)

    @pl.when((g == 0) & (kb == 0))
    def _():
        acc_ref[...] = jnp.zeros_like(acc_ref)
        m_ref[...] = jnp.full_like(m_ref, NEG)
        l_ref[...] = jnp.zeros_like(l_ref)

    k = k_ref[0]
    v = v_ref[0]
    block_count = q_ref.shape[0] // QUERY_BLOCK

    def body(qb, carry):
        @pl.when(present_ref[qb * G + g] > 0)
        def _():
            rows = pl.ds(pl.multiple_of(qb * QUERY_BLOCK, QUERY_BLOCK), QUERY_BLOCK)
            s = lax.dot_general(
                q_ref[rows, :], k, (((1,), (1,)), ((), ())), preferred_element_type=jnp.float32
            ) * scaling
            mask = grp_ref[rows, :] == g
            m_prev = m_ref[rows, :]
            m_cand = jnp.maximum(m_prev, jnp.max(s, axis=1, keepdims=True))
            p = jnp.exp(s - m_cand[:, :1])
            alpha = jnp.exp(m_prev - m_cand)
            l_ref[rows, :] = jnp.where(
                mask, alpha * l_ref[rows, :] + jnp.sum(p, axis=1, keepdims=True), l_ref[rows, :]
            )
            acc_ref[rows, :] = jnp.where(
                mask,
                alpha * acc_ref[rows, :]
                + jnp.dot(p.astype(jnp.bfloat16), v, preferred_element_type=jnp.float32),
                acc_ref[rows, :],
            )
            m_ref[rows, :] = jnp.where(mask, m_cand, m_prev)

        return carry

    lax.fori_loop(0, block_count, body, 0)


def attend_prefix_local(query_rows, query_group, prefix_k, prefix_v):
    row_count = query_rows.shape[0]
    span = prefix_k.shape[1]
    block_count = row_count // QUERY_BLOCK
    present = jnp.any(
        query_group.reshape(block_count, QUERY_BLOCK, 1)
        == jnp.arange(G, dtype=jnp.int32)[None, None, :],
        axis=1,
    ).astype(jnp.int32).reshape(-1)
    grp = jnp.broadcast_to(query_group[:, None], (row_count, HEAD))
    full = lambda g, kb, pr: (0, 0)
    kv_spec = pl.BlockSpec((1, KEY_BLOCK, HEAD), lambda g, kb, pr: (g, kb, 0))
    out_shape = jax.ShapeDtypeStruct((row_count, HEAD), jnp.float32)
    acc, maxima, totals = pl.pallas_call(
        prefix_kernel,
        grid_spec=pltpu.PrefetchScalarGridSpec(
            num_scalar_prefetch=1,
            grid=(G, span // KEY_BLOCK),
            in_specs=[
                pl.BlockSpec((row_count, HEAD), full),
                pl.BlockSpec((row_count, HEAD), full),
                kv_spec,
                kv_spec,
            ],
            out_specs=[pl.BlockSpec((row_count, HEAD), full)] * 3,
        ),
        out_shape=[out_shape] * 3,
        compiler_params=pltpu.CompilerParams(dimension_semantics=("arbitrary", "arbitrary")),
        cost_estimate=pl.CostEstimate(
            flops=4 * row_count * span * HEAD * 2,
            transcendentals=row_count * span * 2,
            bytes_accessed=2 * G * span * HEAD * 2 + row_count * HEAD * 14,
        ),
    )(present, query_rows, grp, prefix_k, prefix_v)
    return (acc, maxima[:, :1], totals[:, :1])


def attend_suffix(queries, keys, values, request, position):
    row_count, columns = queries.shape
    head_count = columns // HEAD
    blocks = split_blocks(row_count)
    block_len = row_count // blocks
    scaling = 1.0 / math.sqrt(HEAD)
    key_grid = keys.reshape(row_count, head_count, HEAD)
    val_grid = values.reshape(row_count, head_count, HEAD)

    def per_block(pieces):
        block_q, block_req, block_pos = pieces
        query_grid = block_q.reshape(block_len, head_count, HEAD)
        scores = (
            jnp.einsum("qhd,khd->hqk", query_grid, key_grid, preferred_element_type=jnp.float32)
            * scaling
        )
        allowed = (request[None, :] == block_req[:, None]) & (
            position[None, :] <= block_pos[:, None]
        )
        scores = jnp.where(allowed[None, :, :], scores, NEG)
        maxima = jnp.max(scores, axis=2)
        exp_terms = jnp.exp(scores - maxima[:, :, None])
        totals = jnp.sum(exp_terms, axis=2)
        weighted = jnp.einsum(
            "hqk,khd->qhd",
            exp_terms.astype(jnp.bfloat16),
            val_grid,
            preferred_element_type=jnp.float32,
        )
        return (weighted.reshape(block_len, columns), maxima.T, totals.T)

    weighted, maxima, totals = lax.map(
        per_block,
        (
            queries.reshape(blocks, block_len, columns),
            request.reshape(blocks, block_len),
            position.reshape(blocks, block_len),
        ),
    )
    return (
        weighted.reshape(row_count, columns),
        maxima.reshape(row_count, head_count),
        totals.reshape(row_count, head_count),
    )


def combine(former, latter):
    weighted_a, maxima_a, totals_a = former
    weighted_b, maxima_b, totals_b = latter
    row_count, head_count = maxima_a.shape
    maxima = jnp.maximum(maxima_a, maxima_b)
    factor_a = jnp.exp(maxima_a - maxima)
    factor_b = jnp.exp(maxima_b - maxima)
    weighted = (
        weighted_a.reshape(row_count, head_count, HEAD) * factor_a[:, :, None]
        + weighted_b.reshape(row_count, head_count, HEAD) * factor_b[:, :, None]
    )
    return (
        weighted.reshape(row_count, head_count * HEAD),
        maxima,
        totals_a * factor_a + totals_b * factor_b,
    )


def per_device(
    queries,
    keys,
    values,
    prefix_keys,
    prefix_values,
    lengths,
    groups,
    residual,
    out_proj,
    norm_gain,
    expert_ids,
    expert_gates,
    w_gate,
    w_up,
    w_down,
):
    row_tok, columns = queries.shape
    head_count = columns // HEAD
    tok_dev = residual.shape[0]
    request, position, tok_group = token_layout(lengths, groups)
    request, position, tok_group = (request[0], position[0], tok_group[0])
    prefix_part = attend_prefix_local(
        queries,
        tok_group,
        lax.all_gather(prefix_keys, "req", axis=1, tiled=True),
        lax.all_gather(prefix_values, "req", axis=1, tiled=True),
    )
    suffix_part = attend_suffix(queries, keys, values, request, position)
    weighted, maxima, totals = combine(prefix_part, suffix_part)
    attended = (
        (weighted.reshape(row_tok, head_count, HEAD) / totals[:, :, None])
        .reshape(row_tok, columns)
        .astype(jnp.bfloat16)
    )
    exp_count = lax.axis_size("exp")
    full_proj = lax.all_gather(out_proj, "exp", axis=0, tiled=True)
    token_rows = lax.all_to_all(attended, "exp", split_axis=0, concat_axis=1, tiled=True)
    projected = jnp.dot(token_rows, full_proj, preferred_element_type=jnp.float32)
    stream = residual.astype(jnp.float32) + projected
    meansq = jnp.mean(stream * stream, axis=-1, keepdims=True)
    normed = (stream * lax.rsqrt(meansq + 1e-06) * norm_gain.astype(jnp.float32)).astype(
        jnp.bfloat16
    )
    capacity = max(2, tok_dev // 4)
    slot_count = EXPERTS * capacity
    flat_ids = expert_ids.reshape(-1)
    onehot = (flat_ids[:, None] == jnp.arange(EXPERTS, dtype=jnp.int32)[None, :]).astype(jnp.int32)
    slot_of = jnp.sum(onehot * (jnp.cumsum(onehot, axis=0) - 1), axis=1)
    dest = flat_ids * capacity + slot_of
    dest_hot = dest[:, None] == jnp.arange(slot_count, dtype=jnp.int32)[None, :]
    select = jnp.sum(dest_hot.reshape(tok_dev, TOPK, slot_count).astype(jnp.float32), axis=1)
    buffer = jnp.dot(
        select.T.astype(jnp.bfloat16), normed, preferred_element_type=jnp.float32
    ).astype(jnp.bfloat16).reshape(EXPERTS, capacity, normed.shape[1])
    exp_dev = w_gate.shape[0]
    received = lax.all_to_all(buffer, "exp", split_axis=0, concat_axis=0, tiled=True)
    slots = received.shape[1]
    grid_in = received.reshape(exp_count, exp_dev, slots, received.shape[2])
    gate_h = jnp.einsum("secd,edf->secf", grid_in, w_gate, preferred_element_type=jnp.float32)
    up_h = jnp.einsum("secd,edf->secf", grid_in, w_up, preferred_element_type=jnp.float32)
    hidden = (jax.nn.silu(gate_h) * up_h).astype(jnp.bfloat16)
    expert_out = jnp.einsum("secf,efd->secd", hidden, w_down, preferred_element_type=jnp.float32)
    returned = lax.all_to_all(
        expert_out.astype(jnp.bfloat16).reshape(EXPERTS, slots, received.shape[2]),
        "exp",
        split_axis=0,
        concat_axis=0,
        tiled=True,
    )
    gates = expert_gates.astype(jnp.float32).reshape(tok_dev, TOPK, 1)
    weights = jnp.sum(dest_hot.reshape(tok_dev, TOPK, slot_count).astype(jnp.float32) * gates, axis=1)
    mixture = jnp.dot(
        weights.astype(jnp.bfloat16),
        returned.reshape(slot_count, received.shape[2]),
        preferred_element_type=jnp.float32,
    )
    return (stream + mixture).astype(jnp.bfloat16)


def solution(mesh):
    in_specs = (
        P("req", "exp"),
        P("req", "exp"),
        P("req", "exp"),
        P(None, "req", "exp"),
        P(None, "req", "exp"),
        P("req", None),
        P("req", None),
        P(("req", "exp"), None),
        P("exp", None),
        P(),
        P(("req", "exp"), None),
        P(("req", "exp"), None),
        P("exp", None, None),
        P("exp", None, None),
        P("exp", None, None),
    )
    out_specs = P(("req", "exp"), None)
    return jax.shard_map(
        per_device, mesh=mesh, in_specs=in_specs, out_specs=out_specs, check_vma=False
    )
```

```python
import math

import jax
import jax.numpy as jnp
from jax import lax
from jax.experimental import pallas as pl
from jax.experimental.pallas import tpu as pltpu
from jax.sharding import PartitionSpec as P

HEAD = 128
TOPK = 4
EXPERTS = 32
G = 4
RQ = 8
ROW_TOK = 1024


NEG = -1e30


def token_layout(lengths, groups):
    req_ends = jnp.cumsum(lengths, axis=-1)
    starts = req_ends - lengths
    position = jnp.arange(ROW_TOK, dtype=jnp.int32)
    request = jnp.sum((position[None, :, None] >= req_ends[:, None, :]).astype(jnp.int32), axis=-1)
    onehot = request[:, :, None] == jnp.arange(RQ, dtype=jnp.int32)[None, None, :]
    first_tok = jnp.sum(jnp.where(onehot, starts[:, None, :], 0), axis=-1)
    tok_group = jnp.sum(jnp.where(onehot, groups[:, None, :], 0), axis=-1)
    return (request, position[None, :] - first_tok, tok_group)


def split_blocks(row_count):
    if row_count % 1024 == 0 and row_count > 1024:
        return row_count // 1024
    return 1


def pack_parts(parts):
    return jnp.concatenate([parts[0], parts[1], parts[2]], axis=1)


def unpack_parts(packed, head_count):
    columns = head_count * HEAD
    return (
        packed[:, :columns],
        packed[:, columns : columns + head_count],
        packed[:, columns + head_count :],
    )


def attend_prefix(query_rows, query_group, prefix_k, prefix_v):
    row_count, columns = query_rows.shape
    head_count = columns // HEAD
    span = prefix_k.shape[1]
    key_grid = prefix_k.reshape(G, span, head_count, HEAD)
    val_grid = prefix_v.reshape(G, span, head_count, HEAD)
    blocks = split_blocks(row_count)
    block_len = row_count // blocks
    scaling = 1.0 / math.sqrt(HEAD)

    def per_block(pieces):
        block_q, block_g = pieces
        query_grid = block_q.reshape(block_len, head_count, HEAD)
        scores = (
            jnp.einsum("qhd,gkhd->hqgk", query_grid, key_grid, preferred_element_type=jnp.float32)
            * scaling
        )
        member = block_g[:, None] == jnp.arange(G, dtype=jnp.int32)[None, :]
        scores = jnp.where(member[None, :, :, None], scores, NEG)
        maxima = jnp.max(scores, axis=(2, 3))
        exp_terms = jnp.exp(scores - maxima[:, :, None, None])
        totals = jnp.sum(exp_terms, axis=(2, 3))
        weighted = jnp.einsum(
            "hqgk,gkhd->qhd",
            exp_terms.astype(jnp.bfloat16),
            val_grid,
            preferred_element_type=jnp.float32,
        )
        return (weighted.reshape(block_len, columns), maxima.T, totals.T)

    weighted, maxima, totals = lax.map(
        per_block,
        (query_rows.reshape(blocks, block_len, columns), query_group.reshape(blocks, block_len)),
    )
    return (
        weighted.reshape(row_count, columns),
        maxima.reshape(row_count, head_count),
        totals.reshape(row_count, head_count),
    )


QUERY_BLOCK = 128
KEY_BLOCK = 2048


def prefix_kernel(present_ref, q_ref, grp_ref, k_ref, v_ref, acc_ref, m_ref, l_ref):
    g = pl.program_id(0)
    kb = pl.program_id(1)
    scaling = 1.0 / math.sqrt(HEAD)

    @pl.when((g == 0) & (kb == 0))
    def _():
        acc_ref[...] = jnp.zeros_like(acc_ref)
        m_ref[...] = jnp.full_like(m_ref, NEG)
        l_ref[...] = jnp.zeros_like(l_ref)

    k = k_ref[0]
    v = v_ref[0]
    block_count = q_ref.shape[0] // QUERY_BLOCK

    def body(qb, carry):
        @pl.when(present_ref[qb * G + g] > 0)
        def _():
            rows = pl.ds(pl.multiple_of(qb * QUERY_BLOCK, QUERY_BLOCK), QUERY_BLOCK)
            s = lax.dot_general(
                q_ref[rows, :], k, (((1,), (1,)), ((), ())), preferred_element_type=jnp.float32
            ) * scaling
            mask = grp_ref[rows, :] == g
            m_prev = m_ref[rows, :]
            m_cand = jnp.maximum(m_prev, jnp.max(s, axis=1, keepdims=True))
            p = jnp.exp(s - m_cand[:, :1])
            alpha = jnp.exp(m_prev - m_cand)
            l_ref[rows, :] = jnp.where(
                mask, alpha * l_ref[rows, :] + jnp.sum(p, axis=1, keepdims=True), l_ref[rows, :]
            )
            acc_ref[rows, :] = jnp.where(
                mask,
                alpha * acc_ref[rows, :]
                + jnp.dot(p.astype(jnp.bfloat16), v, preferred_element_type=jnp.float32),
                acc_ref[rows, :],
            )
            m_ref[rows, :] = jnp.where(mask, m_cand, m_prev)

        return carry

    lax.fori_loop(0, block_count, body, 0)


def attend_prefix_local(query_rows, query_group, prefix_k, prefix_v):
    row_count = query_rows.shape[0]
    span = prefix_k.shape[1]
    block_count = row_count // QUERY_BLOCK
    present = jnp.any(
        query_group.reshape(block_count, QUERY_BLOCK, 1)
        == jnp.arange(G, dtype=jnp.int32)[None, None, :],
        axis=1,
    ).astype(jnp.int32).reshape(-1)
    grp = jnp.broadcast_to(query_group[:, None], (row_count, HEAD))
    full = lambda g, kb, pr: (0, 0)
    kv_spec = pl.BlockSpec((1, KEY_BLOCK, HEAD), lambda g, kb, pr: (g, kb, 0))
    out_shape = jax.ShapeDtypeStruct((row_count, HEAD), jnp.float32)
    acc, maxima, totals = pl.pallas_call(
        prefix_kernel,
        grid_spec=pltpu.PrefetchScalarGridSpec(
            num_scalar_prefetch=1,
            grid=(G, span // KEY_BLOCK),
            in_specs=[
                pl.BlockSpec((row_count, HEAD), full),
                pl.BlockSpec((row_count, HEAD), full),
                kv_spec,
                kv_spec,
            ],
            out_specs=[pl.BlockSpec((row_count, HEAD), full)] * 3,
        ),
        out_shape=[out_shape] * 3,
        compiler_params=pltpu.CompilerParams(dimension_semantics=("arbitrary", "arbitrary")),
        cost_estimate=pl.CostEstimate(
            flops=4 * row_count * span * HEAD * 2,
            transcendentals=row_count * span * 2,
            bytes_accessed=2 * G * span * HEAD * 2 + row_count * HEAD * 14,
        ),
    )(present, query_rows, grp, prefix_k, prefix_v)
    return (acc, maxima[:, :1], totals[:, :1])


def attend_suffix(queries, keys, values, request, position):
    row_count, columns = queries.shape
    head_count = columns // HEAD
    blocks = split_blocks(row_count)
    block_len = row_count // blocks
    scaling = 1.0 / math.sqrt(HEAD)
    key_grid = keys.reshape(row_count, head_count, HEAD)
    val_grid = values.reshape(row_count, head_count, HEAD)

    def per_block(pieces):
        block_q, block_req, block_pos = pieces
        query_grid = block_q.reshape(block_len, head_count, HEAD)
        scores = (
            jnp.einsum("qhd,khd->hqk", query_grid, key_grid, preferred_element_type=jnp.float32)
            * scaling
        )
        allowed = (request[None, :] == block_req[:, None]) & (
            position[None, :] <= block_pos[:, None]
        )
        scores = jnp.where(allowed[None, :, :], scores, NEG)
        maxima = jnp.max(scores, axis=2)
        exp_terms = jnp.exp(scores - maxima[:, :, None])
        totals = jnp.sum(exp_terms, axis=2)
        weighted = jnp.einsum(
            "hqk,khd->qhd",
            exp_terms.astype(jnp.bfloat16),
            val_grid,
            preferred_element_type=jnp.float32,
        )
        return (weighted.reshape(block_len, columns), maxima.T, totals.T)

    weighted, maxima, totals = lax.map(
        per_block,
        (
            queries.reshape(blocks, block_len, columns),
            request.reshape(blocks, block_len),
            position.reshape(blocks, block_len),
        ),
    )
    return (
        weighted.reshape(row_count, columns),
        maxima.reshape(row_count, head_count),
        totals.reshape(row_count, head_count),
    )


def combine(former, latter):
    weighted_a, maxima_a, totals_a = former
    weighted_b, maxima_b, totals_b = latter
    row_count, head_count = maxima_a.shape
    maxima = jnp.maximum(maxima_a, maxima_b)
    factor_a = jnp.exp(maxima_a - maxima)
    factor_b = jnp.exp(maxima_b - maxima)
    weighted = (
        weighted_a.reshape(row_count, head_count, HEAD) * factor_a[:, :, None]
        + weighted_b.reshape(row_count, head_count, HEAD) * factor_b[:, :, None]
    )
    return (
        weighted.reshape(row_count, head_count * HEAD),
        maxima,
        totals_a * factor_a + totals_b * factor_b,
    )


def per_device(
    queries,
    keys,
    values,
    prefix_keys,
    prefix_values,
    lengths,
    groups,
    residual,
    out_proj,
    norm_gain,
    expert_ids,
    expert_gates,
    w_gate,
    w_up,
    w_down,
):
    row_tok, columns = queries.shape
    head_count = columns // HEAD
    tok_dev = residual.shape[0]
    request, position, tok_group = token_layout(lengths, groups)
    request, position, tok_group = (request[0], position[0], tok_group[0])
    req_count = lax.axis_size("req")
    local_kv = jnp.stack([prefix_keys, prefix_values])
    partner = [(i, i ^ 1) for i in range(req_count)]
    partner_kv = lax.ppermute(local_kv, "req", partner)
    ring_kv = jnp.concatenate(
        [
            lax.ppermute(local_kv, "req", [(i, (i + 2 * s) % req_count) for i in range(req_count)])
            for s in range(1, req_count // 2)
        ],
        axis=2,
    )
    forwarded_kv = lax.ppermute(ring_kv, "req", partner)
    prefix_part = None
    for chunk in (
        jnp.concatenate([local_kv, ring_kv], axis=2),
        jnp.concatenate([partner_kv, forwarded_kv], axis=2),
    ):
        part = attend_prefix_local(queries, tok_group, chunk[0], chunk[1])
        prefix_part = part if prefix_part is None else combine(prefix_part, part)
    suffix_part = attend_suffix(queries, keys, values, request, position)
    weighted, maxima, totals = combine(prefix_part, suffix_part)
    attended = (
        (weighted.reshape(row_tok, head_count, HEAD) / totals[:, :, None])
        .reshape(row_tok, columns)
        .astype(jnp.bfloat16)
    )
    exp_count = lax.axis_size("exp")
    full_proj = lax.all_gather(out_proj, "exp", axis=0, tiled=True)
    token_rows = lax.all_to_all(attended, "exp", split_axis=0, concat_axis=1, tiled=True)
    projected = jnp.dot(token_rows, full_proj, preferred_element_type=jnp.float32)
    stream = residual.astype(jnp.float32) + projected
    meansq = jnp.mean(stream * stream, axis=-1, keepdims=True)
    normed = (stream * lax.rsqrt(meansq + 1e-06) * norm_gain.astype(jnp.float32)).astype(
        jnp.bfloat16
    )
    capacity = max(2, tok_dev // 4)
    slot_count = EXPERTS * capacity
    flat_ids = expert_ids.reshape(-1)
    onehot = (flat_ids[:, None] == jnp.arange(EXPERTS, dtype=jnp.int32)[None, :]).astype(jnp.int32)
    slot_of = jnp.sum(onehot * (jnp.cumsum(onehot, axis=0) - 1), axis=1)
    dest = flat_ids * capacity + slot_of
    dest_hot = dest[:, None] == jnp.arange(slot_count, dtype=jnp.int32)[None, :]
    select = jnp.sum(dest_hot.reshape(tok_dev, TOPK, slot_count).astype(jnp.float32), axis=1)
    buffer = jnp.dot(
        select.T.astype(jnp.bfloat16), normed, preferred_element_type=jnp.float32
    ).astype(jnp.bfloat16).reshape(EXPERTS, capacity, normed.shape[1])
    exp_dev = w_gate.shape[0]
    received = lax.all_to_all(buffer, "exp", split_axis=0, concat_axis=0, tiled=True)
    slots = received.shape[1]
    grid_in = received.reshape(exp_count, exp_dev, slots, received.shape[2])
    gate_h = jnp.einsum("secd,edf->secf", grid_in, w_gate, preferred_element_type=jnp.float32)
    up_h = jnp.einsum("secd,edf->secf", grid_in, w_up, preferred_element_type=jnp.float32)
    hidden = (jax.nn.silu(gate_h) * up_h).astype(jnp.bfloat16)
    expert_out = jnp.einsum("secf,efd->secd", hidden, w_down, preferred_element_type=jnp.float32)
    returned = lax.all_to_all(
        expert_out.astype(jnp.bfloat16).reshape(EXPERTS, slots, received.shape[2]),
        "exp",
        split_axis=0,
        concat_axis=0,
        tiled=True,
    )
    gates = expert_gates.astype(jnp.float32).reshape(tok_dev, TOPK, 1)
    weights = jnp.sum(dest_hot.reshape(tok_dev, TOPK, slot_count).astype(jnp.float32) * gates, axis=1)
    mixture = jnp.dot(
        weights.astype(jnp.bfloat16),
        returned.reshape(slot_count, received.shape[2]),
        preferred_element_type=jnp.float32,
    )
    return (stream + mixture).astype(jnp.bfloat16)


def solution(mesh):
    in_specs = (
        P("req", "exp"),
        P("req", "exp"),
        P("req", "exp"),
        P(None, "req", "exp"),
        P(None, "req", "exp"),
        P("req", None),
        P("req", None),
        P(("req", "exp"), None),
        P("exp", None),
        P(),
        P(("req", "exp"), None),
        P(("req", "exp"), None),
        P("exp", None, None),
        P("exp", None, None),
        P("exp", None, None),
    )
    out_specs = P(("req", "exp"), None)
    return jax.shard_map(
        per_device, mesh=mesh, in_specs=in_specs, out_specs=out_specs, check_vma=False
    )
```

```python
import math

import jax
import jax.numpy as jnp
from jax import lax
from jax.experimental import pallas as pl
from jax.experimental.pallas import tpu as pltpu
from jax.sharding import PartitionSpec as P

HEAD = 128
TOPK = 4
EXPERTS = 32
G = 4
RQ = 8
ROW_TOK = 1024


NEG = -1e30


def token_layout(lengths, groups):
    req_ends = jnp.cumsum(lengths, axis=-1)
    starts = req_ends - lengths
    position = jnp.arange(ROW_TOK, dtype=jnp.int32)
    request = jnp.sum((position[None, :, None] >= req_ends[:, None, :]).astype(jnp.int32), axis=-1)
    onehot = request[:, :, None] == jnp.arange(RQ, dtype=jnp.int32)[None, None, :]
    first_tok = jnp.sum(jnp.where(onehot, starts[:, None, :], 0), axis=-1)
    tok_group = jnp.sum(jnp.where(onehot, groups[:, None, :], 0), axis=-1)
    return (request, position[None, :] - first_tok, tok_group)


def split_blocks(row_count):
    if row_count % 1024 == 0 and row_count > 1024:
        return row_count // 1024
    return 1


def pack_parts(parts):
    return jnp.concatenate([parts[0], parts[1], parts[2]], axis=1)


def unpack_parts(packed, head_count):
    columns = head_count * HEAD
    return (
        packed[:, :columns],
        packed[:, columns : columns + head_count],
        packed[:, columns + head_count :],
    )


def attend_prefix(query_rows, query_group, prefix_k, prefix_v):
    row_count, columns = query_rows.shape
    head_count = columns // HEAD
    span = prefix_k.shape[1]
    key_grid = prefix_k.reshape(G, span, head_count, HEAD)
    val_grid = prefix_v.reshape(G, span, head_count, HEAD)
    blocks = split_blocks(row_count)
    block_len = row_count // blocks
    scaling = 1.0 / math.sqrt(HEAD)

    def per_block(pieces):
        block_q, block_g = pieces
        query_grid = block_q.reshape(block_len, head_count, HEAD)
        scores = (
            jnp.einsum("qhd,gkhd->hqgk", query_grid, key_grid, preferred_element_type=jnp.float32)
            * scaling
        )
        member = block_g[:, None] == jnp.arange(G, dtype=jnp.int32)[None, :]
        scores = jnp.where(member[None, :, :, None], scores, NEG)
        maxima = jnp.max(scores, axis=(2, 3))
        exp_terms = jnp.exp(scores - maxima[:, :, None, None])
        totals = jnp.sum(exp_terms, axis=(2, 3))
        weighted = jnp.einsum(
            "hqgk,gkhd->qhd",
            exp_terms.astype(jnp.bfloat16),
            val_grid,
            preferred_element_type=jnp.float32,
        )
        return (weighted.reshape(block_len, columns), maxima.T, totals.T)

    weighted, maxima, totals = lax.map(
        per_block,
        (query_rows.reshape(blocks, block_len, columns), query_group.reshape(blocks, block_len)),
    )
    return (
        weighted.reshape(row_count, columns),
        maxima.reshape(row_count, head_count),
        totals.reshape(row_count, head_count),
    )


QUERY_BLOCK = 128
KEY_BLOCK = 2048


def prefix_kernel(present_ref, q_ref, grp_ref, k_ref, v_ref, acc_ref, m_ref, l_ref):
    g = pl.program_id(0)
    kb = pl.program_id(1)
    scaling = 1.0 / math.sqrt(HEAD)

    @pl.when((g == 0) & (kb == 0))
    def _():
        acc_ref[...] = jnp.zeros_like(acc_ref)
        m_ref[...] = jnp.full_like(m_ref, NEG)
        l_ref[...] = jnp.zeros_like(l_ref)

    k = k_ref[0]
    v = v_ref[0]
    block_count = q_ref.shape[0] // QUERY_BLOCK

    def body(qb, carry):
        @pl.when(present_ref[qb * G + g] > 0)
        def _():
            rows = pl.ds(pl.multiple_of(qb * QUERY_BLOCK, QUERY_BLOCK), QUERY_BLOCK)
            s = lax.dot_general(
                q_ref[rows, :], k, (((1,), (1,)), ((), ())), preferred_element_type=jnp.float32
            ) * scaling
            mask = grp_ref[rows, :] == g
            m_prev = m_ref[rows, :]
            m_cand = jnp.maximum(m_prev, jnp.max(s, axis=1, keepdims=True))
            p = jnp.exp(s - m_cand[:, :1])
            alpha = jnp.exp(m_prev - m_cand)
            l_ref[rows, :] = jnp.where(
                mask, alpha * l_ref[rows, :] + jnp.sum(p, axis=1, keepdims=True), l_ref[rows, :]
            )
            acc_ref[rows, :] = jnp.where(
                mask,
                alpha * acc_ref[rows, :]
                + jnp.dot(p.astype(jnp.bfloat16), v, preferred_element_type=jnp.float32),
                acc_ref[rows, :],
            )
            m_ref[rows, :] = jnp.where(mask, m_cand, m_prev)

        return carry

    lax.fori_loop(0, block_count, body, 0)


def attend_prefix_local(query_rows, query_group, prefix_k, prefix_v):
    row_count = query_rows.shape[0]
    span = prefix_k.shape[1]
    block_count = row_count // QUERY_BLOCK
    present = jnp.any(
        query_group.reshape(block_count, QUERY_BLOCK, 1)
        == jnp.arange(G, dtype=jnp.int32)[None, None, :],
        axis=1,
    ).astype(jnp.int32).reshape(-1)
    grp = jnp.broadcast_to(query_group[:, None], (row_count, HEAD))
    full = lambda g, kb, pr: (0, 0)
    kv_spec = pl.BlockSpec((1, KEY_BLOCK, HEAD), lambda g, kb, pr: (g, kb, 0))
    out_shape = jax.ShapeDtypeStruct((row_count, HEAD), jnp.float32)
    acc, maxima, totals = pl.pallas_call(
        prefix_kernel,
        grid_spec=pltpu.PrefetchScalarGridSpec(
            num_scalar_prefetch=1,
            grid=(G, span // KEY_BLOCK),
            in_specs=[
                pl.BlockSpec((row_count, HEAD), full),
                pl.BlockSpec((row_count, HEAD), full),
                kv_spec,
                kv_spec,
            ],
            out_specs=[pl.BlockSpec((row_count, HEAD), full)] * 3,
        ),
        out_shape=[out_shape] * 3,
        compiler_params=pltpu.CompilerParams(dimension_semantics=("arbitrary", "arbitrary")),
        cost_estimate=pl.CostEstimate(
            flops=4 * row_count * span * HEAD * 2,
            transcendentals=row_count * span * 2,
            bytes_accessed=2 * G * span * HEAD * 2 + row_count * HEAD * 14,
        ),
    )(present, query_rows, grp, prefix_k, prefix_v)
    return (acc, maxima[:, :1], totals[:, :1])


def attend_suffix(queries, keys, values, request, position):
    row_count, columns = queries.shape
    head_count = columns // HEAD
    blocks = split_blocks(row_count)
    block_len = row_count // blocks
    scaling = 1.0 / math.sqrt(HEAD)
    key_grid = keys.reshape(row_count, head_count, HEAD)
    val_grid = values.reshape(row_count, head_count, HEAD)

    def per_block(pieces):
        block_q, block_req, block_pos = pieces
        query_grid = block_q.reshape(block_len, head_count, HEAD)
        scores = (
            jnp.einsum("qhd,khd->hqk", query_grid, key_grid, preferred_element_type=jnp.float32)
            * scaling
        )
        allowed = (request[None, :] == block_req[:, None]) & (
            position[None, :] <= block_pos[:, None]
        )
        scores = jnp.where(allowed[None, :, :], scores, NEG)
        maxima = jnp.max(scores, axis=2)
        exp_terms = jnp.exp(scores - maxima[:, :, None])
        totals = jnp.sum(exp_terms, axis=2)
        weighted = jnp.einsum(
            "hqk,khd->qhd",
            exp_terms.astype(jnp.bfloat16),
            val_grid,
            preferred_element_type=jnp.float32,
        )
        return (weighted.reshape(block_len, columns), maxima.T, totals.T)

    weighted, maxima, totals = lax.map(
        per_block,
        (
            queries.reshape(blocks, block_len, columns),
            request.reshape(blocks, block_len),
            position.reshape(blocks, block_len),
        ),
    )
    return (
        weighted.reshape(row_count, columns),
        maxima.reshape(row_count, head_count),
        totals.reshape(row_count, head_count),
    )


def combine(former, latter):
    weighted_a, maxima_a, totals_a = former
    weighted_b, maxima_b, totals_b = latter
    row_count, head_count = maxima_a.shape
    maxima = jnp.maximum(maxima_a, maxima_b)
    factor_a = jnp.exp(maxima_a - maxima)
    factor_b = jnp.exp(maxima_b - maxima)
    weighted = (
        weighted_a.reshape(row_count, head_count, HEAD) * factor_a[:, :, None]
        + weighted_b.reshape(row_count, head_count, HEAD) * factor_b[:, :, None]
    )
    return (
        weighted.reshape(row_count, head_count * HEAD),
        maxima,
        totals_a * factor_a + totals_b * factor_b,
    )


def per_device(
    queries,
    keys,
    values,
    prefix_keys,
    prefix_values,
    lengths,
    groups,
    residual,
    out_proj,
    norm_gain,
    expert_ids,
    expert_gates,
    w_gate,
    w_up,
    w_down,
):
    row_tok, columns = queries.shape
    head_count = columns // HEAD
    tok_dev = residual.shape[0]
    request, position, tok_group = token_layout(lengths, groups)
    request, position, tok_group = (request[0], position[0], tok_group[0])
    req_count = lax.axis_size("req")
    local_kv = jnp.stack([prefix_keys, prefix_values])
    partner = [(i, i ^ 1) for i in range(req_count)]
    partner_kv = lax.ppermute(local_kv, "req", partner)
    ring_kv = jnp.concatenate(
        [
            lax.ppermute(local_kv, "req", [(i, (i + 2 * s) % req_count) for i in range(req_count)])
            for s in range(1, req_count // 2)
        ],
        axis=2,
    )
    forwarded_kv = lax.ppermute(ring_kv, "req", partner)
    prefix_part = None
    for chunk in (
        jnp.concatenate([local_kv, ring_kv], axis=2),
        jnp.concatenate([partner_kv, forwarded_kv], axis=2),
    ):
        part = attend_prefix_local(queries, tok_group, chunk[0], chunk[1])
        prefix_part = part if prefix_part is None else combine(prefix_part, part)
    suffix_part = attend_suffix(queries, keys, values, request, position)
    weighted, maxima, totals = combine(prefix_part, suffix_part)
    attended = (
        (weighted.reshape(row_tok, head_count, HEAD) / totals[:, :, None])
        .reshape(row_tok, columns)
        .astype(jnp.bfloat16)
    )
    exp_count = lax.axis_size("exp")
    full_proj = lax.all_gather(out_proj, "exp", axis=0, tiled=True)
    token_rows = lax.all_to_all(attended, "exp", split_axis=0, concat_axis=1, tiled=True)
    projected = jnp.dot(token_rows, full_proj, preferred_element_type=jnp.float32)
    stream = residual.astype(jnp.float32) + projected
    meansq = jnp.mean(stream * stream, axis=-1, keepdims=True)
    normed = (stream * lax.rsqrt(meansq + 1e-06) * norm_gain.astype(jnp.float32)).astype(
        jnp.bfloat16
    )
    capacity = max(2, tok_dev // 4)
    slot_count = EXPERTS * capacity
    flat_ids = expert_ids.reshape(-1)
    onehot = (flat_ids[:, None] == jnp.arange(EXPERTS, dtype=jnp.int32)[None, :]).astype(jnp.int32)
    slot_of = jnp.sum(onehot * (jnp.cumsum(onehot, axis=0) - 1), axis=1)
    dest = flat_ids * capacity + slot_of
    dest_hot = dest[:, None] == jnp.arange(slot_count, dtype=jnp.int32)[None, :]
    select = jnp.sum(dest_hot.reshape(tok_dev, TOPK, slot_count).astype(jnp.float32), axis=1)
    buffer = jnp.dot(
        select.T.astype(jnp.bfloat16), normed, preferred_element_type=jnp.float32
    ).astype(jnp.bfloat16).reshape(EXPERTS, capacity, normed.shape[1])
    exp_dev = w_gate.shape[0]
    halves = 2
    piece = capacity // halves
    returned_parts = []
    for half in range(halves):
        received = lax.all_to_all(
            buffer[:, half * piece : (half + 1) * piece], "exp", split_axis=0, concat_axis=0, tiled=True
        )
        grid_in = received.reshape(exp_count, exp_dev, piece, received.shape[2])
        gate_h = jnp.einsum("secd,edf->secf", grid_in, w_gate, preferred_element_type=jnp.float32)
        up_h = jnp.einsum("secd,edf->secf", grid_in, w_up, preferred_element_type=jnp.float32)
        hidden = (jax.nn.silu(gate_h) * up_h).astype(jnp.bfloat16)
        expert_out = jnp.einsum("secf,efd->secd", hidden, w_down, preferred_element_type=jnp.float32)
        returned_parts.append(
            lax.all_to_all(
                expert_out.astype(jnp.bfloat16).reshape(EXPERTS, piece, received.shape[2]),
                "exp",
                split_axis=0,
                concat_axis=0,
                tiled=True,
            )
        )
    returned = jnp.concatenate(returned_parts, axis=1)
    gates = expert_gates.astype(jnp.float32).reshape(tok_dev, TOPK, 1)
    weights = jnp.sum(dest_hot.reshape(tok_dev, TOPK, slot_count).astype(jnp.float32) * gates, axis=1)
    mixture = jnp.dot(
        weights.astype(jnp.bfloat16),
        returned.reshape(slot_count, received.shape[2]),
        preferred_element_type=jnp.float32,
    )
    return (stream + mixture).astype(jnp.bfloat16)


def solution(mesh):
    in_specs = (
        P("req", "exp"),
        P("req", "exp"),
        P("req", "exp"),
        P(None, "req", "exp"),
        P(None, "req", "exp"),
        P("req", None),
        P("req", None),
        P(("req", "exp"), None),
        P("exp", None),
        P(),
        P(("req", "exp"), None),
        P(("req", "exp"), None),
        P("exp", None, None),
        P("exp", None, None),
        P("exp", None, None),
    )
    out_specs = P(("req", "exp"), None)
    return jax.shard_map(
        per_device, mesh=mesh, in_specs=in_specs, out_specs=out_specs, check_vma=False
    )
```

```python
import math

import jax
import jax.numpy as jnp
from jax import lax
from jax.experimental import pallas as pl
from jax.experimental.pallas import tpu as pltpu
from jax.sharding import PartitionSpec as P

HEAD = 128
TOPK = 4
EXPERTS = 32
G = 4
RQ = 8
ROW_TOK = 1024


NEG = -1e30


def token_layout(lengths, groups):
    req_ends = jnp.cumsum(lengths, axis=-1)
    starts = req_ends - lengths
    position = jnp.arange(ROW_TOK, dtype=jnp.int32)
    request = jnp.sum((position[None, :, None] >= req_ends[:, None, :]).astype(jnp.int32), axis=-1)
    onehot = request[:, :, None] == jnp.arange(RQ, dtype=jnp.int32)[None, None, :]
    first_tok = jnp.sum(jnp.where(onehot, starts[:, None, :], 0), axis=-1)
    tok_group = jnp.sum(jnp.where(onehot, groups[:, None, :], 0), axis=-1)
    return (request, position[None, :] - first_tok, tok_group)


def split_blocks(row_count):
    if row_count % 1024 == 0 and row_count > 1024:
        return row_count // 1024
    return 1


def pack_parts(parts):
    return jnp.concatenate([parts[0], parts[1], parts[2]], axis=1)


def unpack_parts(packed, head_count):
    columns = head_count * HEAD
    return (
        packed[:, :columns],
        packed[:, columns : columns + head_count],
        packed[:, columns + head_count :],
    )


def attend_prefix(query_rows, query_group, prefix_k, prefix_v):
    row_count, columns = query_rows.shape
    head_count = columns // HEAD
    span = prefix_k.shape[1]
    key_grid = prefix_k.reshape(G, span, head_count, HEAD)
    val_grid = prefix_v.reshape(G, span, head_count, HEAD)
    blocks = split_blocks(row_count)
    block_len = row_count // blocks
    scaling = 1.0 / math.sqrt(HEAD)

    def per_block(pieces):
        block_q, block_g = pieces
        query_grid = block_q.reshape(block_len, head_count, HEAD)
        scores = (
            jnp.einsum("qhd,gkhd->hqgk", query_grid, key_grid, preferred_element_type=jnp.float32)
            * scaling
        )
        member = block_g[:, None] == jnp.arange(G, dtype=jnp.int32)[None, :]
        scores = jnp.where(member[None, :, :, None], scores, NEG)
        maxima = jnp.max(scores, axis=(2, 3))
        exp_terms = jnp.exp(scores - maxima[:, :, None, None])
        totals = jnp.sum(exp_terms, axis=(2, 3))
        weighted = jnp.einsum(
            "hqgk,gkhd->qhd",
            exp_terms.astype(jnp.bfloat16),
            val_grid,
            preferred_element_type=jnp.float32,
        )
        return (weighted.reshape(block_len, columns), maxima.T, totals.T)

    weighted, maxima, totals = lax.map(
        per_block,
        (query_rows.reshape(blocks, block_len, columns), query_group.reshape(blocks, block_len)),
    )
    return (
        weighted.reshape(row_count, columns),
        maxima.reshape(row_count, head_count),
        totals.reshape(row_count, head_count),
    )


QUERY_BLOCK = 128
KEY_BLOCK = 2048


def prefix_kernel(present_ref, q_ref, grp_ref, k_ref, v_ref, acc_ref, m_ref, l_ref):
    g = pl.program_id(0)
    kb = pl.program_id(1)
    scaling = 1.0 / math.sqrt(HEAD)

    @pl.when((g == 0) & (kb == 0))
    def _():
        acc_ref[...] = jnp.zeros_like(acc_ref)
        m_ref[...] = jnp.full_like(m_ref, NEG)
        l_ref[...] = jnp.zeros_like(l_ref)

    k = k_ref[0]
    v = v_ref[0]
    block_count = q_ref.shape[0] // QUERY_BLOCK

    def body(qb, carry):
        @pl.when(present_ref[qb * G + g] > 0)
        def _():
            rows = pl.ds(pl.multiple_of(qb * QUERY_BLOCK, QUERY_BLOCK), QUERY_BLOCK)
            s = lax.dot_general(
                q_ref[rows, :], k, (((1,), (1,)), ((), ())), preferred_element_type=jnp.float32
            ) * scaling
            mask = grp_ref[rows, :] == g
            m_prev = m_ref[rows, :]
            m_cand = jnp.maximum(m_prev, jnp.max(s, axis=1, keepdims=True))
            p = jnp.exp(s - m_cand[:, :1])
            alpha = jnp.exp(m_prev - m_cand)
            l_ref[rows, :] = jnp.where(
                mask, alpha * l_ref[rows, :] + jnp.sum(p, axis=1, keepdims=True), l_ref[rows, :]
            )
            acc_ref[rows, :] = jnp.where(
                mask,
                alpha * acc_ref[rows, :]
                + jnp.dot(p.astype(jnp.bfloat16), v, preferred_element_type=jnp.float32),
                acc_ref[rows, :],
            )
            m_ref[rows, :] = jnp.where(mask, m_cand, m_prev)

        return carry

    lax.fori_loop(0, block_count, body, 0)


def attend_prefix_local(query_rows, query_group, prefix_k, prefix_v):
    row_count = query_rows.shape[0]
    span = prefix_k.shape[1]
    block_count = row_count // QUERY_BLOCK
    present = jnp.any(
        query_group.reshape(block_count, QUERY_BLOCK, 1)
        == jnp.arange(G, dtype=jnp.int32)[None, None, :],
        axis=1,
    ).astype(jnp.int32).reshape(-1)
    grp = jnp.broadcast_to(query_group[:, None], (row_count, HEAD))
    full = lambda g, kb, pr: (0, 0)
    kv_spec = pl.BlockSpec((1, KEY_BLOCK, HEAD), lambda g, kb, pr: (g, kb, 0))
    out_shape = jax.ShapeDtypeStruct((row_count, HEAD), jnp.float32)
    acc, maxima, totals = pl.pallas_call(
        prefix_kernel,
        grid_spec=pltpu.PrefetchScalarGridSpec(
            num_scalar_prefetch=1,
            grid=(G, span // KEY_BLOCK),
            in_specs=[
                pl.BlockSpec((row_count, HEAD), full),
                pl.BlockSpec((row_count, HEAD), full),
                kv_spec,
                kv_spec,
            ],
            out_specs=[pl.BlockSpec((row_count, HEAD), full)] * 3,
        ),
        out_shape=[out_shape] * 3,
        compiler_params=pltpu.CompilerParams(dimension_semantics=("arbitrary", "arbitrary")),
        cost_estimate=pl.CostEstimate(
            flops=4 * row_count * span * HEAD * 2,
            transcendentals=row_count * span * 2,
            bytes_accessed=2 * G * span * HEAD * 2 + row_count * HEAD * 14,
        ),
    )(present, query_rows, grp, prefix_k, prefix_v)
    return (acc, maxima[:, :1], totals[:, :1])


def expert_kernel(x_ref, wg_ref, wu_ref, wd_ref, o_ref):
    x = x_ref[0]
    gate_h = jnp.dot(x, wg_ref[0], preferred_element_type=jnp.float32)
    up_h = jnp.dot(x, wu_ref[0], preferred_element_type=jnp.float32)
    hidden = (gate_h / (1.0 + jnp.exp(-gate_h)) * up_h).astype(jnp.bfloat16)
    o_ref[0] = jnp.dot(hidden, wd_ref[0], preferred_element_type=jnp.float32).astype(o_ref.dtype)


def expert_ffn(rows, w_gate, w_up, w_down):
    exp_dev, row_count, width = rows.shape
    inner = w_gate.shape[2]
    return pl.pallas_call(
        expert_kernel,
        grid=(exp_dev,),
        in_specs=[
            pl.BlockSpec((1, row_count, width), lambda e: (e, 0, 0)),
            pl.BlockSpec((1, width, inner), lambda e: (e, 0, 0)),
            pl.BlockSpec((1, width, inner), lambda e: (e, 0, 0)),
            pl.BlockSpec((1, inner, width), lambda e: (e, 0, 0)),
        ],
        out_specs=pl.BlockSpec((1, row_count, width), lambda e: (e, 0, 0)),
        out_shape=jax.ShapeDtypeStruct((exp_dev, row_count, width), jnp.bfloat16),
        compiler_params=pltpu.CompilerParams(
            dimension_semantics=("arbitrary",), vmem_limit_bytes=56 * 1024 * 1024
        ),
        cost_estimate=pl.CostEstimate(
            flops=6 * exp_dev * row_count * width * inner,
            transcendentals=exp_dev * row_count * inner,
            bytes_accessed=exp_dev * (3 * width * inner + 2 * row_count * width) * 2,
        ),
    )(rows, w_gate, w_up, w_down)


def attend_suffix(queries, keys, values, request, position):
    row_count, columns = queries.shape
    head_count = columns // HEAD
    blocks = split_blocks(row_count)
    block_len = row_count // blocks
    scaling = 1.0 / math.sqrt(HEAD)
    key_grid = keys.reshape(row_count, head_count, HEAD)
    val_grid = values.reshape(row_count, head_count, HEAD)

    def per_block(pieces):
        block_q, block_req, block_pos = pieces
        query_grid = block_q.reshape(block_len, head_count, HEAD)
        scores = (
            jnp.einsum("qhd,khd->hqk", query_grid, key_grid, preferred_element_type=jnp.float32)
            * scaling
        )
        allowed = (request[None, :] == block_req[:, None]) & (
            position[None, :] <= block_pos[:, None]
        )
        scores = jnp.where(allowed[None, :, :], scores, NEG)
        maxima = jnp.max(scores, axis=2)
        exp_terms = jnp.exp(scores - maxima[:, :, None])
        totals = jnp.sum(exp_terms, axis=2)
        weighted = jnp.einsum(
            "hqk,khd->qhd",
            exp_terms.astype(jnp.bfloat16),
            val_grid,
            preferred_element_type=jnp.float32,
        )
        return (weighted.reshape(block_len, columns), maxima.T, totals.T)

    weighted, maxima, totals = lax.map(
        per_block,
        (
            queries.reshape(blocks, block_len, columns),
            request.reshape(blocks, block_len),
            position.reshape(blocks, block_len),
        ),
    )
    return (
        weighted.reshape(row_count, columns),
        maxima.reshape(row_count, head_count),
        totals.reshape(row_count, head_count),
    )


def combine(former, latter):
    weighted_a, maxima_a, totals_a = former
    weighted_b, maxima_b, totals_b = latter
    row_count, head_count = maxima_a.shape
    maxima = jnp.maximum(maxima_a, maxima_b)
    factor_a = jnp.exp(maxima_a - maxima)
    factor_b = jnp.exp(maxima_b - maxima)
    weighted = (
        weighted_a.reshape(row_count, head_count, HEAD) * factor_a[:, :, None]
        + weighted_b.reshape(row_count, head_count, HEAD) * factor_b[:, :, None]
    )
    return (
        weighted.reshape(row_count, head_count * HEAD),
        maxima,
        totals_a * factor_a + totals_b * factor_b,
    )


def per_device(
    queries,
    keys,
    values,
    prefix_keys,
    prefix_values,
    lengths,
    groups,
    residual,
    out_proj,
    norm_gain,
    expert_ids,
    expert_gates,
    w_gate,
    w_up,
    w_down,
):
    row_tok, columns = queries.shape
    head_count = columns // HEAD
    tok_dev = residual.shape[0]
    request, position, tok_group = token_layout(lengths, groups)
    request, position, tok_group = (request[0], position[0], tok_group[0])
    req_count = lax.axis_size("req")
    local_kv = jnp.stack([prefix_keys, prefix_values])
    partner = [(i, i ^ 1) for i in range(req_count)]
    partner_kv = lax.ppermute(local_kv, "req", partner)
    ring_kv = jnp.concatenate(
        [
            lax.ppermute(local_kv, "req", [(i, (i + 2 * s) % req_count) for i in range(req_count)])
            for s in range(1, req_count // 2)
        ],
        axis=2,
    )
    forwarded_kv = lax.ppermute(ring_kv, "req", partner)
    prefix_part = None
    for chunk in (
        jnp.concatenate([local_kv, ring_kv], axis=2),
        jnp.concatenate([partner_kv, forwarded_kv], axis=2),
    ):
        part = attend_prefix_local(queries, tok_group, chunk[0], chunk[1])
        prefix_part = part if prefix_part is None else combine(prefix_part, part)
    suffix_part = attend_suffix(queries, keys, values, request, position)
    weighted, maxima, totals = combine(prefix_part, suffix_part)
    attended = (
        (weighted.reshape(row_tok, head_count, HEAD) / totals[:, :, None])
        .reshape(row_tok, columns)
        .astype(jnp.bfloat16)
    )
    exp_count = lax.axis_size("exp")
    full_proj = lax.all_gather(out_proj, "exp", axis=0, tiled=True)
    token_rows = lax.all_to_all(attended, "exp", split_axis=0, concat_axis=1, tiled=True)
    projected = jnp.dot(token_rows, full_proj, preferred_element_type=jnp.float32)
    stream = residual.astype(jnp.float32) + projected
    meansq = jnp.mean(stream * stream, axis=-1, keepdims=True)
    normed = (stream * lax.rsqrt(meansq + 1e-06) * norm_gain.astype(jnp.float32)).astype(
        jnp.bfloat16
    )
    capacity = max(2, tok_dev // 4)
    slot_count = EXPERTS * capacity
    flat_ids = expert_ids.reshape(-1)
    onehot = (flat_ids[:, None] == jnp.arange(EXPERTS, dtype=jnp.int32)[None, :]).astype(jnp.int32)
    slot_of = jnp.sum(onehot * (jnp.cumsum(onehot, axis=0) - 1), axis=1)
    dest = flat_ids * capacity + slot_of
    dest_hot = dest[:, None] == jnp.arange(slot_count, dtype=jnp.int32)[None, :]
    select = jnp.sum(dest_hot.reshape(tok_dev, TOPK, slot_count).astype(jnp.float32), axis=1)
    buffer = jnp.dot(
        select.T.astype(jnp.bfloat16), normed, preferred_element_type=jnp.float32
    ).astype(jnp.bfloat16).reshape(EXPERTS, capacity, normed.shape[1])
    exp_dev = w_gate.shape[0]
    halves = 2
    piece = capacity // halves
    returned_parts = []
    for half in range(halves):
        received = lax.all_to_all(
            buffer[:, half * piece : (half + 1) * piece], "exp", split_axis=0, concat_axis=0, tiled=True
        )
        width = received.shape[2]
        rows = jnp.swapaxes(received.reshape(exp_count, exp_dev, piece, width), 0, 1)
        expert_out = expert_ffn(rows.reshape(exp_dev, exp_count * piece, width), w_gate, w_up, w_down)
        expert_out = jnp.swapaxes(expert_out.reshape(exp_dev, exp_count, piece, width), 0, 1)
        returned_parts.append(
            lax.all_to_all(
                expert_out.reshape(EXPERTS, piece, width),
                "exp",
                split_axis=0,
                concat_axis=0,
                tiled=True,
            )
        )
    returned = jnp.concatenate(returned_parts, axis=1)
    gates = expert_gates.astype(jnp.float32).reshape(tok_dev, TOPK, 1)
    weights = jnp.sum(dest_hot.reshape(tok_dev, TOPK, slot_count).astype(jnp.float32) * gates, axis=1)
    mixture = jnp.dot(
        weights.astype(jnp.bfloat16),
        returned.reshape(slot_count, received.shape[2]),
        preferred_element_type=jnp.float32,
    )
    return (stream + mixture).astype(jnp.bfloat16)


def solution(mesh):
    in_specs = (
        P("req", "exp"),
        P("req", "exp"),
        P("req", "exp"),
        P(None, "req", "exp"),
        P(None, "req", "exp"),
        P("req", None),
        P("req", None),
        P(("req", "exp"), None),
        P("exp", None),
        P(),
        P(("req", "exp"), None),
        P(("req", "exp"), None),
        P("exp", None, None),
        P("exp", None, None),
        P("exp", None, None),
    )
    out_specs = P(("req", "exp"), None)
    return jax.shard_map(
        per_device, mesh=mesh, in_specs=in_specs, out_specs=out_specs, check_vma=False
    )
```

```python
import math

import jax
import jax.numpy as jnp
from jax import lax
from jax.experimental import pallas as pl
from jax.experimental.pallas import tpu as pltpu
from jax.sharding import PartitionSpec as P

HEAD = 128
TOPK = 4
EXPERTS = 32
G = 4
RQ = 8
ROW_TOK = 1024


NEG = -1e30


def token_layout(lengths, groups):
    req_ends = jnp.cumsum(lengths, axis=-1)
    starts = req_ends - lengths
    position = jnp.arange(ROW_TOK, dtype=jnp.int32)
    request = jnp.sum((position[None, :, None] >= req_ends[:, None, :]).astype(jnp.int32), axis=-1)
    onehot = request[:, :, None] == jnp.arange(RQ, dtype=jnp.int32)[None, None, :]
    first_tok = jnp.sum(jnp.where(onehot, starts[:, None, :], 0), axis=-1)
    tok_group = jnp.sum(jnp.where(onehot, groups[:, None, :], 0), axis=-1)
    return (request, position[None, :] - first_tok, tok_group)


def split_blocks(row_count):
    if row_count % 1024 == 0 and row_count > 1024:
        return row_count // 1024
    return 1


def pack_parts(parts):
    return jnp.concatenate([parts[0], parts[1], parts[2]], axis=1)


def unpack_parts(packed, head_count):
    columns = head_count * HEAD
    return (
        packed[:, :columns],
        packed[:, columns : columns + head_count],
        packed[:, columns + head_count :],
    )


def attend_prefix(query_rows, query_group, prefix_k, prefix_v):
    row_count, columns = query_rows.shape
    head_count = columns // HEAD
    span = prefix_k.shape[1]
    key_grid = prefix_k.reshape(G, span, head_count, HEAD)
    val_grid = prefix_v.reshape(G, span, head_count, HEAD)
    blocks = split_blocks(row_count)
    block_len = row_count // blocks
    scaling = 1.0 / math.sqrt(HEAD)

    def per_block(pieces):
        block_q, block_g = pieces
        query_grid = block_q.reshape(block_len, head_count, HEAD)
        scores = (
            jnp.einsum("qhd,gkhd->hqgk", query_grid, key_grid, preferred_element_type=jnp.float32)
            * scaling
        )
        member = block_g[:, None] == jnp.arange(G, dtype=jnp.int32)[None, :]
        scores = jnp.where(member[None, :, :, None], scores, NEG)
        maxima = jnp.max(scores, axis=(2, 3))
        exp_terms = jnp.exp(scores - maxima[:, :, None, None])
        totals = jnp.sum(exp_terms, axis=(2, 3))
        weighted = jnp.einsum(
            "hqgk,gkhd->qhd",
            exp_terms.astype(jnp.bfloat16),
            val_grid,
            preferred_element_type=jnp.float32,
        )
        return (weighted.reshape(block_len, columns), maxima.T, totals.T)

    weighted, maxima, totals = lax.map(
        per_block,
        (query_rows.reshape(blocks, block_len, columns), query_group.reshape(blocks, block_len)),
    )
    return (
        weighted.reshape(row_count, columns),
        maxima.reshape(row_count, head_count),
        totals.reshape(row_count, head_count),
    )


QUERY_BLOCK = 128
KEY_BLOCK = 2048


def prefix_kernel(present_ref, q_ref, grp_ref, k_ref, v_ref, acc_ref, m_ref, l_ref):
    g = pl.program_id(0)
    kb = pl.program_id(1)
    scaling = 1.0 / math.sqrt(HEAD)

    @pl.when((g == 0) & (kb == 0))
    def _():
        acc_ref[...] = jnp.zeros_like(acc_ref)
        m_ref[...] = jnp.full_like(m_ref, NEG)
        l_ref[...] = jnp.zeros_like(l_ref)

    k = k_ref[0]
    v = v_ref[0]
    block_count = q_ref.shape[0] // QUERY_BLOCK

    def body(qb, carry):
        @pl.when(present_ref[qb * G + g] > 0)
        def _():
            rows = pl.ds(pl.multiple_of(qb * QUERY_BLOCK, QUERY_BLOCK), QUERY_BLOCK)
            s = lax.dot_general(
                q_ref[rows, :], k, (((1,), (1,)), ((), ())), preferred_element_type=jnp.float32
            ) * scaling
            mask = grp_ref[rows, :] == g
            m_prev = m_ref[rows, :]
            m_cand = jnp.maximum(m_prev, jnp.max(s, axis=1, keepdims=True))
            p = jnp.exp(s - m_cand[:, :1])
            alpha = jnp.exp(m_prev - m_cand)
            l_ref[rows, :] = jnp.where(
                mask, alpha * l_ref[rows, :] + jnp.sum(p, axis=1, keepdims=True), l_ref[rows, :]
            )
            acc_ref[rows, :] = jnp.where(
                mask,
                alpha * acc_ref[rows, :]
                + jnp.dot(p.astype(jnp.bfloat16), v, preferred_element_type=jnp.float32),
                acc_ref[rows, :],
            )
            m_ref[rows, :] = jnp.where(mask, m_cand, m_prev)

        return carry

    lax.fori_loop(0, block_count, body, 0)


def attend_prefix_local(query_rows, query_group, prefix_k, prefix_v):
    row_count = query_rows.shape[0]
    span = prefix_k.shape[1]
    block_count = row_count // QUERY_BLOCK
    present = jnp.any(
        query_group.reshape(block_count, QUERY_BLOCK, 1)
        == jnp.arange(G, dtype=jnp.int32)[None, None, :],
        axis=1,
    ).astype(jnp.int32).reshape(-1)
    grp = jnp.broadcast_to(query_group[:, None], (row_count, HEAD))
    full = lambda g, kb, pr: (0, 0)
    kv_spec = pl.BlockSpec((1, KEY_BLOCK, HEAD), lambda g, kb, pr: (g, kb, 0))
    out_shape = jax.ShapeDtypeStruct((row_count, HEAD), jnp.float32)
    acc, maxima, totals = pl.pallas_call(
        prefix_kernel,
        grid_spec=pltpu.PrefetchScalarGridSpec(
            num_scalar_prefetch=1,
            grid=(G, span // KEY_BLOCK),
            in_specs=[
                pl.BlockSpec((row_count, HEAD), full),
                pl.BlockSpec((row_count, HEAD), full),
                kv_spec,
                kv_spec,
            ],
            out_specs=[pl.BlockSpec((row_count, HEAD), full)] * 3,
        ),
        out_shape=[out_shape] * 3,
        compiler_params=pltpu.CompilerParams(dimension_semantics=("arbitrary", "arbitrary")),
        cost_estimate=pl.CostEstimate(
            flops=4 * row_count * span * HEAD * 2,
            transcendentals=row_count * span * 2,
            bytes_accessed=2 * G * span * HEAD * 2 + row_count * HEAD * 14,
        ),
    )(present, query_rows, grp, prefix_k, prefix_v)
    return (acc, maxima[:, :1], totals[:, :1])


def expert_kernel(x_ref, wg_ref, wu_ref, wd_ref, o_ref, total):
    f = pl.program_id(1)

    @pl.when(f == 0)
    def _():
        total[...] = jnp.zeros_like(total)

    x = x_ref[0]
    contract = (((1,), (1,)), ((), ()))
    gate_h = lax.dot_general(x, wg_ref[0], contract, preferred_element_type=jnp.float32)
    up_h = lax.dot_general(x, wu_ref[0], contract, preferred_element_type=jnp.float32)
    hidden = (gate_h / (1.0 + jnp.exp(-gate_h)) * up_h).astype(jnp.bfloat16)
    total[...] += jnp.dot(hidden, wd_ref[0], preferred_element_type=jnp.float32)

    @pl.when(f == pl.num_programs(1) - 1)
    def _():
        o_ref[0] = total[...].astype(o_ref.dtype)


FE_CHUNK = 176


def expert_ffn(rows, w_gate, w_up, w_down):
    exp_dev, row_count, width = rows.shape
    inner = w_gate.shape[2]
    chunk = FE_CHUNK if inner % FE_CHUNK == 0 else inner
    gate_t = jnp.swapaxes(w_gate, 1, 2)
    up_t = jnp.swapaxes(w_up, 1, 2)
    return pl.pallas_call(
        expert_kernel,
        grid=(exp_dev, inner // chunk),
        in_specs=[
            pl.BlockSpec((1, row_count, width), lambda e, f: (e, 0, 0)),
            pl.BlockSpec((1, chunk, width), lambda e, f: (e, f, 0)),
            pl.BlockSpec((1, chunk, width), lambda e, f: (e, f, 0)),
            pl.BlockSpec((1, chunk, width), lambda e, f: (e, f, 0)),
        ],
        out_specs=pl.BlockSpec((1, row_count, width), lambda e, f: (e, 0, 0)),
        out_shape=jax.ShapeDtypeStruct((exp_dev, row_count, width), jnp.bfloat16),
        scratch_shapes=[pltpu.VMEM((row_count, width), jnp.float32)],
        compiler_params=pltpu.CompilerParams(dimension_semantics=("arbitrary", "arbitrary")),
        cost_estimate=pl.CostEstimate(
            flops=6 * exp_dev * row_count * width * inner,
            transcendentals=exp_dev * row_count * inner,
            bytes_accessed=exp_dev * (3 * width * inner + 2 * row_count * width) * 2,
        ),
    )(rows, gate_t, up_t, w_down)


def attend_suffix(queries, keys, values, request, position):
    row_count, columns = queries.shape
    head_count = columns // HEAD
    blocks = split_blocks(row_count)
    block_len = row_count // blocks
    scaling = 1.0 / math.sqrt(HEAD)
    key_grid = keys.reshape(row_count, head_count, HEAD)
    val_grid = values.reshape(row_count, head_count, HEAD)

    def per_block(pieces):
        block_q, block_req, block_pos = pieces
        query_grid = block_q.reshape(block_len, head_count, HEAD)
        scores = (
            jnp.einsum("qhd,khd->hqk", query_grid, key_grid, preferred_element_type=jnp.float32)
            * scaling
        )
        allowed = (request[None, :] == block_req[:, None]) & (
            position[None, :] <= block_pos[:, None]
        )
        scores = jnp.where(allowed[None, :, :], scores, NEG)
        maxima = jnp.max(scores, axis=2)
        exp_terms = jnp.exp(scores - maxima[:, :, None])
        totals = jnp.sum(exp_terms, axis=2)
        weighted = jnp.einsum(
            "hqk,khd->qhd",
            exp_terms.astype(jnp.bfloat16),
            val_grid,
            preferred_element_type=jnp.float32,
        )
        return (weighted.reshape(block_len, columns), maxima.T, totals.T)

    weighted, maxima, totals = lax.map(
        per_block,
        (
            queries.reshape(blocks, block_len, columns),
            request.reshape(blocks, block_len),
            position.reshape(blocks, block_len),
        ),
    )
    return (
        weighted.reshape(row_count, columns),
        maxima.reshape(row_count, head_count),
        totals.reshape(row_count, head_count),
    )


def combine(former, latter):
    weighted_a, maxima_a, totals_a = former
    weighted_b, maxima_b, totals_b = latter
    row_count, head_count = maxima_a.shape
    maxima = jnp.maximum(maxima_a, maxima_b)
    factor_a = jnp.exp(maxima_a - maxima)
    factor_b = jnp.exp(maxima_b - maxima)
    weighted = (
        weighted_a.reshape(row_count, head_count, HEAD) * factor_a[:, :, None]
        + weighted_b.reshape(row_count, head_count, HEAD) * factor_b[:, :, None]
    )
    return (
        weighted.reshape(row_count, head_count * HEAD),
        maxima,
        totals_a * factor_a + totals_b * factor_b,
    )


def per_device(
    queries,
    keys,
    values,
    prefix_keys,
    prefix_values,
    lengths,
    groups,
    residual,
    out_proj,
    norm_gain,
    expert_ids,
    expert_gates,
    w_gate,
    w_up,
    w_down,
):
    row_tok, columns = queries.shape
    head_count = columns // HEAD
    tok_dev = residual.shape[0]
    request, position, tok_group = token_layout(lengths, groups)
    request, position, tok_group = (request[0], position[0], tok_group[0])
    req_count = lax.axis_size("req")
    local_kv = jnp.stack([prefix_keys, prefix_values])
    partner = [(i, i ^ 1) for i in range(req_count)]
    partner_kv = lax.ppermute(local_kv, "req", partner)
    ring_kv = jnp.concatenate(
        [
            lax.ppermute(local_kv, "req", [(i, (i + 2 * s) % req_count) for i in range(req_count)])
            for s in range(1, req_count // 2)
        ],
        axis=2,
    )
    forwarded_kv = lax.ppermute(ring_kv, "req", partner)
    prefix_part = None
    for chunk in (
        jnp.concatenate([local_kv, ring_kv], axis=2),
        jnp.concatenate([partner_kv, forwarded_kv], axis=2),
    ):
        part = attend_prefix_local(queries, tok_group, chunk[0], chunk[1])
        prefix_part = part if prefix_part is None else combine(prefix_part, part)
    suffix_part = attend_suffix(queries, keys, values, request, position)
    weighted, maxima, totals = combine(prefix_part, suffix_part)
    attended = (
        (weighted.reshape(row_tok, head_count, HEAD) / totals[:, :, None])
        .reshape(row_tok, columns)
        .astype(jnp.bfloat16)
    )
    exp_count = lax.axis_size("exp")
    full_proj = lax.all_gather(out_proj, "exp", axis=0, tiled=True)
    token_rows = lax.all_to_all(attended, "exp", split_axis=0, concat_axis=1, tiled=True)
    projected = jnp.dot(token_rows, full_proj, preferred_element_type=jnp.float32)
    stream = residual.astype(jnp.float32) + projected
    meansq = jnp.mean(stream * stream, axis=-1, keepdims=True)
    normed = (stream * lax.rsqrt(meansq + 1e-06) * norm_gain.astype(jnp.float32)).astype(
        jnp.bfloat16
    )
    capacity = max(2, tok_dev // 4)
    slot_count = EXPERTS * capacity
    flat_ids = expert_ids.reshape(-1)
    onehot = (flat_ids[:, None] == jnp.arange(EXPERTS, dtype=jnp.int32)[None, :]).astype(jnp.int32)
    slot_of = jnp.sum(onehot * (jnp.cumsum(onehot, axis=0) - 1), axis=1)
    dest = flat_ids * capacity + slot_of
    dest_hot = dest[:, None] == jnp.arange(slot_count, dtype=jnp.int32)[None, :]
    select = jnp.sum(dest_hot.reshape(tok_dev, TOPK, slot_count).astype(jnp.float32), axis=1)
    buffer = jnp.dot(
        select.T.astype(jnp.bfloat16), normed, preferred_element_type=jnp.float32
    ).astype(jnp.bfloat16).reshape(EXPERTS, capacity, normed.shape[1])
    exp_dev = w_gate.shape[0]
    halves = 2
    piece = capacity // halves
    returned_parts = []
    for half in range(halves):
        received = lax.all_to_all(
            buffer[:, half * piece : (half + 1) * piece], "exp", split_axis=0, concat_axis=0, tiled=True
        )
        width = received.shape[2]
        rows = jnp.swapaxes(received.reshape(exp_count, exp_dev, piece, width), 0, 1)
        expert_out = expert_ffn(rows.reshape(exp_dev, exp_count * piece, width), w_gate, w_up, w_down)
        expert_out = jnp.swapaxes(expert_out.reshape(exp_dev, exp_count, piece, width), 0, 1)
        returned_parts.append(
            lax.all_to_all(
                expert_out.reshape(EXPERTS, piece, width),
                "exp",
                split_axis=0,
                concat_axis=0,
                tiled=True,
            )
        )
    returned = jnp.concatenate(returned_parts, axis=1)
    gates = expert_gates.astype(jnp.float32).reshape(tok_dev, TOPK, 1)
    weights = jnp.sum(dest_hot.reshape(tok_dev, TOPK, slot_count).astype(jnp.float32) * gates, axis=1)
    mixture = jnp.dot(
        weights.astype(jnp.bfloat16),
        returned.reshape(slot_count, received.shape[2]),
        preferred_element_type=jnp.float32,
    )
    return (stream + mixture).astype(jnp.bfloat16)


def solution(mesh):
    in_specs = (
        P("req", "exp"),
        P("req", "exp"),
        P("req", "exp"),
        P(None, "req", "exp"),
        P(None, "req", "exp"),
        P("req", None),
        P("req", None),
        P(("req", "exp"), None),
        P("exp", None),
        P(),
        P(("req", "exp"), None),
        P(("req", "exp"), None),
        P("exp", None, None),
        P("exp", None, None),
        P("exp", None, None),
    )
    out_specs = P(("req", "exp"), None)
    return jax.shard_map(
        per_device, mesh=mesh, in_specs=in_specs, out_specs=out_specs, check_vma=False
    )
```

```python
import math

import jax
import jax.numpy as jnp
from jax import lax
from jax.experimental import pallas as pl
from jax.experimental.pallas import tpu as pltpu
from jax.sharding import PartitionSpec as P

HEAD = 128
TOPK = 4
EXPERTS = 32
G = 4
RQ = 8
ROW_TOK = 1024


NEG = -1e30


def token_layout(lengths, groups):
    req_ends = jnp.cumsum(lengths, axis=-1)
    starts = req_ends - lengths
    position = jnp.arange(ROW_TOK, dtype=jnp.int32)
    request = jnp.sum((position[None, :, None] >= req_ends[:, None, :]).astype(jnp.int32), axis=-1)
    onehot = request[:, :, None] == jnp.arange(RQ, dtype=jnp.int32)[None, None, :]
    first_tok = jnp.sum(jnp.where(onehot, starts[:, None, :], 0), axis=-1)
    tok_group = jnp.sum(jnp.where(onehot, groups[:, None, :], 0), axis=-1)
    return (request, position[None, :] - first_tok, tok_group)


def split_blocks(row_count):
    if row_count % 1024 == 0 and row_count > 1024:
        return row_count // 1024
    return 1


def pack_parts(parts):
    return jnp.concatenate([parts[0], parts[1], parts[2]], axis=1)


def unpack_parts(packed, head_count):
    columns = head_count * HEAD
    return (
        packed[:, :columns],
        packed[:, columns : columns + head_count],
        packed[:, columns + head_count :],
    )


def attend_prefix(query_rows, query_group, prefix_k, prefix_v):
    row_count, columns = query_rows.shape
    head_count = columns // HEAD
    span = prefix_k.shape[1]
    key_grid = prefix_k.reshape(G, span, head_count, HEAD)
    val_grid = prefix_v.reshape(G, span, head_count, HEAD)
    blocks = split_blocks(row_count)
    block_len = row_count // blocks
    scaling = 1.0 / math.sqrt(HEAD)

    def per_block(pieces):
        block_q, block_g = pieces
        query_grid = block_q.reshape(block_len, head_count, HEAD)
        scores = (
            jnp.einsum("qhd,gkhd->hqgk", query_grid, key_grid, preferred_element_type=jnp.float32)
            * scaling
        )
        member = block_g[:, None] == jnp.arange(G, dtype=jnp.int32)[None, :]
        scores = jnp.where(member[None, :, :, None], scores, NEG)
        maxima = jnp.max(scores, axis=(2, 3))
        exp_terms = jnp.exp(scores - maxima[:, :, None, None])
        totals = jnp.sum(exp_terms, axis=(2, 3))
        weighted = jnp.einsum(
            "hqgk,gkhd->qhd",
            exp_terms.astype(jnp.bfloat16),
            val_grid,
            preferred_element_type=jnp.float32,
        )
        return (weighted.reshape(block_len, columns), maxima.T, totals.T)

    weighted, maxima, totals = lax.map(
        per_block,
        (query_rows.reshape(blocks, block_len, columns), query_group.reshape(blocks, block_len)),
    )
    return (
        weighted.reshape(row_count, columns),
        maxima.reshape(row_count, head_count),
        totals.reshape(row_count, head_count),
    )


QUERY_BLOCK = 128
KEY_BLOCK = 2048


def prefix_kernel(present_ref, q_ref, grp_ref, k_ref, v_ref, acc_ref, m_ref, l_ref):
    g = pl.program_id(0)
    kb = pl.program_id(1)
    scaling = 1.0 / math.sqrt(HEAD)

    @pl.when((g == 0) & (kb == 0))
    def _():
        acc_ref[...] = jnp.zeros_like(acc_ref)
        m_ref[...] = jnp.full_like(m_ref, NEG)
        l_ref[...] = jnp.zeros_like(l_ref)

    k = k_ref[0]
    v = v_ref[0]
    block_count = q_ref.shape[0] // QUERY_BLOCK

    def body(qb, carry):
        @pl.when(present_ref[qb * G + g] > 0)
        def _():
            rows = pl.ds(pl.multiple_of(qb * QUERY_BLOCK, QUERY_BLOCK), QUERY_BLOCK)
            s = lax.dot_general(
                q_ref[rows, :], k, (((1,), (1,)), ((), ())), preferred_element_type=jnp.float32
            ) * scaling
            mask = grp_ref[rows, :] == g
            m_prev = m_ref[rows, :]
            m_cand = jnp.maximum(m_prev, jnp.max(s, axis=1, keepdims=True))
            p = jnp.exp(s - m_cand[:, :1])
            alpha = jnp.exp(m_prev - m_cand)
            l_ref[rows, :] = jnp.where(
                mask, alpha * l_ref[rows, :] + jnp.sum(p, axis=1, keepdims=True), l_ref[rows, :]
            )
            acc_ref[rows, :] = jnp.where(
                mask,
                alpha * acc_ref[rows, :]
                + jnp.dot(p.astype(jnp.bfloat16), v, preferred_element_type=jnp.float32),
                acc_ref[rows, :],
            )
            m_ref[rows, :] = jnp.where(mask, m_cand, m_prev)

        return carry

    lax.fori_loop(0, block_count, body, 0)


def attend_prefix_local(query_rows, query_group, prefix_k, prefix_v):
    row_count = query_rows.shape[0]
    span = prefix_k.shape[1]
    block_count = row_count // QUERY_BLOCK
    present = jnp.any(
        query_group.reshape(block_count, QUERY_BLOCK, 1)
        == jnp.arange(G, dtype=jnp.int32)[None, None, :],
        axis=1,
    ).astype(jnp.int32).reshape(-1)
    grp = jnp.broadcast_to(query_group[:, None], (row_count, HEAD))
    full = lambda g, kb, pr: (0, 0)
    kv_spec = pl.BlockSpec((1, KEY_BLOCK, HEAD), lambda g, kb, pr: (g, kb, 0))
    out_shape = jax.ShapeDtypeStruct((row_count, HEAD), jnp.float32)
    acc, maxima, totals = pl.pallas_call(
        prefix_kernel,
        grid_spec=pltpu.PrefetchScalarGridSpec(
            num_scalar_prefetch=1,
            grid=(G, span // KEY_BLOCK),
            in_specs=[
                pl.BlockSpec((row_count, HEAD), full),
                pl.BlockSpec((row_count, HEAD), full),
                kv_spec,
                kv_spec,
            ],
            out_specs=[pl.BlockSpec((row_count, HEAD), full)] * 3,
        ),
        out_shape=[out_shape] * 3,
        compiler_params=pltpu.CompilerParams(dimension_semantics=("arbitrary", "arbitrary")),
        cost_estimate=pl.CostEstimate(
            flops=4 * row_count * span * HEAD * 2,
            transcendentals=row_count * span * 2,
            bytes_accessed=2 * G * span * HEAD * 2 + row_count * HEAD * 14,
        ),
    )(present, query_rows, grp, prefix_k, prefix_v)
    return (acc, maxima[:, :1], totals[:, :1])


def expert_kernel(x_ref, wg_ref, wu_ref, wd_ref, o_ref, total):
    f = pl.program_id(1)

    @pl.when(f == 0)
    def _():
        total[...] = jnp.zeros_like(total)

    x_t = x_ref[0]
    gate_t = jnp.dot(wg_ref[0], x_t, preferred_element_type=jnp.float32)
    up_t = jnp.dot(wu_ref[0], x_t, preferred_element_type=jnp.float32)
    hidden = (gate_t / (1.0 + jnp.exp(-gate_t)) * up_t).T.astype(jnp.bfloat16)
    total[...] += jnp.dot(hidden, wd_ref[0], preferred_element_type=jnp.float32)

    @pl.when(f == pl.num_programs(1) - 1)
    def _():
        o_ref[0] = total[...].astype(o_ref.dtype)


FE_CHUNK = 176


def expert_ffn(rows, w_gate, w_up, w_down):
    exp_dev, row_count, width = rows.shape
    inner = w_gate.shape[2]
    chunk = FE_CHUNK if inner % FE_CHUNK == 0 else inner
    gate_t = jnp.swapaxes(w_gate, 1, 2)
    up_t = jnp.swapaxes(w_up, 1, 2)
    return pl.pallas_call(
        expert_kernel,
        grid=(exp_dev, inner // chunk),
        in_specs=[
            pl.BlockSpec((1, width, row_count), lambda e, f: (e, 0, 0)),
            pl.BlockSpec((1, chunk, width), lambda e, f: (e, f, 0)),
            pl.BlockSpec((1, chunk, width), lambda e, f: (e, f, 0)),
            pl.BlockSpec((1, chunk, width), lambda e, f: (e, f, 0)),
        ],
        out_specs=pl.BlockSpec((1, row_count, width), lambda e, f: (e, 0, 0)),
        out_shape=jax.ShapeDtypeStruct((exp_dev, row_count, width), jnp.bfloat16),
        scratch_shapes=[pltpu.VMEM((row_count, width), jnp.float32)],
        compiler_params=pltpu.CompilerParams(dimension_semantics=("arbitrary", "arbitrary")),
        cost_estimate=pl.CostEstimate(
            flops=6 * exp_dev * row_count * width * inner,
            transcendentals=exp_dev * row_count * inner,
            bytes_accessed=exp_dev * (3 * width * inner + 2 * row_count * width) * 2,
        ),
    )(jnp.swapaxes(rows, 1, 2), gate_t, up_t, w_down)


def attend_suffix(queries, keys, values, request, position):
    row_count, columns = queries.shape
    head_count = columns // HEAD
    blocks = split_blocks(row_count)
    block_len = row_count // blocks
    scaling = 1.0 / math.sqrt(HEAD)
    key_grid = keys.reshape(row_count, head_count, HEAD)
    val_grid = values.reshape(row_count, head_count, HEAD)

    def per_block(pieces):
        block_q, block_req, block_pos = pieces
        query_grid = block_q.reshape(block_len, head_count, HEAD)
        scores = (
            jnp.einsum("qhd,khd->hqk", query_grid, key_grid, preferred_element_type=jnp.float32)
            * scaling
        )
        allowed = (request[None, :] == block_req[:, None]) & (
            position[None, :] <= block_pos[:, None]
        )
        scores = jnp.where(allowed[None, :, :], scores, NEG)
        maxima = jnp.max(scores, axis=2)
        exp_terms = jnp.exp(scores - maxima[:, :, None])
        totals = jnp.sum(exp_terms, axis=2)
        weighted = jnp.einsum(
            "hqk,khd->qhd",
            exp_terms.astype(jnp.bfloat16),
            val_grid,
            preferred_element_type=jnp.float32,
        )
        return (weighted.reshape(block_len, columns), maxima.T, totals.T)

    weighted, maxima, totals = lax.map(
        per_block,
        (
            queries.reshape(blocks, block_len, columns),
            request.reshape(blocks, block_len),
            position.reshape(blocks, block_len),
        ),
    )
    return (
        weighted.reshape(row_count, columns),
        maxima.reshape(row_count, head_count),
        totals.reshape(row_count, head_count),
    )


def combine(former, latter):
    weighted_a, maxima_a, totals_a = former
    weighted_b, maxima_b, totals_b = latter
    row_count, head_count = maxima_a.shape
    maxima = jnp.maximum(maxima_a, maxima_b)
    factor_a = jnp.exp(maxima_a - maxima)
    factor_b = jnp.exp(maxima_b - maxima)
    weighted = (
        weighted_a.reshape(row_count, head_count, HEAD) * factor_a[:, :, None]
        + weighted_b.reshape(row_count, head_count, HEAD) * factor_b[:, :, None]
    )
    return (
        weighted.reshape(row_count, head_count * HEAD),
        maxima,
        totals_a * factor_a + totals_b * factor_b,
    )


def per_device(
    queries,
    keys,
    values,
    prefix_keys,
    prefix_values,
    lengths,
    groups,
    residual,
    out_proj,
    norm_gain,
    expert_ids,
    expert_gates,
    w_gate,
    w_up,
    w_down,
):
    row_tok, columns = queries.shape
    head_count = columns // HEAD
    tok_dev = residual.shape[0]
    request, position, tok_group = token_layout(lengths, groups)
    request, position, tok_group = (request[0], position[0], tok_group[0])
    req_count = lax.axis_size("req")
    local_kv = jnp.stack([prefix_keys, prefix_values])
    partner = [(i, i ^ 1) for i in range(req_count)]
    partner_kv = lax.ppermute(local_kv, "req", partner)
    ring_kv = jnp.concatenate(
        [
            lax.ppermute(local_kv, "req", [(i, (i + 2 * s) % req_count) for i in range(req_count)])
            for s in range(1, req_count // 2)
        ],
        axis=2,
    )
    forwarded_kv = lax.ppermute(ring_kv, "req", partner)
    prefix_part = None
    for chunk in (
        jnp.concatenate([local_kv, ring_kv], axis=2),
        jnp.concatenate([partner_kv, forwarded_kv], axis=2),
    ):
        part = attend_prefix_local(queries, tok_group, chunk[0], chunk[1])
        prefix_part = part if prefix_part is None else combine(prefix_part, part)
    suffix_part = attend_suffix(queries, keys, values, request, position)
    weighted, maxima, totals = combine(prefix_part, suffix_part)
    attended = (
        (weighted.reshape(row_tok, head_count, HEAD) / totals[:, :, None])
        .reshape(row_tok, columns)
        .astype(jnp.bfloat16)
    )
    exp_count = lax.axis_size("exp")
    full_proj = lax.all_gather(out_proj, "exp", axis=0, tiled=True)
    token_rows = lax.all_to_all(attended, "exp", split_axis=0, concat_axis=1, tiled=True)
    projected = jnp.dot(token_rows, full_proj, preferred_element_type=jnp.float32)
    stream = residual.astype(jnp.float32) + projected
    meansq = jnp.mean(stream * stream, axis=-1, keepdims=True)
    normed = (stream * lax.rsqrt(meansq + 1e-06) * norm_gain.astype(jnp.float32)).astype(
        jnp.bfloat16
    )
    capacity = max(2, tok_dev // 4)
    slot_count = EXPERTS * capacity
    flat_ids = expert_ids.reshape(-1)
    onehot = (flat_ids[:, None] == jnp.arange(EXPERTS, dtype=jnp.int32)[None, :]).astype(jnp.int32)
    slot_of = jnp.sum(onehot * (jnp.cumsum(onehot, axis=0) - 1), axis=1)
    dest = flat_ids * capacity + slot_of
    dest_hot = dest[:, None] == jnp.arange(slot_count, dtype=jnp.int32)[None, :]
    select = jnp.sum(dest_hot.reshape(tok_dev, TOPK, slot_count).astype(jnp.float32), axis=1)
    buffer = jnp.dot(
        select.T.astype(jnp.bfloat16), normed, preferred_element_type=jnp.float32
    ).astype(jnp.bfloat16).reshape(EXPERTS, capacity, normed.shape[1])
    exp_dev = w_gate.shape[0]
    halves = 2
    piece = capacity // halves
    returned_parts = []
    for half in range(halves):
        received = lax.all_to_all(
            buffer[:, half * piece : (half + 1) * piece], "exp", split_axis=0, concat_axis=0, tiled=True
        )
        width = received.shape[2]
        rows = jnp.swapaxes(received.reshape(exp_count, exp_dev, piece, width), 0, 1)
        expert_out = expert_ffn(rows.reshape(exp_dev, exp_count * piece, width), w_gate, w_up, w_down)
        expert_out = jnp.swapaxes(expert_out.reshape(exp_dev, exp_count, piece, width), 0, 1)
        returned_parts.append(
            lax.all_to_all(
                expert_out.reshape(EXPERTS, piece, width),
                "exp",
                split_axis=0,
                concat_axis=0,
                tiled=True,
            )
        )
    returned = jnp.concatenate(returned_parts, axis=1)
    gates = expert_gates.astype(jnp.float32).reshape(tok_dev, TOPK, 1)
    weights = jnp.sum(dest_hot.reshape(tok_dev, TOPK, slot_count).astype(jnp.float32) * gates, axis=1)
    mixture = jnp.dot(
        weights.astype(jnp.bfloat16),
        returned.reshape(slot_count, received.shape[2]),
        preferred_element_type=jnp.float32,
    )
    return (stream + mixture).astype(jnp.bfloat16)


def solution(mesh):
    in_specs = (
        P("req", "exp"),
        P("req", "exp"),
        P("req", "exp"),
        P(None, "req", "exp"),
        P(None, "req", "exp"),
        P("req", None),
        P("req", None),
        P(("req", "exp"), None),
        P("exp", None),
        P(),
        P(("req", "exp"), None),
        P(("req", "exp"), None),
        P("exp", None, None),
        P("exp", None, None),
        P("exp", None, None),
    )
    out_specs = P(("req", "exp"), None)
    return jax.shard_map(
        per_device, mesh=mesh, in_specs=in_specs, out_specs=out_specs, check_vma=False
    )
```

```python
import math

import jax
import jax.numpy as jnp
from jax import lax
from jax.experimental import pallas as pl
from jax.experimental.pallas import tpu as pltpu
from jax.sharding import PartitionSpec as P

HEAD = 128
TOPK = 4
EXPERTS = 32
G = 4
RQ = 8
ROW_TOK = 1024


NEG = -1e30


def token_layout(lengths, groups):
    req_ends = jnp.cumsum(lengths, axis=-1)
    starts = req_ends - lengths
    position = jnp.arange(ROW_TOK, dtype=jnp.int32)
    request = jnp.sum((position[None, :, None] >= req_ends[:, None, :]).astype(jnp.int32), axis=-1)
    onehot = request[:, :, None] == jnp.arange(RQ, dtype=jnp.int32)[None, None, :]
    first_tok = jnp.sum(jnp.where(onehot, starts[:, None, :], 0), axis=-1)
    tok_group = jnp.sum(jnp.where(onehot, groups[:, None, :], 0), axis=-1)
    return (request, position[None, :] - first_tok, tok_group)


def split_blocks(row_count):
    if row_count % 1024 == 0 and row_count > 1024:
        return row_count // 1024
    return 1


def pack_parts(parts):
    return jnp.concatenate([parts[0], parts[1], parts[2]], axis=1)


def unpack_parts(packed, head_count):
    columns = head_count * HEAD
    return (
        packed[:, :columns],
        packed[:, columns : columns + head_count],
        packed[:, columns + head_count :],
    )


def attend_prefix(query_rows, query_group, prefix_k, prefix_v):
    row_count, columns = query_rows.shape
    head_count = columns // HEAD
    span = prefix_k.shape[1]
    key_grid = prefix_k.reshape(G, span, head_count, HEAD)
    val_grid = prefix_v.reshape(G, span, head_count, HEAD)
    blocks = split_blocks(row_count)
    block_len = row_count // blocks
    scaling = 1.0 / math.sqrt(HEAD)

    def per_block(pieces):
        block_q, block_g = pieces
        query_grid = block_q.reshape(block_len, head_count, HEAD)
        scores = (
            jnp.einsum("qhd,gkhd->hqgk", query_grid, key_grid, preferred_element_type=jnp.float32)
            * scaling
        )
        member = block_g[:, None] == jnp.arange(G, dtype=jnp.int32)[None, :]
        scores = jnp.where(member[None, :, :, None], scores, NEG)
        maxima = jnp.max(scores, axis=(2, 3))
        exp_terms = jnp.exp(scores - maxima[:, :, None, None])
        totals = jnp.sum(exp_terms, axis=(2, 3))
        weighted = jnp.einsum(
            "hqgk,gkhd->qhd",
            exp_terms.astype(jnp.bfloat16),
            val_grid,
            preferred_element_type=jnp.float32,
        )
        return (weighted.reshape(block_len, columns), maxima.T, totals.T)

    weighted, maxima, totals = lax.map(
        per_block,
        (query_rows.reshape(blocks, block_len, columns), query_group.reshape(blocks, block_len)),
    )
    return (
        weighted.reshape(row_count, columns),
        maxima.reshape(row_count, head_count),
        totals.reshape(row_count, head_count),
    )


QUERY_BLOCK = 128
KEY_BLOCK = 2048


def prefix_kernel(present_ref, q_ref, grp_ref, k_ref, v_ref, acc_ref, m_ref, l_ref):
    g = pl.program_id(0)
    kb = pl.program_id(1)
    scaling = 1.0 / math.sqrt(HEAD)

    @pl.when((g == 0) & (kb == 0))
    def _():
        acc_ref[...] = jnp.zeros_like(acc_ref)
        m_ref[...] = jnp.full_like(m_ref, NEG)
        l_ref[...] = jnp.zeros_like(l_ref)

    k = k_ref[0]
    v = v_ref[0]
    block_count = q_ref.shape[0] // QUERY_BLOCK

    def body(qb, carry):
        @pl.when(present_ref[qb * G + g] > 0)
        def _():
            rows = pl.ds(pl.multiple_of(qb * QUERY_BLOCK, QUERY_BLOCK), QUERY_BLOCK)
            s = lax.dot_general(
                q_ref[rows, :], k, (((1,), (1,)), ((), ())), preferred_element_type=jnp.float32
            ) * scaling
            mask = grp_ref[rows, :] == g
            m_prev = m_ref[rows, :]
            m_cand = jnp.maximum(m_prev, jnp.max(s, axis=1, keepdims=True))
            p = jnp.exp(s - m_cand[:, :1])
            alpha = jnp.exp(m_prev - m_cand)
            l_ref[rows, :] = jnp.where(
                mask, alpha * l_ref[rows, :] + jnp.sum(p, axis=1, keepdims=True), l_ref[rows, :]
            )
            acc_ref[rows, :] = jnp.where(
                mask,
                alpha * acc_ref[rows, :]
                + jnp.dot(p.astype(jnp.bfloat16), v, preferred_element_type=jnp.float32),
                acc_ref[rows, :],
            )
            m_ref[rows, :] = jnp.where(mask, m_cand, m_prev)

        return carry

    lax.fori_loop(0, block_count, body, 0)


def attend_prefix_local(query_rows, query_group, prefix_k, prefix_v):
    row_count = query_rows.shape[0]
    span = prefix_k.shape[1]
    block_count = row_count // QUERY_BLOCK
    present = jnp.any(
        query_group.reshape(block_count, QUERY_BLOCK, 1)
        == jnp.arange(G, dtype=jnp.int32)[None, None, :],
        axis=1,
    ).astype(jnp.int32).reshape(-1)
    grp = jnp.broadcast_to(query_group[:, None], (row_count, HEAD))
    full = lambda g, kb, pr: (0, 0)
    kv_spec = pl.BlockSpec((1, KEY_BLOCK, HEAD), lambda g, kb, pr: (g, kb, 0))
    out_shape = jax.ShapeDtypeStruct((row_count, HEAD), jnp.float32)
    acc, maxima, totals = pl.pallas_call(
        prefix_kernel,
        grid_spec=pltpu.PrefetchScalarGridSpec(
            num_scalar_prefetch=1,
            grid=(G, span // KEY_BLOCK),
            in_specs=[
                pl.BlockSpec((row_count, HEAD), full),
                pl.BlockSpec((row_count, HEAD), full),
                kv_spec,
                kv_spec,
            ],
            out_specs=[pl.BlockSpec((row_count, HEAD), full)] * 3,
        ),
        out_shape=[out_shape] * 3,
        compiler_params=pltpu.CompilerParams(dimension_semantics=("arbitrary", "arbitrary")),
        cost_estimate=pl.CostEstimate(
            flops=4 * row_count * span * HEAD * 2,
            transcendentals=row_count * span * 2,
            bytes_accessed=2 * G * span * HEAD * 2 + row_count * HEAD * 14,
        ),
    )(present, query_rows, grp, prefix_k, prefix_v)
    return (acc, maxima[:, :1], totals[:, :1])


def expert_kernel(x_ref, wg_ref, wu_ref, wd_ref, o_ref, total):
    f = pl.program_id(1)

    @pl.when(f == 0)
    def _():
        total[...] = jnp.zeros_like(total)

    x_t = x_ref[0]
    gate_t = jnp.dot(wg_ref[0], x_t, preferred_element_type=jnp.float32)
    up_t = jnp.dot(wu_ref[0], x_t, preferred_element_type=jnp.float32)
    hidden = (gate_t / (1.0 + jnp.exp(-gate_t)) * up_t).T.astype(jnp.bfloat16)
    total[...] += jnp.dot(hidden, wd_ref[0], preferred_element_type=jnp.float32)

    @pl.when(f == pl.num_programs(1) - 1)
    def _():
        o_ref[0] = total[...].astype(o_ref.dtype)


FE_CHUNK = 176


def expert_ffn(rows, w_gate, w_up, w_down):
    exp_dev, row_count, width = rows.shape
    inner = w_gate.shape[2]
    chunk = FE_CHUNK if inner % FE_CHUNK == 0 else inner
    gate_t = jnp.swapaxes(w_gate, 1, 2)
    up_t = jnp.swapaxes(w_up, 1, 2)
    return pl.pallas_call(
        expert_kernel,
        grid=(exp_dev, inner // chunk),
        in_specs=[
            pl.BlockSpec((1, width, row_count), lambda e, f: (e, 0, 0)),
            pl.BlockSpec((1, chunk, width), lambda e, f: (e, f, 0)),
            pl.BlockSpec((1, chunk, width), lambda e, f: (e, f, 0)),
            pl.BlockSpec((1, chunk, width), lambda e, f: (e, f, 0)),
        ],
        out_specs=pl.BlockSpec((1, row_count, width), lambda e, f: (e, 0, 0)),
        out_shape=jax.ShapeDtypeStruct((exp_dev, row_count, width), jnp.bfloat16),
        scratch_shapes=[pltpu.VMEM((row_count, width), jnp.float32)],
        compiler_params=pltpu.CompilerParams(dimension_semantics=("arbitrary", "arbitrary")),
        cost_estimate=pl.CostEstimate(
            flops=6 * exp_dev * row_count * width * inner,
            transcendentals=exp_dev * row_count * inner,
            bytes_accessed=exp_dev * (3 * width * inner + 2 * row_count * width) * 2,
        ),
    )(jnp.swapaxes(rows, 1, 2), gate_t, up_t, w_down)


def attend_suffix(queries, keys, values, request, position):
    row_count, columns = queries.shape
    head_count = columns // HEAD
    blocks = split_blocks(row_count)
    block_len = row_count // blocks
    scaling = 1.0 / math.sqrt(HEAD)
    key_grid = keys.reshape(row_count, head_count, HEAD)
    val_grid = values.reshape(row_count, head_count, HEAD)

    def per_block(pieces):
        block_q, block_req, block_pos = pieces
        query_grid = block_q.reshape(block_len, head_count, HEAD)
        scores = (
            jnp.einsum("qhd,khd->hqk", query_grid, key_grid, preferred_element_type=jnp.float32)
            * scaling
        )
        allowed = (request[None, :] == block_req[:, None]) & (
            position[None, :] <= block_pos[:, None]
        )
        scores = jnp.where(allowed[None, :, :], scores, NEG)
        maxima = jnp.max(scores, axis=2)
        exp_terms = jnp.exp(scores - maxima[:, :, None])
        totals = jnp.sum(exp_terms, axis=2)
        weighted = jnp.einsum(
            "hqk,khd->qhd",
            exp_terms.astype(jnp.bfloat16),
            val_grid,
            preferred_element_type=jnp.float32,
        )
        return (weighted.reshape(block_len, columns), maxima.T, totals.T)

    weighted, maxima, totals = lax.map(
        per_block,
        (
            queries.reshape(blocks, block_len, columns),
            request.reshape(blocks, block_len),
            position.reshape(blocks, block_len),
        ),
    )
    return (
        weighted.reshape(row_count, columns),
        maxima.reshape(row_count, head_count),
        totals.reshape(row_count, head_count),
    )


def combine(former, latter):
    weighted_a, maxima_a, totals_a = former
    weighted_b, maxima_b, totals_b = latter
    row_count, head_count = maxima_a.shape
    maxima = jnp.maximum(maxima_a, maxima_b)
    factor_a = jnp.exp(maxima_a - maxima)
    factor_b = jnp.exp(maxima_b - maxima)
    weighted = (
        weighted_a.reshape(row_count, head_count, HEAD) * factor_a[:, :, None]
        + weighted_b.reshape(row_count, head_count, HEAD) * factor_b[:, :, None]
    )
    return (
        weighted.reshape(row_count, head_count * HEAD),
        maxima,
        totals_a * factor_a + totals_b * factor_b,
    )


def per_device(
    queries,
    keys,
    values,
    prefix_keys,
    prefix_values,
    lengths,
    groups,
    residual,
    out_proj,
    norm_gain,
    expert_ids,
    expert_gates,
    w_gate,
    w_up,
    w_down,
):
    row_tok, columns = queries.shape
    head_count = columns // HEAD
    tok_dev = residual.shape[0]
    request, position, tok_group = token_layout(lengths, groups)
    request, position, tok_group = (request[0], position[0], tok_group[0])
    req_count = lax.axis_size("req")
    local_kv = jnp.stack([prefix_keys, prefix_values])
    partner = [(i, i ^ 1) for i in range(req_count)]
    partner_kv = lax.ppermute(local_kv, "req", partner)
    ring_kv = jnp.concatenate(
        [
            lax.ppermute(local_kv, "req", [(i, (i + 2 * s) % req_count) for i in range(req_count)])
            for s in range(1, req_count // 2)
        ],
        axis=2,
    )
    forwarded_kv = lax.ppermute(ring_kv, "req", partner)
    prefix_part = None
    for chunk in (
        jnp.concatenate([local_kv, ring_kv], axis=2),
        jnp.concatenate([partner_kv, forwarded_kv], axis=2),
    ):
        part = attend_prefix_local(queries, tok_group, chunk[0], chunk[1])
        prefix_part = part if prefix_part is None else combine(prefix_part, part)
    suffix_part = attend_suffix(queries, keys, values, request, position)
    weighted, maxima, totals = combine(prefix_part, suffix_part)
    attended = (
        (weighted.reshape(row_tok, head_count, HEAD) / totals[:, :, None])
        .reshape(row_tok, columns)
        .astype(jnp.bfloat16)
    )
    exp_count = lax.axis_size("exp")
    full_proj = lax.all_gather(out_proj, "exp", axis=0, tiled=True)
    token_rows = lax.all_to_all(attended, "exp", split_axis=0, concat_axis=1, tiled=True)
    projected = jnp.dot(token_rows, full_proj, preferred_element_type=jnp.float32)
    stream = residual.astype(jnp.float32) + projected
    meansq = jnp.mean(stream * stream, axis=-1, keepdims=True)
    normed = (stream * lax.rsqrt(meansq + 1e-06) * norm_gain.astype(jnp.float32)).astype(
        jnp.bfloat16
    )
    capacity = max(2, tok_dev // 4)
    slot_count = EXPERTS * capacity
    flat_ids = expert_ids.reshape(-1)
    onehot = (flat_ids[:, None] == jnp.arange(EXPERTS, dtype=jnp.int32)[None, :]).astype(jnp.int32)
    slot_of = jnp.sum(onehot * (jnp.cumsum(onehot, axis=0) - 1), axis=1)
    dest = flat_ids * capacity + slot_of
    dest_hot = dest[:, None] == jnp.arange(slot_count, dtype=jnp.int32)[None, :]
    select = jnp.sum(dest_hot.reshape(tok_dev, TOPK, slot_count).astype(jnp.float32), axis=1)
    buffer = jnp.dot(
        select.T.astype(jnp.bfloat16), normed, preferred_element_type=jnp.float32
    ).astype(jnp.bfloat16).reshape(EXPERTS, capacity, normed.shape[1])
    exp_dev = w_gate.shape[0]
    received = lax.all_to_all(buffer, "exp", split_axis=0, concat_axis=0, tiled=True)
    slots = received.shape[1]
    width = received.shape[2]
    rows = jnp.swapaxes(received.reshape(exp_count, exp_dev, slots, width), 0, 1)
    expert_out = expert_ffn(rows.reshape(exp_dev, exp_count * slots, width), w_gate, w_up, w_down)
    expert_out = jnp.swapaxes(expert_out.reshape(exp_dev, exp_count, slots, width), 0, 1)
    returned = lax.all_to_all(
        expert_out.reshape(EXPERTS, slots, width),
        "exp",
        split_axis=0,
        concat_axis=0,
        tiled=True,
    )
    gates = expert_gates.astype(jnp.float32).reshape(tok_dev, TOPK, 1)
    weights = jnp.sum(dest_hot.reshape(tok_dev, TOPK, slot_count).astype(jnp.float32) * gates, axis=1)
    mixture = jnp.dot(
        weights.astype(jnp.bfloat16),
        returned.reshape(slot_count, received.shape[2]),
        preferred_element_type=jnp.float32,
    )
    return (stream + mixture).astype(jnp.bfloat16)


def solution(mesh):
    in_specs = (
        P("req", "exp"),
        P("req", "exp"),
        P("req", "exp"),
        P(None, "req", "exp"),
        P(None, "req", "exp"),
        P("req", None),
        P("req", None),
        P(("req", "exp"), None),
        P("exp", None),
        P(),
        P(("req", "exp"), None),
        P(("req", "exp"), None),
        P("exp", None, None),
        P("exp", None, None),
        P("exp", None, None),
    )
    out_specs = P(("req", "exp"), None)
    return jax.shard_map(
        per_device, mesh=mesh, in_specs=in_specs, out_specs=out_specs, check_vma=False
    )
```

```python
import math

import jax
import jax.numpy as jnp
from jax import lax
from jax.experimental import pallas as pl
from jax.experimental.pallas import tpu as pltpu
from jax.sharding import PartitionSpec as P

HEAD = 128
TOPK = 4
EXPERTS = 32
G = 4
RQ = 8
ROW_TOK = 1024


NEG = -1e30


def token_layout(lengths, groups):
    req_ends = jnp.cumsum(lengths, axis=-1)
    starts = req_ends - lengths
    position = jnp.arange(ROW_TOK, dtype=jnp.int32)
    request = jnp.sum((position[None, :, None] >= req_ends[:, None, :]).astype(jnp.int32), axis=-1)
    onehot = request[:, :, None] == jnp.arange(RQ, dtype=jnp.int32)[None, None, :]
    first_tok = jnp.sum(jnp.where(onehot, starts[:, None, :], 0), axis=-1)
    tok_group = jnp.sum(jnp.where(onehot, groups[:, None, :], 0), axis=-1)
    return (request, position[None, :] - first_tok, tok_group)


def split_blocks(row_count):
    if row_count % 1024 == 0 and row_count > 1024:
        return row_count // 1024
    return 1


def pack_parts(parts):
    return jnp.concatenate([parts[0], parts[1], parts[2]], axis=1)


def unpack_parts(packed, head_count):
    columns = head_count * HEAD
    return (
        packed[:, :columns],
        packed[:, columns : columns + head_count],
        packed[:, columns + head_count :],
    )


def attend_prefix(query_rows, query_group, prefix_k, prefix_v):
    row_count, columns = query_rows.shape
    head_count = columns // HEAD
    span = prefix_k.shape[1]
    key_grid = prefix_k.reshape(G, span, head_count, HEAD)
    val_grid = prefix_v.reshape(G, span, head_count, HEAD)
    blocks = split_blocks(row_count)
    block_len = row_count // blocks
    scaling = 1.0 / math.sqrt(HEAD)

    def per_block(pieces):
        block_q, block_g = pieces
        query_grid = block_q.reshape(block_len, head_count, HEAD)
        scores = (
            jnp.einsum("qhd,gkhd->hqgk", query_grid, key_grid, preferred_element_type=jnp.float32)
            * scaling
        )
        member = block_g[:, None] == jnp.arange(G, dtype=jnp.int32)[None, :]
        scores = jnp.where(member[None, :, :, None], scores, NEG)
        maxima = jnp.max(scores, axis=(2, 3))
        exp_terms = jnp.exp(scores - maxima[:, :, None, None])
        totals = jnp.sum(exp_terms, axis=(2, 3))
        weighted = jnp.einsum(
            "hqgk,gkhd->qhd",
            exp_terms.astype(jnp.bfloat16),
            val_grid,
            preferred_element_type=jnp.float32,
        )
        return (weighted.reshape(block_len, columns), maxima.T, totals.T)

    weighted, maxima, totals = lax.map(
        per_block,
        (query_rows.reshape(blocks, block_len, columns), query_group.reshape(blocks, block_len)),
    )
    return (
        weighted.reshape(row_count, columns),
        maxima.reshape(row_count, head_count),
        totals.reshape(row_count, head_count),
    )


QUERY_BLOCK = 128
KEY_BLOCK = 2048


def prefix_kernel(block_group_ref, q_ref, k_ref, v_ref, acc_ref, m_ref, l_ref):
    scaling = 1.0 / math.sqrt(HEAD)
    s = lax.dot_general(
        q_ref[...], k_ref[0], (((1,), (1,)), ((), ())), preferred_element_type=jnp.float32
    ) * scaling
    m = jnp.max(s, axis=1, keepdims=True)
    p = jnp.exp(s - m)
    acc_ref[...] = jnp.dot(p.astype(jnp.bfloat16), v_ref[0], preferred_element_type=jnp.float32)
    m_ref[...] = jnp.broadcast_to(m, m_ref.shape)
    l_ref[...] = jnp.broadcast_to(jnp.sum(p, axis=1, keepdims=True), l_ref.shape)


def group_layout(query_group):
    row_count = query_group.shape[0]
    block_count = row_count // QUERY_BLOCK + G - 1
    member = query_group[:, None] == jnp.arange(G, dtype=jnp.int32)[None, :]
    counts = jnp.sum(member.astype(jnp.int32), axis=0)
    blocks = (counts + QUERY_BLOCK - 1) // QUERY_BLOCK
    first_block = jnp.cumsum(blocks) - blocks
    rank = jnp.sum(jnp.where(member, jnp.cumsum(member.astype(jnp.int32), axis=0) - 1, 0), axis=1)
    padded_index = jnp.sum(jnp.where(member, first_block[None, :], 0), axis=1) * QUERY_BLOCK + rank
    source = jnp.zeros((block_count * QUERY_BLOCK,), jnp.int32).at[padded_index].set(
        jnp.arange(row_count, dtype=jnp.int32)
    )
    block_group = jnp.sum(
        (jnp.arange(block_count, dtype=jnp.int32)[:, None] >= first_block[None, 1:]).astype(jnp.int32),
        axis=1,
    )
    return padded_index, source, block_group


def attend_prefix_grouped(padded_rows, block_group, prefix_k, prefix_v):
    padded_count = padded_rows.shape[0]
    span = prefix_k.shape[1]
    block_count = padded_count // QUERY_BLOCK
    row_spec = pl.BlockSpec((QUERY_BLOCK, HEAD), lambda b, bg: (b, 0))
    kv_spec = pl.BlockSpec((1, span, HEAD), lambda b, bg: (bg[b], 0, 0))
    out_shape = jax.ShapeDtypeStruct((padded_count, HEAD), jnp.float32)
    acc, maxima, totals = pl.pallas_call(
        prefix_kernel,
        grid_spec=pltpu.PrefetchScalarGridSpec(
            num_scalar_prefetch=1,
            grid=(block_count,),
            in_specs=[row_spec, kv_spec, kv_spec],
            out_specs=[row_spec] * 3,
        ),
        out_shape=[out_shape] * 3,
        compiler_params=pltpu.CompilerParams(dimension_semantics=("arbitrary",)),
        cost_estimate=pl.CostEstimate(
            flops=4 * padded_count * span * HEAD,
            transcendentals=padded_count * span,
            bytes_accessed=2 * G * span * HEAD * 2 + padded_count * HEAD * 14,
        ),
    )(block_group, padded_rows, prefix_k, prefix_v)
    return (acc, maxima[:, :1], totals[:, :1])


def expert_kernel(x_ref, wg_ref, wu_ref, wd_ref, o_ref, total):
    f = pl.program_id(1)

    @pl.when(f == 0)
    def _():
        total[...] = jnp.zeros_like(total)

    x_t = x_ref[0]
    gate_t = jnp.dot(wg_ref[0], x_t, preferred_element_type=jnp.float32)
    up_t = jnp.dot(wu_ref[0], x_t, preferred_element_type=jnp.float32)
    hidden = (gate_t / (1.0 + jnp.exp(-gate_t)) * up_t).T.astype(jnp.bfloat16)
    total[...] += jnp.dot(hidden, wd_ref[0], preferred_element_type=jnp.float32)

    @pl.when(f == pl.num_programs(1) - 1)
    def _():
        o_ref[0] = total[...].astype(o_ref.dtype)


FE_CHUNK = 176


def expert_ffn(rows, w_gate, w_up, w_down):
    exp_dev, row_count, width = rows.shape
    inner = w_gate.shape[2]
    chunk = FE_CHUNK if inner % FE_CHUNK == 0 else inner
    gate_t = jnp.swapaxes(w_gate, 1, 2)
    up_t = jnp.swapaxes(w_up, 1, 2)
    return pl.pallas_call(
        expert_kernel,
        grid=(exp_dev, inner // chunk),
        in_specs=[
            pl.BlockSpec((1, width, row_count), lambda e, f: (e, 0, 0)),
            pl.BlockSpec((1, chunk, width), lambda e, f: (e, f, 0)),
            pl.BlockSpec((1, chunk, width), lambda e, f: (e, f, 0)),
            pl.BlockSpec((1, chunk, width), lambda e, f: (e, f, 0)),
        ],
        out_specs=pl.BlockSpec((1, row_count, width), lambda e, f: (e, 0, 0)),
        out_shape=jax.ShapeDtypeStruct((exp_dev, row_count, width), jnp.bfloat16),
        scratch_shapes=[pltpu.VMEM((row_count, width), jnp.float32)],
        compiler_params=pltpu.CompilerParams(dimension_semantics=("arbitrary", "arbitrary")),
        cost_estimate=pl.CostEstimate(
            flops=6 * exp_dev * row_count * width * inner,
            transcendentals=exp_dev * row_count * inner,
            bytes_accessed=exp_dev * (3 * width * inner + 2 * row_count * width) * 2,
        ),
    )(jnp.swapaxes(rows, 1, 2), gate_t, up_t, w_down)


def attend_suffix(queries, keys, values, request, position):
    row_count, columns = queries.shape
    head_count = columns // HEAD
    blocks = split_blocks(row_count)
    block_len = row_count // blocks
    scaling = 1.0 / math.sqrt(HEAD)
    key_grid = keys.reshape(row_count, head_count, HEAD)
    val_grid = values.reshape(row_count, head_count, HEAD)

    def per_block(pieces):
        block_q, block_req, block_pos = pieces
        query_grid = block_q.reshape(block_len, head_count, HEAD)
        scores = (
            jnp.einsum("qhd,khd->hqk", query_grid, key_grid, preferred_element_type=jnp.float32)
            * scaling
        )
        allowed = (request[None, :] == block_req[:, None]) & (
            position[None, :] <= block_pos[:, None]
        )
        scores = jnp.where(allowed[None, :, :], scores, NEG)
        maxima = jnp.max(scores, axis=2)
        exp_terms = jnp.exp(scores - maxima[:, :, None])
        totals = jnp.sum(exp_terms, axis=2)
        weighted = jnp.einsum(
            "hqk,khd->qhd",
            exp_terms.astype(jnp.bfloat16),
            val_grid,
            preferred_element_type=jnp.float32,
        )
        return (weighted.reshape(block_len, columns), maxima.T, totals.T)

    weighted, maxima, totals = lax.map(
        per_block,
        (
            queries.reshape(blocks, block_len, columns),
            request.reshape(blocks, block_len),
            position.reshape(blocks, block_len),
        ),
    )
    return (
        weighted.reshape(row_count, columns),
        maxima.reshape(row_count, head_count),
        totals.reshape(row_count, head_count),
    )


def combine(former, latter):
    weighted_a, maxima_a, totals_a = former
    weighted_b, maxima_b, totals_b = latter
    row_count, head_count = maxima_a.shape
    maxima = jnp.maximum(maxima_a, maxima_b)
    factor_a = jnp.exp(maxima_a - maxima)
    factor_b = jnp.exp(maxima_b - maxima)
    weighted = (
        weighted_a.reshape(row_count, head_count, HEAD) * factor_a[:, :, None]
        + weighted_b.reshape(row_count, head_count, HEAD) * factor_b[:, :, None]
    )
    return (
        weighted.reshape(row_count, head_count * HEAD),
        maxima,
        totals_a * factor_a + totals_b * factor_b,
    )


def per_device(
    queries,
    keys,
    values,
    prefix_keys,
    prefix_values,
    lengths,
    groups,
    residual,
    out_proj,
    norm_gain,
    expert_ids,
    expert_gates,
    w_gate,
    w_up,
    w_down,
):
    row_tok, columns = queries.shape
    head_count = columns // HEAD
    tok_dev = residual.shape[0]
    request, position, tok_group = token_layout(lengths, groups)
    request, position, tok_group = (request[0], position[0], tok_group[0])
    req_count = lax.axis_size("req")
    local_kv = jnp.stack([prefix_keys, prefix_values])
    partner = [(i, i ^ 1) for i in range(req_count)]
    partner_kv = lax.ppermute(local_kv, "req", partner)
    ring_kv = jnp.concatenate(
        [
            lax.ppermute(local_kv, "req", [(i, (i + 2 * s) % req_count) for i in range(req_count)])
            for s in range(1, req_count // 2)
        ],
        axis=2,
    )
    forwarded_kv = lax.ppermute(ring_kv, "req", partner)
    padded_index, source, block_group = group_layout(tok_group)
    padded_rows = jnp.take(queries, source, axis=0)
    prefix_part = None
    for chunk in (
        jnp.concatenate([local_kv, ring_kv], axis=2),
        jnp.concatenate([partner_kv, forwarded_kv], axis=2),
    ):
        part = attend_prefix_grouped(padded_rows, block_group, chunk[0], chunk[1])
        prefix_part = part if prefix_part is None else combine(prefix_part, part)
    prefix_part = tuple(jnp.take(piece, padded_index, axis=0) for piece in prefix_part)
    suffix_part = attend_suffix(queries, keys, values, request, position)
    weighted, maxima, totals = combine(prefix_part, suffix_part)
    attended = (
        (weighted.reshape(row_tok, head_count, HEAD) / totals[:, :, None])
        .reshape(row_tok, columns)
        .astype(jnp.bfloat16)
    )
    exp_count = lax.axis_size("exp")
    full_proj = lax.all_gather(out_proj, "exp", axis=0, tiled=True)
    token_rows = lax.all_to_all(attended, "exp", split_axis=0, concat_axis=1, tiled=True)
    projected = jnp.dot(token_rows, full_proj, preferred_element_type=jnp.float32)
    stream = residual.astype(jnp.float32) + projected
    meansq = jnp.mean(stream * stream, axis=-1, keepdims=True)
    normed = (stream * lax.rsqrt(meansq + 1e-06) * norm_gain.astype(jnp.float32)).astype(
        jnp.bfloat16
    )
    capacity = max(2, tok_dev // 4)
    slot_count = EXPERTS * capacity
    flat_ids = expert_ids.reshape(-1)
    onehot = (flat_ids[:, None] == jnp.arange(EXPERTS, dtype=jnp.int32)[None, :]).astype(jnp.int32)
    slot_of = jnp.sum(onehot * (jnp.cumsum(onehot, axis=0) - 1), axis=1)
    dest = flat_ids * capacity + slot_of
    dest_hot = dest[:, None] == jnp.arange(slot_count, dtype=jnp.int32)[None, :]
    select = jnp.sum(dest_hot.reshape(tok_dev, TOPK, slot_count).astype(jnp.float32), axis=1)
    buffer = jnp.dot(
        select.T.astype(jnp.bfloat16), normed, preferred_element_type=jnp.float32
    ).astype(jnp.bfloat16).reshape(EXPERTS, capacity, normed.shape[1])
    exp_dev = w_gate.shape[0]
    received = lax.all_to_all(buffer, "exp", split_axis=0, concat_axis=0, tiled=True)
    slots = received.shape[1]
    width = received.shape[2]
    rows = jnp.swapaxes(received.reshape(exp_count, exp_dev, slots, width), 0, 1)
    expert_out = expert_ffn(rows.reshape(exp_dev, exp_count * slots, width), w_gate, w_up, w_down)
    expert_out = jnp.swapaxes(expert_out.reshape(exp_dev, exp_count, slots, width), 0, 1)
    returned = lax.all_to_all(
        expert_out.reshape(EXPERTS, slots, width),
        "exp",
        split_axis=0,
        concat_axis=0,
        tiled=True,
    )
    gates = expert_gates.astype(jnp.float32).reshape(tok_dev, TOPK, 1)
    weights = jnp.sum(dest_hot.reshape(tok_dev, TOPK, slot_count).astype(jnp.float32) * gates, axis=1)
    mixture = jnp.dot(
        weights.astype(jnp.bfloat16),
        returned.reshape(slot_count, received.shape[2]),
        preferred_element_type=jnp.float32,
    )
    return (stream + mixture).astype(jnp.bfloat16)


def solution(mesh):
    in_specs = (
        P("req", "exp"),
        P("req", "exp"),
        P("req", "exp"),
        P(None, "req", "exp"),
        P(None, "req", "exp"),
        P("req", None),
        P("req", None),
        P(("req", "exp"), None),
        P("exp", None),
        P(),
        P(("req", "exp"), None),
        P(("req", "exp"), None),
        P("exp", None, None),
        P("exp", None, None),
        P("exp", None, None),
    )
    out_specs = P(("req", "exp"), None)
    return jax.shard_map(
        per_device, mesh=mesh, in_specs=in_specs, out_specs=out_specs, check_vma=False
    )
```

```python
import math

import jax
import jax.numpy as jnp
from jax import lax
from jax.experimental import pallas as pl
from jax.experimental.pallas import tpu as pltpu
from jax.sharding import PartitionSpec as P

HEAD = 128
TOPK = 4
EXPERTS = 32
G = 4
RQ = 8
ROW_TOK = 1024


NEG = -1e30


def token_layout(lengths, groups):
    req_ends = jnp.cumsum(lengths, axis=-1)
    starts = req_ends - lengths
    position = jnp.arange(ROW_TOK, dtype=jnp.int32)
    request = jnp.sum((position[None, :, None] >= req_ends[:, None, :]).astype(jnp.int32), axis=-1)
    onehot = request[:, :, None] == jnp.arange(RQ, dtype=jnp.int32)[None, None, :]
    first_tok = jnp.sum(jnp.where(onehot, starts[:, None, :], 0), axis=-1)
    tok_group = jnp.sum(jnp.where(onehot, groups[:, None, :], 0), axis=-1)
    return (request, position[None, :] - first_tok, tok_group)


def split_blocks(row_count):
    if row_count % 1024 == 0 and row_count > 1024:
        return row_count // 1024
    return 1


def pack_parts(parts):
    return jnp.concatenate([parts[0], parts[1], parts[2]], axis=1)


def unpack_parts(packed, head_count):
    columns = head_count * HEAD
    return (
        packed[:, :columns],
        packed[:, columns : columns + head_count],
        packed[:, columns + head_count :],
    )


def attend_prefix(query_rows, query_group, prefix_k, prefix_v):
    row_count, columns = query_rows.shape
    head_count = columns // HEAD
    span = prefix_k.shape[1]
    key_grid = prefix_k.reshape(G, span, head_count, HEAD)
    val_grid = prefix_v.reshape(G, span, head_count, HEAD)
    blocks = split_blocks(row_count)
    block_len = row_count // blocks
    scaling = 1.0 / math.sqrt(HEAD)

    def per_block(pieces):
        block_q, block_g = pieces
        query_grid = block_q.reshape(block_len, head_count, HEAD)
        scores = (
            jnp.einsum("qhd,gkhd->hqgk", query_grid, key_grid, preferred_element_type=jnp.float32)
            * scaling
        )
        member = block_g[:, None] == jnp.arange(G, dtype=jnp.int32)[None, :]
        scores = jnp.where(member[None, :, :, None], scores, NEG)
        maxima = jnp.max(scores, axis=(2, 3))
        exp_terms = jnp.exp(scores - maxima[:, :, None, None])
        totals = jnp.sum(exp_terms, axis=(2, 3))
        weighted = jnp.einsum(
            "hqgk,gkhd->qhd",
            exp_terms.astype(jnp.bfloat16),
            val_grid,
            preferred_element_type=jnp.float32,
        )
        return (weighted.reshape(block_len, columns), maxima.T, totals.T)

    weighted, maxima, totals = lax.map(
        per_block,
        (query_rows.reshape(blocks, block_len, columns), query_group.reshape(blocks, block_len)),
    )
    return (
        weighted.reshape(row_count, columns),
        maxima.reshape(row_count, head_count),
        totals.reshape(row_count, head_count),
    )


QUERY_BLOCK = 128
KEY_BLOCK = 2048


def prefix_kernel(block_group_ref, q_ref, k_ref, v_ref, acc_ref, m_ref, l_ref):
    scaling = 1.0 / math.sqrt(HEAD)
    s = lax.dot_general(
        q_ref[...], k_ref[0], (((1,), (1,)), ((), ())), preferred_element_type=jnp.float32
    ) * scaling
    m = jnp.max(s, axis=1, keepdims=True)
    p = jnp.exp(s - m)
    acc_ref[...] = jnp.dot(p.astype(jnp.bfloat16), v_ref[0], preferred_element_type=jnp.float32)
    m_ref[...] = jnp.broadcast_to(m, m_ref.shape)
    l_ref[...] = jnp.broadcast_to(jnp.sum(p, axis=1, keepdims=True), l_ref.shape)


def group_layout(query_group):
    row_count = query_group.shape[0]
    block_count = row_count // QUERY_BLOCK + G - 1
    member = query_group[:, None] == jnp.arange(G, dtype=jnp.int32)[None, :]
    counts = jnp.sum(member.astype(jnp.int32), axis=0)
    blocks = (counts + QUERY_BLOCK - 1) // QUERY_BLOCK
    first_block = jnp.cumsum(blocks) - blocks
    rank = jnp.sum(jnp.where(member, jnp.cumsum(member.astype(jnp.int32), axis=0) - 1, 0), axis=1)
    padded_index = jnp.sum(jnp.where(member, first_block[None, :], 0), axis=1) * QUERY_BLOCK + rank
    source = jnp.zeros((block_count * QUERY_BLOCK,), jnp.int32).at[padded_index].set(
        jnp.arange(row_count, dtype=jnp.int32)
    )
    block_group = jnp.sum(
        (jnp.arange(block_count, dtype=jnp.int32)[:, None] >= first_block[None, 1:]).astype(jnp.int32),
        axis=1,
    )
    return padded_index, source, block_group


def attend_prefix_grouped(padded_rows, block_group, prefix_k, prefix_v):
    padded_count = padded_rows.shape[0]
    span = prefix_k.shape[1]
    block_count = padded_count // QUERY_BLOCK
    row_spec = pl.BlockSpec((QUERY_BLOCK, HEAD), lambda b, bg: (b, 0))
    kv_spec = pl.BlockSpec((1, span, HEAD), lambda b, bg: (bg[b], 0, 0))
    out_shape = jax.ShapeDtypeStruct((padded_count, HEAD), jnp.float32)
    acc, maxima, totals = pl.pallas_call(
        prefix_kernel,
        grid_spec=pltpu.PrefetchScalarGridSpec(
            num_scalar_prefetch=1,
            grid=(block_count,),
            in_specs=[row_spec, kv_spec, kv_spec],
            out_specs=[row_spec] * 3,
        ),
        out_shape=[out_shape] * 3,
        compiler_params=pltpu.CompilerParams(dimension_semantics=("arbitrary",)),
        cost_estimate=pl.CostEstimate(
            flops=4 * padded_count * span * HEAD,
            transcendentals=padded_count * span,
            bytes_accessed=2 * G * span * HEAD * 2 + padded_count * HEAD * 14,
        ),
    )(block_group, padded_rows, prefix_k, prefix_v)
    return (acc, maxima[:, :1], totals[:, :1])


def expert_kernel(x_ref, wg_ref, wu_ref, wd_ref, o_ref, total):
    f = pl.program_id(1)

    @pl.when(f == 0)
    def _():
        total[...] = jnp.zeros_like(total)

    x_t = x_ref[0]
    gate_t = jnp.dot(wg_ref[0], x_t, preferred_element_type=jnp.float32)
    up_t = jnp.dot(wu_ref[0], x_t, preferred_element_type=jnp.float32)
    hidden = (gate_t / (1.0 + jnp.exp(-gate_t)) * up_t).T.astype(jnp.bfloat16)
    total[...] += jnp.dot(hidden, wd_ref[0], preferred_element_type=jnp.float32)

    @pl.when(f == pl.num_programs(1) - 1)
    def _():
        o_ref[0] = total[...].astype(o_ref.dtype)


FE_CHUNK = 176


def expert_ffn(rows, w_gate, w_up, w_down):
    exp_dev, row_count, width = rows.shape
    inner = w_gate.shape[2]
    chunk = FE_CHUNK if inner % FE_CHUNK == 0 else inner
    gate_t = jnp.swapaxes(w_gate, 1, 2)
    up_t = jnp.swapaxes(w_up, 1, 2)
    return pl.pallas_call(
        expert_kernel,
        grid=(exp_dev, inner // chunk),
        in_specs=[
            pl.BlockSpec((1, width, row_count), lambda e, f: (e, 0, 0)),
            pl.BlockSpec((1, chunk, width), lambda e, f: (e, f, 0)),
            pl.BlockSpec((1, chunk, width), lambda e, f: (e, f, 0)),
            pl.BlockSpec((1, chunk, width), lambda e, f: (e, f, 0)),
        ],
        out_specs=pl.BlockSpec((1, row_count, width), lambda e, f: (e, 0, 0)),
        out_shape=jax.ShapeDtypeStruct((exp_dev, row_count, width), jnp.bfloat16),
        scratch_shapes=[pltpu.VMEM((row_count, width), jnp.float32)],
        compiler_params=pltpu.CompilerParams(dimension_semantics=("arbitrary", "arbitrary")),
        cost_estimate=pl.CostEstimate(
            flops=6 * exp_dev * row_count * width * inner,
            transcendentals=exp_dev * row_count * inner,
            bytes_accessed=exp_dev * (3 * width * inner + 2 * row_count * width) * 2,
        ),
    )(jnp.swapaxes(rows, 1, 2), gate_t, up_t, w_down)


def attend_suffix(queries, keys, values, request, position):
    row_count, columns = queries.shape
    head_count = columns // HEAD
    blocks = split_blocks(row_count)
    block_len = row_count // blocks
    scaling = 1.0 / math.sqrt(HEAD)
    key_grid = keys.reshape(row_count, head_count, HEAD)
    val_grid = values.reshape(row_count, head_count, HEAD)

    def per_block(pieces):
        block_q, block_req, block_pos = pieces
        query_grid = block_q.reshape(block_len, head_count, HEAD)
        scores = (
            jnp.einsum("qhd,khd->hqk", query_grid, key_grid, preferred_element_type=jnp.float32)
            * scaling
        )
        allowed = (request[None, :] == block_req[:, None]) & (
            position[None, :] <= block_pos[:, None]
        )
        scores = jnp.where(allowed[None, :, :], scores, NEG)
        maxima = jnp.max(scores, axis=2)
        exp_terms = jnp.exp(scores - maxima[:, :, None])
        totals = jnp.sum(exp_terms, axis=2)
        weighted = jnp.einsum(
            "hqk,khd->qhd",
            exp_terms.astype(jnp.bfloat16),
            val_grid,
            preferred_element_type=jnp.float32,
        )
        return (weighted.reshape(block_len, columns), maxima.T, totals.T)

    weighted, maxima, totals = lax.map(
        per_block,
        (
            queries.reshape(blocks, block_len, columns),
            request.reshape(blocks, block_len),
            position.reshape(blocks, block_len),
        ),
    )
    return (
        weighted.reshape(row_count, columns),
        maxima.reshape(row_count, head_count),
        totals.reshape(row_count, head_count),
    )


def attend_suffix_rows(query_rows, query_req, query_pos, keys, values, request, position):
    scaling = 1.0 / math.sqrt(HEAD)
    scores = jnp.dot(query_rows, keys.T, preferred_element_type=jnp.float32) * scaling
    allowed = (request[None, :] == query_req[:, None]) & (position[None, :] <= query_pos[:, None])
    scores = jnp.where(allowed, scores, NEG)
    maxima = jnp.max(scores, axis=1, keepdims=True)
    exp_terms = jnp.exp(scores - maxima)
    totals = jnp.sum(exp_terms, axis=1, keepdims=True)
    weighted = jnp.dot(exp_terms.astype(jnp.bfloat16), values, preferred_element_type=jnp.float32)
    return (weighted, maxima, totals)


def combine(former, latter):
    weighted_a, maxima_a, totals_a = former
    weighted_b, maxima_b, totals_b = latter
    row_count, head_count = maxima_a.shape
    maxima = jnp.maximum(maxima_a, maxima_b)
    factor_a = jnp.exp(maxima_a - maxima)
    factor_b = jnp.exp(maxima_b - maxima)
    weighted = (
        weighted_a.reshape(row_count, head_count, HEAD) * factor_a[:, :, None]
        + weighted_b.reshape(row_count, head_count, HEAD) * factor_b[:, :, None]
    )
    return (
        weighted.reshape(row_count, head_count * HEAD),
        maxima,
        totals_a * factor_a + totals_b * factor_b,
    )


def per_device(
    queries,
    keys,
    values,
    prefix_keys,
    prefix_values,
    lengths,
    groups,
    residual,
    out_proj,
    norm_gain,
    expert_ids,
    expert_gates,
    w_gate,
    w_up,
    w_down,
):
    row_tok, columns = queries.shape
    head_count = columns // HEAD
    tok_dev = residual.shape[0]
    request, position, tok_group = token_layout(lengths, groups)
    request, position, tok_group = (request[0], position[0], tok_group[0])
    req_count = lax.axis_size("req")
    local_kv = jnp.stack([prefix_keys, prefix_values])
    partner = [(i, i ^ 1) for i in range(req_count)]
    partner_kv = lax.ppermute(local_kv, "req", partner)
    ring_kv = jnp.concatenate(
        [
            lax.ppermute(local_kv, "req", [(i, (i + 2 * s) % req_count) for i in range(req_count)])
            for s in range(1, req_count // 2)
        ],
        axis=2,
    )
    forwarded_kv = lax.ppermute(ring_kv, "req", partner)
    padded_index, source, block_group = group_layout(tok_group)
    padded_rows = jnp.take(queries, source, axis=0)
    prefix_part = None
    for chunk in (
        jnp.concatenate([local_kv, ring_kv], axis=2),
        jnp.concatenate([partner_kv, forwarded_kv], axis=2),
    ):
        part = attend_prefix_grouped(padded_rows, block_group, chunk[0], chunk[1])
        prefix_part = part if prefix_part is None else combine(prefix_part, part)
    suffix_part = attend_suffix_rows(
        padded_rows,
        jnp.take(request, source, axis=0),
        jnp.take(position, source, axis=0),
        keys,
        values,
        request,
        position,
    )
    weighted, maxima, totals = combine(prefix_part, suffix_part)
    padded_attended = (weighted / totals).astype(jnp.bfloat16)
    back = (padded_index[:, None] == jnp.arange(padded_rows.shape[0], dtype=jnp.int32)[None, :])
    attended = jnp.dot(
        back.astype(jnp.bfloat16), padded_attended, preferred_element_type=jnp.float32
    ).astype(jnp.bfloat16)
    exp_count = lax.axis_size("exp")
    full_proj = lax.all_gather(out_proj, "exp", axis=0, tiled=True)
    token_rows = lax.all_to_all(attended, "exp", split_axis=0, concat_axis=1, tiled=True)
    projected = jnp.dot(token_rows, full_proj, preferred_element_type=jnp.float32)
    stream = residual.astype(jnp.float32) + projected
    meansq = jnp.mean(stream * stream, axis=-1, keepdims=True)
    normed = (stream * lax.rsqrt(meansq + 1e-06) * norm_gain.astype(jnp.float32)).astype(
        jnp.bfloat16
    )
    capacity = max(2, tok_dev // 4)
    slot_count = EXPERTS * capacity
    flat_ids = expert_ids.reshape(-1)
    onehot = (flat_ids[:, None] == jnp.arange(EXPERTS, dtype=jnp.int32)[None, :]).astype(jnp.int32)
    slot_of = jnp.sum(onehot * (jnp.cumsum(onehot, axis=0) - 1), axis=1)
    dest = flat_ids * capacity + slot_of
    dest_hot = dest[:, None] == jnp.arange(slot_count, dtype=jnp.int32)[None, :]
    select = jnp.sum(dest_hot.reshape(tok_dev, TOPK, slot_count).astype(jnp.float32), axis=1)
    buffer = jnp.dot(
        select.T.astype(jnp.bfloat16), normed, preferred_element_type=jnp.float32
    ).astype(jnp.bfloat16).reshape(EXPERTS, capacity, normed.shape[1])
    exp_dev = w_gate.shape[0]
    received = lax.all_to_all(buffer, "exp", split_axis=0, concat_axis=0, tiled=True)
    slots = received.shape[1]
    width = received.shape[2]
    rows = jnp.swapaxes(received.reshape(exp_count, exp_dev, slots, width), 0, 1)
    expert_out = expert_ffn(rows.reshape(exp_dev, exp_count * slots, width), w_gate, w_up, w_down)
    expert_out = jnp.swapaxes(expert_out.reshape(exp_dev, exp_count, slots, width), 0, 1)
    returned = lax.all_to_all(
        expert_out.reshape(EXPERTS, slots, width),
        "exp",
        split_axis=0,
        concat_axis=0,
        tiled=True,
    )
    gates = expert_gates.astype(jnp.float32).reshape(tok_dev, TOPK, 1)
    weights = jnp.sum(dest_hot.reshape(tok_dev, TOPK, slot_count).astype(jnp.float32) * gates, axis=1)
    mixture = jnp.dot(
        weights.astype(jnp.bfloat16),
        returned.reshape(slot_count, received.shape[2]),
        preferred_element_type=jnp.float32,
    )
    return (stream + mixture).astype(jnp.bfloat16)


def solution(mesh):
    in_specs = (
        P("req", "exp"),
        P("req", "exp"),
        P("req", "exp"),
        P(None, "req", "exp"),
        P(None, "req", "exp"),
        P("req", None),
        P("req", None),
        P(("req", "exp"), None),
        P("exp", None),
        P(),
        P(("req", "exp"), None),
        P(("req", "exp"), None),
        P("exp", None, None),
        P("exp", None, None),
        P("exp", None, None),
    )
    out_specs = P(("req", "exp"), None)
    return jax.shard_map(
        per_device, mesh=mesh, in_specs=in_specs, out_specs=out_specs, check_vma=False
    )
```

```python
import math

import jax
import jax.numpy as jnp
from jax import lax
from jax.experimental import pallas as pl
from jax.experimental.pallas import tpu as pltpu
from jax.sharding import PartitionSpec as P

HEAD = 128
TOPK = 4
EXPERTS = 32
G = 4
RQ = 8
ROW_TOK = 1024


NEG = -1e30


def token_layout(lengths, groups):
    req_ends = jnp.cumsum(lengths, axis=-1)
    starts = req_ends - lengths
    position = jnp.arange(ROW_TOK, dtype=jnp.int32)
    request = jnp.sum((position[None, :, None] >= req_ends[:, None, :]).astype(jnp.int32), axis=-1)
    onehot = request[:, :, None] == jnp.arange(RQ, dtype=jnp.int32)[None, None, :]
    first_tok = jnp.sum(jnp.where(onehot, starts[:, None, :], 0), axis=-1)
    tok_group = jnp.sum(jnp.where(onehot, groups[:, None, :], 0), axis=-1)
    return (request, position[None, :] - first_tok, tok_group)


def split_blocks(row_count):
    if row_count % 1024 == 0 and row_count > 1024:
        return row_count // 1024
    return 1


def pack_parts(parts):
    return jnp.concatenate([parts[0], parts[1], parts[2]], axis=1)


def unpack_parts(packed, head_count):
    columns = head_count * HEAD
    return (
        packed[:, :columns],
        packed[:, columns : columns + head_count],
        packed[:, columns + head_count :],
    )


def attend_prefix(query_rows, query_group, prefix_k, prefix_v):
    row_count, columns = query_rows.shape
    head_count = columns // HEAD
    span = prefix_k.shape[1]
    key_grid = prefix_k.reshape(G, span, head_count, HEAD)
    val_grid = prefix_v.reshape(G, span, head_count, HEAD)
    blocks = split_blocks(row_count)
    block_len = row_count // blocks
    scaling = 1.0 / math.sqrt(HEAD)

    def per_block(pieces):
        block_q, block_g = pieces
        query_grid = block_q.reshape(block_len, head_count, HEAD)
        scores = (
            jnp.einsum("qhd,gkhd->hqgk", query_grid, key_grid, preferred_element_type=jnp.float32)
            * scaling
        )
        member = block_g[:, None] == jnp.arange(G, dtype=jnp.int32)[None, :]
        scores = jnp.where(member[None, :, :, None], scores, NEG)
        maxima = jnp.max(scores, axis=(2, 3))
        exp_terms = jnp.exp(scores - maxima[:, :, None, None])
        totals = jnp.sum(exp_terms, axis=(2, 3))
        weighted = jnp.einsum(
            "hqgk,gkhd->qhd",
            exp_terms.astype(jnp.bfloat16),
            val_grid,
            preferred_element_type=jnp.float32,
        )
        return (weighted.reshape(block_len, columns), maxima.T, totals.T)

    weighted, maxima, totals = lax.map(
        per_block,
        (query_rows.reshape(blocks, block_len, columns), query_group.reshape(blocks, block_len)),
    )
    return (
        weighted.reshape(row_count, columns),
        maxima.reshape(row_count, head_count),
        totals.reshape(row_count, head_count),
    )


QUERY_BLOCK = 128
KEY_BLOCK = 2048


def prefix_kernel(block_group_ref, q_ref, ka_ref, va_ref, kb_ref, vb_ref, acc_ref, m_ref, l_ref):
    scaling = 1.0 / math.sqrt(HEAD)
    q = q_ref[...]
    contract = (((1,), (1,)), ((), ()))
    s_a = lax.dot_general(q, ka_ref[0, 0], contract, preferred_element_type=jnp.float32) * scaling
    s_b = lax.dot_general(q, kb_ref[0, 0], contract, preferred_element_type=jnp.float32) * scaling
    m = jnp.maximum(jnp.max(s_a, axis=1, keepdims=True), jnp.max(s_b, axis=1, keepdims=True))
    p_a = jnp.exp(s_a - m)
    p_b = jnp.exp(s_b - m)
    acc_ref[...] = jnp.dot(
        p_a.astype(jnp.bfloat16), va_ref[0, 0], preferred_element_type=jnp.float32
    ) + jnp.dot(p_b.astype(jnp.bfloat16), vb_ref[0, 0], preferred_element_type=jnp.float32)
    m_ref[...] = jnp.broadcast_to(m, m_ref.shape)
    l_ref[...] = jnp.broadcast_to(
        jnp.sum(p_a, axis=1, keepdims=True) + jnp.sum(p_b, axis=1, keepdims=True), l_ref.shape
    )


def group_layout(query_group):
    row_count = query_group.shape[0]
    block_count = row_count // QUERY_BLOCK + G - 1
    member = query_group[:, None] == jnp.arange(G, dtype=jnp.int32)[None, :]
    counts = jnp.sum(member.astype(jnp.int32), axis=0)
    blocks = (counts + QUERY_BLOCK - 1) // QUERY_BLOCK
    first_block = jnp.cumsum(blocks) - blocks
    rank = jnp.sum(jnp.where(member, jnp.cumsum(member.astype(jnp.int32), axis=0) - 1, 0), axis=1)
    padded_index = jnp.sum(jnp.where(member, first_block[None, :], 0), axis=1) * QUERY_BLOCK + rank
    source = jnp.zeros((block_count * QUERY_BLOCK,), jnp.int32).at[padded_index].set(
        jnp.arange(row_count, dtype=jnp.int32)
    )
    block_group = jnp.sum(
        (jnp.arange(block_count, dtype=jnp.int32)[:, None] >= first_block[None, 1:]).astype(jnp.int32),
        axis=1,
    )
    return padded_index, source, block_group


def attend_prefix_grouped(padded_rows, block_group, kv_a, kv_b):
    padded_count = padded_rows.shape[0]
    block_count = padded_count // QUERY_BLOCK
    row_spec = pl.BlockSpec((QUERY_BLOCK, HEAD), lambda b, bg: (b, 0))

    def piece_specs(kv):
        span = kv.shape[2]
        return [
            pl.BlockSpec((1, 1, span, HEAD), lambda b, bg: (0, bg[b], 0, 0)),
            pl.BlockSpec((1, 1, span, HEAD), lambda b, bg: (1, bg[b], 0, 0)),
        ]

    span = kv_a.shape[2] + kv_b.shape[2]
    out_shape = jax.ShapeDtypeStruct((padded_count, HEAD), jnp.float32)
    acc, maxima, totals = pl.pallas_call(
        prefix_kernel,
        grid_spec=pltpu.PrefetchScalarGridSpec(
            num_scalar_prefetch=1,
            grid=(block_count,),
            in_specs=[row_spec] + piece_specs(kv_a) + piece_specs(kv_b),
            out_specs=[row_spec] * 3,
        ),
        out_shape=[out_shape] * 3,
        compiler_params=pltpu.CompilerParams(dimension_semantics=("arbitrary",)),
        cost_estimate=pl.CostEstimate(
            flops=4 * padded_count * span * HEAD,
            transcendentals=padded_count * span,
            bytes_accessed=2 * G * span * HEAD * 2 + padded_count * HEAD * 14,
        ),
    )(block_group, padded_rows, kv_a, kv_a, kv_b, kv_b)
    return (acc, maxima[:, :1], totals[:, :1])


def expert_kernel(x_ref, wg_ref, wu_ref, wd_ref, o_ref, total):
    f = pl.program_id(1)

    @pl.when(f == 0)
    def _():
        total[...] = jnp.zeros_like(total)

    x_t = x_ref[0]
    gate_t = jnp.dot(wg_ref[0], x_t, preferred_element_type=jnp.float32)
    up_t = jnp.dot(wu_ref[0], x_t, preferred_element_type=jnp.float32)
    hidden = (gate_t / (1.0 + jnp.exp(-gate_t)) * up_t).T.astype(jnp.bfloat16)
    total[...] += jnp.dot(hidden, wd_ref[0], preferred_element_type=jnp.float32)

    @pl.when(f == pl.num_programs(1) - 1)
    def _():
        o_ref[0] = total[...].astype(o_ref.dtype)


FE_CHUNK = 176


def expert_ffn(rows, w_gate, w_up, w_down):
    exp_dev, row_count, width = rows.shape
    inner = w_gate.shape[2]
    chunk = FE_CHUNK if inner % FE_CHUNK == 0 else inner
    gate_t = jnp.swapaxes(w_gate, 1, 2)
    up_t = jnp.swapaxes(w_up, 1, 2)
    return pl.pallas_call(
        expert_kernel,
        grid=(exp_dev, inner // chunk),
        in_specs=[
            pl.BlockSpec((1, width, row_count), lambda e, f: (e, 0, 0)),
            pl.BlockSpec((1, chunk, width), lambda e, f: (e, f, 0)),
            pl.BlockSpec((1, chunk, width), lambda e, f: (e, f, 0)),
            pl.BlockSpec((1, chunk, width), lambda e, f: (e, f, 0)),
        ],
        out_specs=pl.BlockSpec((1, row_count, width), lambda e, f: (e, 0, 0)),
        out_shape=jax.ShapeDtypeStruct((exp_dev, row_count, width), jnp.bfloat16),
        scratch_shapes=[pltpu.VMEM((row_count, width), jnp.float32)],
        compiler_params=pltpu.CompilerParams(dimension_semantics=("arbitrary", "arbitrary")),
        cost_estimate=pl.CostEstimate(
            flops=6 * exp_dev * row_count * width * inner,
            transcendentals=exp_dev * row_count * inner,
            bytes_accessed=exp_dev * (3 * width * inner + 2 * row_count * width) * 2,
        ),
    )(jnp.swapaxes(rows, 1, 2), gate_t, up_t, w_down)


def attend_suffix(queries, keys, values, request, position):
    row_count, columns = queries.shape
    head_count = columns // HEAD
    blocks = split_blocks(row_count)
    block_len = row_count // blocks
    scaling = 1.0 / math.sqrt(HEAD)
    key_grid = keys.reshape(row_count, head_count, HEAD)
    val_grid = values.reshape(row_count, head_count, HEAD)

    def per_block(pieces):
        block_q, block_req, block_pos = pieces
        query_grid = block_q.reshape(block_len, head_count, HEAD)
        scores = (
            jnp.einsum("qhd,khd->hqk", query_grid, key_grid, preferred_element_type=jnp.float32)
            * scaling
        )
        allowed = (request[None, :] == block_req[:, None]) & (
            position[None, :] <= block_pos[:, None]
        )
        scores = jnp.where(allowed[None, :, :], scores, NEG)
        maxima = jnp.max(scores, axis=2)
        exp_terms = jnp.exp(scores - maxima[:, :, None])
        totals = jnp.sum(exp_terms, axis=2)
        weighted = jnp.einsum(
            "hqk,khd->qhd",
            exp_terms.astype(jnp.bfloat16),
            val_grid,
            preferred_element_type=jnp.float32,
        )
        return (weighted.reshape(block_len, columns), maxima.T, totals.T)

    weighted, maxima, totals = lax.map(
        per_block,
        (
            queries.reshape(blocks, block_len, columns),
            request.reshape(blocks, block_len),
            position.reshape(blocks, block_len),
        ),
    )
    return (
        weighted.reshape(row_count, columns),
        maxima.reshape(row_count, head_count),
        totals.reshape(row_count, head_count),
    )


def attend_suffix_rows(query_rows, query_req, query_pos, keys, values, request, position):
    scaling = 1.0 / math.sqrt(HEAD)
    scores = jnp.dot(query_rows, keys.T, preferred_element_type=jnp.float32) * scaling
    allowed = (request[None, :] == query_req[:, None]) & (position[None, :] <= query_pos[:, None])
    scores = jnp.where(allowed, scores, NEG)
    maxima = jnp.max(scores, axis=1, keepdims=True)
    exp_terms = jnp.exp(scores - maxima)
    totals = jnp.sum(exp_terms, axis=1, keepdims=True)
    weighted = jnp.dot(exp_terms.astype(jnp.bfloat16), values, preferred_element_type=jnp.float32)
    return (weighted, maxima, totals)


def combine(former, latter):
    weighted_a, maxima_a, totals_a = former
    weighted_b, maxima_b, totals_b = latter
    row_count, head_count = maxima_a.shape
    maxima = jnp.maximum(maxima_a, maxima_b)
    factor_a = jnp.exp(maxima_a - maxima)
    factor_b = jnp.exp(maxima_b - maxima)
    weighted = (
        weighted_a.reshape(row_count, head_count, HEAD) * factor_a[:, :, None]
        + weighted_b.reshape(row_count, head_count, HEAD) * factor_b[:, :, None]
    )
    return (
        weighted.reshape(row_count, head_count * HEAD),
        maxima,
        totals_a * factor_a + totals_b * factor_b,
    )


def per_device(
    queries,
    keys,
    values,
    prefix_keys,
    prefix_values,
    lengths,
    groups,
    residual,
    out_proj,
    norm_gain,
    expert_ids,
    expert_gates,
    w_gate,
    w_up,
    w_down,
):
    row_tok, columns = queries.shape
    head_count = columns // HEAD
    tok_dev = residual.shape[0]
    request, position, tok_group = token_layout(lengths, groups)
    request, position, tok_group = (request[0], position[0], tok_group[0])
    req_count = lax.axis_size("req")
    local_kv = jnp.stack([prefix_keys, prefix_values])
    partner = [(i, i ^ 1) for i in range(req_count)]
    partner_kv = lax.ppermute(local_kv, "req", partner)
    ring_parts = [
        lax.ppermute(local_kv, "req", [(i, (i + 2 * s) % req_count) for i in range(req_count)])
        for s in range(1, req_count // 2)
    ]
    ring_kv = jnp.concatenate(ring_parts, axis=2)
    forwarded_kv = lax.ppermute(ring_kv, "req", partner)
    padded_index, source, block_group = group_layout(tok_group)
    padded_rows = jnp.take(queries, source, axis=0)
    prefix_part = combine(
        attend_prefix_grouped(padded_rows, block_group, local_kv, ring_kv),
        attend_prefix_grouped(padded_rows, block_group, partner_kv, forwarded_kv),
    )
    suffix_part = attend_suffix_rows(
        padded_rows,
        jnp.take(request, source, axis=0),
        jnp.take(position, source, axis=0),
        keys,
        values,
        request,
        position,
    )
    weighted, maxima, totals = combine(prefix_part, suffix_part)
    padded_attended = (weighted / totals).astype(jnp.bfloat16)
    back = (padded_index[:, None] == jnp.arange(padded_rows.shape[0], dtype=jnp.int32)[None, :])
    attended = jnp.dot(
        back.astype(jnp.bfloat16), padded_attended, preferred_element_type=jnp.float32
    ).astype(jnp.bfloat16)
    exp_count = lax.axis_size("exp")
    full_proj = lax.all_gather(out_proj, "exp", axis=0, tiled=True)
    token_rows = lax.all_to_all(attended, "exp", split_axis=0, concat_axis=1, tiled=True)
    projected = jnp.dot(token_rows, full_proj, preferred_element_type=jnp.float32)
    stream = residual.astype(jnp.float32) + projected
    meansq = jnp.mean(stream * stream, axis=-1, keepdims=True)
    normed = (stream * lax.rsqrt(meansq + 1e-06) * norm_gain.astype(jnp.float32)).astype(
        jnp.bfloat16
    )
    capacity = max(2, tok_dev // 4)
    slot_count = EXPERTS * capacity
    flat_ids = expert_ids.reshape(-1)
    onehot = (flat_ids[:, None] == jnp.arange(EXPERTS, dtype=jnp.int32)[None, :]).astype(jnp.int32)
    slot_of = jnp.sum(onehot * (jnp.cumsum(onehot, axis=0) - 1), axis=1)
    dest = flat_ids * capacity + slot_of
    dest_hot = dest[:, None] == jnp.arange(slot_count, dtype=jnp.int32)[None, :]
    select = jnp.sum(dest_hot.reshape(tok_dev, TOPK, slot_count).astype(jnp.float32), axis=1)
    buffer = jnp.dot(
        select.T.astype(jnp.bfloat16), normed, preferred_element_type=jnp.float32
    ).astype(jnp.bfloat16).reshape(EXPERTS, capacity, normed.shape[1])
    exp_dev = w_gate.shape[0]
    received = lax.all_to_all(buffer, "exp", split_axis=0, concat_axis=0, tiled=True)
    slots = received.shape[1]
    width = received.shape[2]
    rows = jnp.swapaxes(received.reshape(exp_count, exp_dev, slots, width), 0, 1)
    expert_out = expert_ffn(rows.reshape(exp_dev, exp_count * slots, width), w_gate, w_up, w_down)
    expert_out = jnp.swapaxes(expert_out.reshape(exp_dev, exp_count, slots, width), 0, 1)
    returned = lax.all_to_all(
        expert_out.reshape(EXPERTS, slots, width),
        "exp",
        split_axis=0,
        concat_axis=0,
        tiled=True,
    )
    gates = expert_gates.astype(jnp.float32).reshape(tok_dev, TOPK, 1)
    weights = jnp.sum(dest_hot.reshape(tok_dev, TOPK, slot_count).astype(jnp.float32) * gates, axis=1)
    mixture = jnp.dot(
        weights.astype(jnp.bfloat16),
        returned.reshape(slot_count, received.shape[2]),
        preferred_element_type=jnp.float32,
    )
    return (stream + mixture).astype(jnp.bfloat16)


def solution(mesh):
    in_specs = (
        P("req", "exp"),
        P("req", "exp"),
        P("req", "exp"),
        P(None, "req", "exp"),
        P(None, "req", "exp"),
        P("req", None),
        P("req", None),
        P(("req", "exp"), None),
        P("exp", None),
        P(),
        P(("req", "exp"), None),
        P(("req", "exp"), None),
        P("exp", None, None),
        P("exp", None, None),
        P("exp", None, None),
    )
    out_specs = P(("req", "exp"), None)
    return jax.shard_map(
        per_device, mesh=mesh, in_specs=in_specs, out_specs=out_specs, check_vma=False
    )
```

```python
import math

import jax
import jax.numpy as jnp
from jax import lax
from jax.experimental import pallas as pl
from jax.experimental.pallas import tpu as pltpu
from jax.sharding import PartitionSpec as P

HEAD = 128
TOPK = 4
EXPERTS = 32
G = 4
RQ = 8
ROW_TOK = 1024


NEG = -1e30


def token_layout(lengths, groups):
    req_ends = jnp.cumsum(lengths, axis=-1)
    starts = req_ends - lengths
    position = jnp.arange(ROW_TOK, dtype=jnp.int32)
    request = jnp.sum((position[None, :, None] >= req_ends[:, None, :]).astype(jnp.int32), axis=-1)
    onehot = request[:, :, None] == jnp.arange(RQ, dtype=jnp.int32)[None, None, :]
    first_tok = jnp.sum(jnp.where(onehot, starts[:, None, :], 0), axis=-1)
    tok_group = jnp.sum(jnp.where(onehot, groups[:, None, :], 0), axis=-1)
    return (request, position[None, :] - first_tok, tok_group)


def split_blocks(row_count):
    if row_count % 1024 == 0 and row_count > 1024:
        return row_count // 1024
    return 1


def pack_parts(parts):
    return jnp.concatenate([parts[0], parts[1], parts[2]], axis=1)


def unpack_parts(packed, head_count):
    columns = head_count * HEAD
    return (
        packed[:, :columns],
        packed[:, columns : columns + head_count],
        packed[:, columns + head_count :],
    )


def attend_prefix(query_rows, query_group, prefix_k, prefix_v):
    row_count, columns = query_rows.shape
    head_count = columns // HEAD
    span = prefix_k.shape[1]
    key_grid = prefix_k.reshape(G, span, head_count, HEAD)
    val_grid = prefix_v.reshape(G, span, head_count, HEAD)
    blocks = split_blocks(row_count)
    block_len = row_count // blocks
    scaling = 1.0 / math.sqrt(HEAD)

    def per_block(pieces):
        block_q, block_g = pieces
        query_grid = block_q.reshape(block_len, head_count, HEAD)
        scores = (
            jnp.einsum("qhd,gkhd->hqgk", query_grid, key_grid, preferred_element_type=jnp.float32)
            * scaling
        )
        member = block_g[:, None] == jnp.arange(G, dtype=jnp.int32)[None, :]
        scores = jnp.where(member[None, :, :, None], scores, NEG)
        maxima = jnp.max(scores, axis=(2, 3))
        exp_terms = jnp.exp(scores - maxima[:, :, None, None])
        totals = jnp.sum(exp_terms, axis=(2, 3))
        weighted = jnp.einsum(
            "hqgk,gkhd->qhd",
            exp_terms.astype(jnp.bfloat16),
            val_grid,
            preferred_element_type=jnp.float32,
        )
        return (weighted.reshape(block_len, columns), maxima.T, totals.T)

    weighted, maxima, totals = lax.map(
        per_block,
        (query_rows.reshape(blocks, block_len, columns), query_group.reshape(blocks, block_len)),
    )
    return (
        weighted.reshape(row_count, columns),
        maxima.reshape(row_count, head_count),
        totals.reshape(row_count, head_count),
    )


QUERY_BLOCK = 128
KEY_BLOCK = 2048


def prefix_kernel(block_group_ref, q_ref, ka_ref, va_ref, kb_ref, vb_ref, acc_ref, m_ref, l_ref):
    scaling = 1.0 / math.sqrt(HEAD)
    q = q_ref[...]
    contract = (((1,), (1,)), ((), ()))
    s_a = lax.dot_general(q, ka_ref[0, 0], contract, preferred_element_type=jnp.float32) * scaling
    s_b = lax.dot_general(q, kb_ref[0, 0], contract, preferred_element_type=jnp.float32) * scaling
    m = jnp.maximum(jnp.max(s_a, axis=1, keepdims=True), jnp.max(s_b, axis=1, keepdims=True))
    p_a = jnp.exp(s_a - m)
    p_b = jnp.exp(s_b - m)
    acc_ref[...] = jnp.dot(
        p_a.astype(jnp.bfloat16), va_ref[0, 0], preferred_element_type=jnp.float32
    ) + jnp.dot(p_b.astype(jnp.bfloat16), vb_ref[0, 0], preferred_element_type=jnp.float32)
    m_ref[...] = jnp.broadcast_to(m, m_ref.shape)
    l_ref[...] = jnp.broadcast_to(
        jnp.sum(p_a, axis=1, keepdims=True) + jnp.sum(p_b, axis=1, keepdims=True), l_ref.shape
    )


def group_layout(query_group):
    row_count = query_group.shape[0]
    block_count = row_count // QUERY_BLOCK + G - 1
    member = query_group[:, None] == jnp.arange(G, dtype=jnp.int32)[None, :]
    counts = jnp.sum(member.astype(jnp.int32), axis=0)
    blocks = (counts + QUERY_BLOCK - 1) // QUERY_BLOCK
    first_block = jnp.cumsum(blocks) - blocks
    rank = jnp.sum(jnp.where(member, jnp.cumsum(member.astype(jnp.int32), axis=0) - 1, 0), axis=1)
    padded_index = jnp.sum(jnp.where(member, first_block[None, :], 0), axis=1) * QUERY_BLOCK + rank
    source = jnp.arange(block_count * QUERY_BLOCK, dtype=jnp.int32)[:, None] == padded_index[None, :]
    block_group = jnp.sum(
        (jnp.arange(block_count, dtype=jnp.int32)[:, None] >= first_block[None, 1:]).astype(jnp.int32),
        axis=1,
    )
    return padded_index, source, block_group


def attend_prefix_grouped(padded_rows, block_group, kv_a, kv_b):
    padded_count = padded_rows.shape[0]
    block_count = padded_count // QUERY_BLOCK
    row_spec = pl.BlockSpec((QUERY_BLOCK, HEAD), lambda b, bg: (b, 0))

    def piece_specs(kv):
        span = kv.shape[2]
        return [
            pl.BlockSpec((1, 1, span, HEAD), lambda b, bg: (0, bg[b], 0, 0)),
            pl.BlockSpec((1, 1, span, HEAD), lambda b, bg: (1, bg[b], 0, 0)),
        ]

    span = kv_a.shape[2] + kv_b.shape[2]
    out_shape = jax.ShapeDtypeStruct((padded_count, HEAD), jnp.float32)
    acc, maxima, totals = pl.pallas_call(
        prefix_kernel,
        grid_spec=pltpu.PrefetchScalarGridSpec(
            num_scalar_prefetch=1,
            grid=(block_count,),
            in_specs=[row_spec] + piece_specs(kv_a) + piece_specs(kv_b),
            out_specs=[row_spec] * 3,
        ),
        out_shape=[out_shape] * 3,
        compiler_params=pltpu.CompilerParams(dimension_semantics=("arbitrary",)),
        cost_estimate=pl.CostEstimate(
            flops=4 * padded_count * span * HEAD,
            transcendentals=padded_count * span,
            bytes_accessed=2 * G * span * HEAD * 2 + padded_count * HEAD * 14,
        ),
    )(block_group, padded_rows, kv_a, kv_a, kv_b, kv_b)
    return (acc, maxima[:, :1], totals[:, :1])


def expert_kernel(x_ref, wg_ref, wu_ref, wd_ref, o_ref, total):
    f = pl.program_id(1)

    @pl.when(f == 0)
    def _():
        total[...] = jnp.zeros_like(total)

    x_t = x_ref[0]
    gate_t = jnp.dot(wg_ref[0], x_t, preferred_element_type=jnp.float32)
    up_t = jnp.dot(wu_ref[0], x_t, preferred_element_type=jnp.float32)
    hidden = (gate_t / (1.0 + jnp.exp(-gate_t)) * up_t).T.astype(jnp.bfloat16)
    total[...] += jnp.dot(hidden, wd_ref[0], preferred_element_type=jnp.float32)

    @pl.when(f == pl.num_programs(1) - 1)
    def _():
        o_ref[0] = total[...].astype(o_ref.dtype)


FE_CHUNK = 176


def expert_ffn(rows, w_gate, w_up, w_down):
    exp_dev, row_count, width = rows.shape
    inner = w_gate.shape[2]
    chunk = FE_CHUNK if inner % FE_CHUNK == 0 else inner
    gate_t = jnp.swapaxes(w_gate, 1, 2)
    up_t = jnp.swapaxes(w_up, 1, 2)
    return pl.pallas_call(
        expert_kernel,
        grid=(exp_dev, inner // chunk),
        in_specs=[
            pl.BlockSpec((1, width, row_count), lambda e, f: (e, 0, 0)),
            pl.BlockSpec((1, chunk, width), lambda e, f: (e, f, 0)),
            pl.BlockSpec((1, chunk, width), lambda e, f: (e, f, 0)),
            pl.BlockSpec((1, chunk, width), lambda e, f: (e, f, 0)),
        ],
        out_specs=pl.BlockSpec((1, row_count, width), lambda e, f: (e, 0, 0)),
        out_shape=jax.ShapeDtypeStruct((exp_dev, row_count, width), jnp.bfloat16),
        scratch_shapes=[pltpu.VMEM((row_count, width), jnp.float32)],
        compiler_params=pltpu.CompilerParams(dimension_semantics=("arbitrary", "arbitrary")),
        cost_estimate=pl.CostEstimate(
            flops=6 * exp_dev * row_count * width * inner,
            transcendentals=exp_dev * row_count * inner,
            bytes_accessed=exp_dev * (3 * width * inner + 2 * row_count * width) * 2,
        ),
    )(jnp.swapaxes(rows, 1, 2), gate_t, up_t, w_down)


def attend_suffix(queries, keys, values, request, position):
    row_count, columns = queries.shape
    head_count = columns // HEAD
    blocks = split_blocks(row_count)
    block_len = row_count // blocks
    scaling = 1.0 / math.sqrt(HEAD)
    key_grid = keys.reshape(row_count, head_count, HEAD)
    val_grid = values.reshape(row_count, head_count, HEAD)

    def per_block(pieces):
        block_q, block_req, block_pos = pieces
        query_grid = block_q.reshape(block_len, head_count, HEAD)
        scores = (
            jnp.einsum("qhd,khd->hqk", query_grid, key_grid, preferred_element_type=jnp.float32)
            * scaling
        )
        allowed = (request[None, :] == block_req[:, None]) & (
            position[None, :] <= block_pos[:, None]
        )
        scores = jnp.where(allowed[None, :, :], scores, NEG)
        maxima = jnp.max(scores, axis=2)
        exp_terms = jnp.exp(scores - maxima[:, :, None])
        totals = jnp.sum(exp_terms, axis=2)
        weighted = jnp.einsum(
            "hqk,khd->qhd",
            exp_terms.astype(jnp.bfloat16),
            val_grid,
            preferred_element_type=jnp.float32,
        )
        return (weighted.reshape(block_len, columns), maxima.T, totals.T)

    weighted, maxima, totals = lax.map(
        per_block,
        (
            queries.reshape(blocks, block_len, columns),
            request.reshape(blocks, block_len),
            position.reshape(blocks, block_len),
        ),
    )
    return (
        weighted.reshape(row_count, columns),
        maxima.reshape(row_count, head_count),
        totals.reshape(row_count, head_count),
    )


def attend_suffix_rows(query_rows, query_req, query_pos, keys, values, request, position):
    scaling = 1.0 / math.sqrt(HEAD)
    scores = jnp.dot(query_rows, keys.T, preferred_element_type=jnp.float32) * scaling
    allowed = (request[None, :] == query_req[:, None]) & (position[None, :] <= query_pos[:, None])
    scores = jnp.where(allowed, scores, NEG)
    maxima = jnp.max(scores, axis=1, keepdims=True)
    exp_terms = jnp.exp(scores - maxima)
    totals = jnp.sum(exp_terms, axis=1, keepdims=True)
    weighted = jnp.dot(exp_terms.astype(jnp.bfloat16), values, preferred_element_type=jnp.float32)
    return (weighted, maxima, totals)


def combine(former, latter):
    weighted_a, maxima_a, totals_a = former
    weighted_b, maxima_b, totals_b = latter
    row_count, head_count = maxima_a.shape
    maxima = jnp.maximum(maxima_a, maxima_b)
    factor_a = jnp.exp(maxima_a - maxima)
    factor_b = jnp.exp(maxima_b - maxima)
    weighted = (
        weighted_a.reshape(row_count, head_count, HEAD) * factor_a[:, :, None]
        + weighted_b.reshape(row_count, head_count, HEAD) * factor_b[:, :, None]
    )
    return (
        weighted.reshape(row_count, head_count * HEAD),
        maxima,
        totals_a * factor_a + totals_b * factor_b,
    )


def per_device(
    queries,
    keys,
    values,
    prefix_keys,
    prefix_values,
    lengths,
    groups,
    residual,
    out_proj,
    norm_gain,
    expert_ids,
    expert_gates,
    w_gate,
    w_up,
    w_down,
):
    row_tok, columns = queries.shape
    head_count = columns // HEAD
    tok_dev = residual.shape[0]
    request, position, tok_group = token_layout(lengths, groups)
    request, position, tok_group = (request[0], position[0], tok_group[0])
    req_count = lax.axis_size("req")
    local_kv = jnp.stack([prefix_keys, prefix_values])
    partner = [(i, i ^ 1) for i in range(req_count)]
    partner_kv = lax.ppermute(local_kv, "req", partner)
    ring_parts = [
        lax.ppermute(local_kv, "req", [(i, (i + 2 * s) % req_count) for i in range(req_count)])
        for s in range(1, req_count // 2)
    ]
    ring_kv = jnp.concatenate(ring_parts, axis=2)
    forwarded_kv = lax.ppermute(ring_kv, "req", partner)
    padded_index, source, block_group = group_layout(tok_group)
    padded_rows = jnp.dot(
        source.astype(jnp.bfloat16), queries, preferred_element_type=jnp.float32
    ).astype(jnp.bfloat16)
    prefix_part = combine(
        attend_prefix_grouped(padded_rows, block_group, local_kv, ring_kv),
        attend_prefix_grouped(padded_rows, block_group, partner_kv, forwarded_kv),
    )
    suffix_part = attend_suffix_rows(
        padded_rows,
        jnp.sum(jnp.where(source, request[None, :], 0), axis=1),
        jnp.sum(jnp.where(source, position[None, :], 0), axis=1),
        keys,
        values,
        request,
        position,
    )
    weighted, maxima, totals = combine(prefix_part, suffix_part)
    padded_attended = (weighted / totals).astype(jnp.bfloat16)
    back = (padded_index[:, None] == jnp.arange(padded_rows.shape[0], dtype=jnp.int32)[None, :])
    attended = jnp.dot(
        back.astype(jnp.bfloat16), padded_attended, preferred_element_type=jnp.float32
    ).astype(jnp.bfloat16)
    exp_count = lax.axis_size("exp")
    full_proj = lax.all_gather(out_proj, "exp", axis=0, tiled=True)
    token_rows = lax.all_to_all(attended, "exp", split_axis=0, concat_axis=1, tiled=True)
    projected = jnp.dot(token_rows, full_proj, preferred_element_type=jnp.float32)
    stream = residual.astype(jnp.float32) + projected
    meansq = jnp.mean(stream * stream, axis=-1, keepdims=True)
    normed = (stream * lax.rsqrt(meansq + 1e-06) * norm_gain.astype(jnp.float32)).astype(
        jnp.bfloat16
    )
    capacity = max(2, tok_dev // 4)
    slot_count = EXPERTS * capacity
    flat_ids = expert_ids.reshape(-1)
    onehot = (flat_ids[:, None] == jnp.arange(EXPERTS, dtype=jnp.int32)[None, :]).astype(jnp.int32)
    slot_of = jnp.sum(onehot * (jnp.cumsum(onehot, axis=0) - 1), axis=1)
    dest = flat_ids * capacity + slot_of
    dest_hot = dest[:, None] == jnp.arange(slot_count, dtype=jnp.int32)[None, :]
    select = jnp.sum(dest_hot.reshape(tok_dev, TOPK, slot_count).astype(jnp.float32), axis=1)
    buffer = jnp.dot(
        select.T.astype(jnp.bfloat16), normed, preferred_element_type=jnp.float32
    ).astype(jnp.bfloat16).reshape(EXPERTS, capacity, normed.shape[1])
    exp_dev = w_gate.shape[0]
    received = lax.all_to_all(buffer, "exp", split_axis=0, concat_axis=0, tiled=True)
    slots = received.shape[1]
    width = received.shape[2]
    rows = jnp.swapaxes(received.reshape(exp_count, exp_dev, slots, width), 0, 1)
    expert_out = expert_ffn(rows.reshape(exp_dev, exp_count * slots, width), w_gate, w_up, w_down)
    expert_out = jnp.swapaxes(expert_out.reshape(exp_dev, exp_count, slots, width), 0, 1)
    returned = lax.all_to_all(
        expert_out.reshape(EXPERTS, slots, width),
        "exp",
        split_axis=0,
        concat_axis=0,
        tiled=True,
    )
    gates = expert_gates.astype(jnp.float32).reshape(tok_dev, TOPK, 1)
    weights = jnp.sum(dest_hot.reshape(tok_dev, TOPK, slot_count).astype(jnp.float32) * gates, axis=1)
    mixture = jnp.dot(
        weights.astype(jnp.bfloat16),
        returned.reshape(slot_count, received.shape[2]),
        preferred_element_type=jnp.float32,
    )
    return (stream + mixture).astype(jnp.bfloat16)


def solution(mesh):
    in_specs = (
        P("req", "exp"),
        P("req", "exp"),
        P("req", "exp"),
        P(None, "req", "exp"),
        P(None, "req", "exp"),
        P("req", None),
        P("req", None),
        P(("req", "exp"), None),
        P("exp", None),
        P(),
        P(("req", "exp"), None),
        P(("req", "exp"), None),
        P("exp", None, None),
        P("exp", None, None),
        P("exp", None, None),
    )
    out_specs = P(("req", "exp"), None)
    return jax.shard_map(
        per_device, mesh=mesh, in_specs=in_specs, out_specs=out_specs, check_vma=False
    )
```

```python
import math

import jax
import jax.numpy as jnp
from jax import lax
from jax.experimental import pallas as pl
from jax.experimental.pallas import tpu as pltpu
from jax.sharding import PartitionSpec as P

HEAD = 128
TOPK = 4
EXPERTS = 32
G = 4
RQ = 8
ROW_TOK = 1024


NEG = -1e30


def token_layout(lengths, groups):
    req_ends = jnp.cumsum(lengths, axis=-1)
    starts = req_ends - lengths
    position = jnp.arange(ROW_TOK, dtype=jnp.int32)
    request = jnp.sum((position[None, :, None] >= req_ends[:, None, :]).astype(jnp.int32), axis=-1)
    onehot = request[:, :, None] == jnp.arange(RQ, dtype=jnp.int32)[None, None, :]
    first_tok = jnp.sum(jnp.where(onehot, starts[:, None, :], 0), axis=-1)
    tok_group = jnp.sum(jnp.where(onehot, groups[:, None, :], 0), axis=-1)
    return (request, position[None, :] - first_tok, tok_group)


def split_blocks(row_count):
    if row_count % 1024 == 0 and row_count > 1024:
        return row_count // 1024
    return 1


def pack_parts(parts):
    return jnp.concatenate([parts[0], parts[1], parts[2]], axis=1)


def unpack_parts(packed, head_count):
    columns = head_count * HEAD
    return (
        packed[:, :columns],
        packed[:, columns : columns + head_count],
        packed[:, columns + head_count :],
    )


def attend_prefix(query_rows, query_group, prefix_k, prefix_v):
    row_count, columns = query_rows.shape
    head_count = columns // HEAD
    span = prefix_k.shape[1]
    key_grid = prefix_k.reshape(G, span, head_count, HEAD)
    val_grid = prefix_v.reshape(G, span, head_count, HEAD)
    blocks = split_blocks(row_count)
    block_len = row_count // blocks
    scaling = 1.0 / math.sqrt(HEAD)

    def per_block(pieces):
        block_q, block_g = pieces
        query_grid = block_q.reshape(block_len, head_count, HEAD)
        scores = (
            jnp.einsum("qhd,gkhd->hqgk", query_grid, key_grid, preferred_element_type=jnp.float32)
            * scaling
        )
        member = block_g[:, None] == jnp.arange(G, dtype=jnp.int32)[None, :]
        scores = jnp.where(member[None, :, :, None], scores, NEG)
        maxima = jnp.max(scores, axis=(2, 3))
        exp_terms = jnp.exp(scores - maxima[:, :, None, None])
        totals = jnp.sum(exp_terms, axis=(2, 3))
        weighted = jnp.einsum(
            "hqgk,gkhd->qhd",
            exp_terms.astype(jnp.bfloat16),
            val_grid,
            preferred_element_type=jnp.float32,
        )
        return (weighted.reshape(block_len, columns), maxima.T, totals.T)

    weighted, maxima, totals = lax.map(
        per_block,
        (query_rows.reshape(blocks, block_len, columns), query_group.reshape(blocks, block_len)),
    )
    return (
        weighted.reshape(row_count, columns),
        maxima.reshape(row_count, head_count),
        totals.reshape(row_count, head_count),
    )


QUERY_BLOCK = 128
KEY_BLOCK = 2048


def prefix_kernel(block_group_ref, q_ref, ka_ref, va_ref, kb_ref, vb_ref, acc_ref, m_ref, l_ref):
    scaling = 1.0 / math.sqrt(HEAD)
    q = q_ref[...]
    contract = (((1,), (1,)), ((), ()))
    s_a = lax.dot_general(q, ka_ref[0, 0], contract, preferred_element_type=jnp.float32) * scaling
    s_b = lax.dot_general(q, kb_ref[0, 0], contract, preferred_element_type=jnp.float32) * scaling
    m = jnp.maximum(jnp.max(s_a, axis=1, keepdims=True), jnp.max(s_b, axis=1, keepdims=True))
    p_a = jnp.exp(s_a - m)
    p_b = jnp.exp(s_b - m)
    acc_ref[...] = jnp.dot(
        p_a.astype(jnp.bfloat16), va_ref[0, 0], preferred_element_type=jnp.float32
    ) + jnp.dot(p_b.astype(jnp.bfloat16), vb_ref[0, 0], preferred_element_type=jnp.float32)
    m_ref[...] = jnp.broadcast_to(m, m_ref.shape)
    l_ref[...] = jnp.broadcast_to(
        jnp.sum(p_a, axis=1, keepdims=True) + jnp.sum(p_b, axis=1, keepdims=True), l_ref.shape
    )


def group_layout(query_group):
    row_count = query_group.shape[0]
    block_count = row_count // QUERY_BLOCK + G - 1
    member = query_group[:, None] == jnp.arange(G, dtype=jnp.int32)[None, :]
    counts = jnp.sum(member.astype(jnp.int32), axis=0)
    blocks = (counts + QUERY_BLOCK - 1) // QUERY_BLOCK
    first_block = jnp.cumsum(blocks) - blocks
    rank = jnp.sum(jnp.where(member, jnp.cumsum(member.astype(jnp.int32), axis=0) - 1, 0), axis=1)
    padded_index = jnp.sum(jnp.where(member, first_block[None, :], 0), axis=1) * QUERY_BLOCK + rank
    source = jnp.arange(block_count * QUERY_BLOCK, dtype=jnp.int32)[:, None] == padded_index[None, :]
    block_group = jnp.sum(
        (jnp.arange(block_count, dtype=jnp.int32)[:, None] >= first_block[None, 1:]).astype(jnp.int32),
        axis=1,
    )
    return padded_index, source, block_group


def attend_prefix_grouped(padded_rows, block_group, kv_a, kv_b):
    padded_count = padded_rows.shape[0]
    block_count = padded_count // QUERY_BLOCK
    row_spec = pl.BlockSpec((QUERY_BLOCK, HEAD), lambda b, bg: (b, 0))

    def piece_specs(kv):
        span = kv.shape[2]
        return [
            pl.BlockSpec((1, 1, span, HEAD), lambda b, bg: (0, bg[b], 0, 0)),
            pl.BlockSpec((1, 1, span, HEAD), lambda b, bg: (1, bg[b], 0, 0)),
        ]

    span = kv_a.shape[2] + kv_b.shape[2]
    out_shape = jax.ShapeDtypeStruct((padded_count, HEAD), jnp.float32)
    acc, maxima, totals = pl.pallas_call(
        prefix_kernel,
        grid_spec=pltpu.PrefetchScalarGridSpec(
            num_scalar_prefetch=1,
            grid=(block_count,),
            in_specs=[row_spec] + piece_specs(kv_a) + piece_specs(kv_b),
            out_specs=[row_spec] * 3,
        ),
        out_shape=[out_shape] * 3,
        compiler_params=pltpu.CompilerParams(dimension_semantics=("arbitrary",)),
        cost_estimate=pl.CostEstimate(
            flops=4 * padded_count * span * HEAD,
            transcendentals=padded_count * span,
            bytes_accessed=2 * G * span * HEAD * 2 + padded_count * HEAD * 14,
        ),
    )(block_group, padded_rows, kv_a, kv_a, kv_b, kv_b)
    return (acc, maxima[:, :1], totals[:, :1])


def expert_kernel(x_ref, wg_ref, wu_ref, wd_ref, o_ref, total):
    f = pl.program_id(1)

    @pl.when(f == 0)
    def _():
        total[...] = jnp.zeros_like(total)

    x_t = x_ref[0]
    gate_t = jnp.dot(wg_ref[0], x_t, preferred_element_type=jnp.float32)
    up_t = jnp.dot(wu_ref[0], x_t, preferred_element_type=jnp.float32)
    hidden = (gate_t / (1.0 + jnp.exp(-gate_t)) * up_t).T.astype(jnp.bfloat16)
    total[...] += jnp.dot(hidden, wd_ref[0], preferred_element_type=jnp.float32)

    @pl.when(f == pl.num_programs(1) - 1)
    def _():
        o_ref[0] = total[...].astype(o_ref.dtype)


FE_CHUNK = 176


def expert_ffn(rows, w_gate, w_up, w_down):
    exp_dev, row_count, width = rows.shape
    inner = w_gate.shape[2]
    chunk = FE_CHUNK if inner % FE_CHUNK == 0 else inner
    gate_t = jnp.swapaxes(w_gate, 1, 2)
    up_t = jnp.swapaxes(w_up, 1, 2)
    return pl.pallas_call(
        expert_kernel,
        grid=(exp_dev, inner // chunk),
        in_specs=[
            pl.BlockSpec((1, width, row_count), lambda e, f: (e, 0, 0)),
            pl.BlockSpec((1, chunk, width), lambda e, f: (e, f, 0)),
            pl.BlockSpec((1, chunk, width), lambda e, f: (e, f, 0)),
            pl.BlockSpec((1, chunk, width), lambda e, f: (e, f, 0)),
        ],
        out_specs=pl.BlockSpec((1, row_count, width), lambda e, f: (e, 0, 0)),
        out_shape=jax.ShapeDtypeStruct((exp_dev, row_count, width), jnp.bfloat16),
        scratch_shapes=[pltpu.VMEM((row_count, width), jnp.float32)],
        compiler_params=pltpu.CompilerParams(dimension_semantics=("arbitrary", "arbitrary")),
        cost_estimate=pl.CostEstimate(
            flops=6 * exp_dev * row_count * width * inner,
            transcendentals=exp_dev * row_count * inner,
            bytes_accessed=exp_dev * (3 * width * inner + 2 * row_count * width) * 2,
        ),
    )(jnp.swapaxes(rows, 1, 2), gate_t, up_t, w_down)


def attend_suffix(queries, keys, values, request, position):
    row_count, columns = queries.shape
    head_count = columns // HEAD
    blocks = split_blocks(row_count)
    block_len = row_count // blocks
    scaling = 1.0 / math.sqrt(HEAD)
    key_grid = keys.reshape(row_count, head_count, HEAD)
    val_grid = values.reshape(row_count, head_count, HEAD)

    def per_block(pieces):
        block_q, block_req, block_pos = pieces
        query_grid = block_q.reshape(block_len, head_count, HEAD)
        scores = (
            jnp.einsum("qhd,khd->hqk", query_grid, key_grid, preferred_element_type=jnp.float32)
            * scaling
        )
        allowed = (request[None, :] == block_req[:, None]) & (
            position[None, :] <= block_pos[:, None]
        )
        scores = jnp.where(allowed[None, :, :], scores, NEG)
        maxima = jnp.max(scores, axis=2)
        exp_terms = jnp.exp(scores - maxima[:, :, None])
        totals = jnp.sum(exp_terms, axis=2)
        weighted = jnp.einsum(
            "hqk,khd->qhd",
            exp_terms.astype(jnp.bfloat16),
            val_grid,
            preferred_element_type=jnp.float32,
        )
        return (weighted.reshape(block_len, columns), maxima.T, totals.T)

    weighted, maxima, totals = lax.map(
        per_block,
        (
            queries.reshape(blocks, block_len, columns),
            request.reshape(blocks, block_len),
            position.reshape(blocks, block_len),
        ),
    )
    return (
        weighted.reshape(row_count, columns),
        maxima.reshape(row_count, head_count),
        totals.reshape(row_count, head_count),
    )


def attend_suffix_rows(query_rows, query_req, query_pos, keys, values, request, position):
    scaling = 1.0 / math.sqrt(HEAD)
    scores = jnp.dot(query_rows, keys.T, preferred_element_type=jnp.float32) * scaling
    allowed = (request[None, :] == query_req[:, None]) & (position[None, :] <= query_pos[:, None])
    scores = jnp.where(allowed, scores, NEG)
    maxima = jnp.max(scores, axis=1, keepdims=True)
    exp_terms = jnp.exp(scores - maxima)
    totals = jnp.sum(exp_terms, axis=1, keepdims=True)
    weighted = jnp.dot(exp_terms.astype(jnp.bfloat16), values, preferred_element_type=jnp.float32)
    return (weighted, maxima, totals)


def combine(former, latter):
    weighted_a, maxima_a, totals_a = former
    weighted_b, maxima_b, totals_b = latter
    row_count, head_count = maxima_a.shape
    maxima = jnp.maximum(maxima_a, maxima_b)
    factor_a = jnp.exp(maxima_a - maxima)
    factor_b = jnp.exp(maxima_b - maxima)
    weighted = (
        weighted_a.reshape(row_count, head_count, HEAD) * factor_a[:, :, None]
        + weighted_b.reshape(row_count, head_count, HEAD) * factor_b[:, :, None]
    )
    return (
        weighted.reshape(row_count, head_count * HEAD),
        maxima,
        totals_a * factor_a + totals_b * factor_b,
    )


def per_device(
    queries,
    keys,
    values,
    prefix_keys,
    prefix_values,
    lengths,
    groups,
    residual,
    out_proj,
    norm_gain,
    expert_ids,
    expert_gates,
    w_gate,
    w_up,
    w_down,
):
    row_tok, columns = queries.shape
    head_count = columns // HEAD
    tok_dev = residual.shape[0]
    request, position, tok_group = token_layout(lengths, groups)
    request, position, tok_group = (request[0], position[0], tok_group[0])
    req_count = lax.axis_size("req")
    local_kv = jnp.stack([prefix_keys, prefix_values])
    partner = [(i, i ^ 1) for i in range(req_count)]
    partner_kv = lax.ppermute(local_kv, "req", partner)
    ring_parts = [
        lax.ppermute(local_kv, "req", [(i, (i + 2 * s) % req_count) for i in range(req_count)])
        for s in range(1, req_count // 2)
    ]
    padded_index, source, block_group = group_layout(tok_group)
    padded_rows = jnp.dot(
        source.astype(jnp.bfloat16), queries, preferred_element_type=jnp.float32
    ).astype(jnp.bfloat16)
    suffix_part = attend_suffix_rows(
        padded_rows,
        jnp.sum(jnp.where(source, request[None, :], 0), axis=1),
        jnp.sum(jnp.where(source, position[None, :], 0), axis=1),
        keys,
        values,
        request,
        position,
    )
    ring_parts, suffix_part = lax.optimization_barrier((ring_parts, suffix_part))
    ring_kv = jnp.concatenate(ring_parts, axis=2)
    forwarded_kv = lax.ppermute(ring_kv, "req", partner)
    prefix_part = combine(
        attend_prefix_grouped(padded_rows, block_group, local_kv, ring_kv),
        attend_prefix_grouped(padded_rows, block_group, partner_kv, forwarded_kv),
    )
    weighted, maxima, totals = combine(prefix_part, suffix_part)
    padded_attended = (weighted / totals).astype(jnp.bfloat16)
    back = (padded_index[:, None] == jnp.arange(padded_rows.shape[0], dtype=jnp.int32)[None, :])
    attended = jnp.dot(
        back.astype(jnp.bfloat16), padded_attended, preferred_element_type=jnp.float32
    ).astype(jnp.bfloat16)
    exp_count = lax.axis_size("exp")
    full_proj = lax.all_gather(out_proj, "exp", axis=0, tiled=True)
    token_rows = lax.all_to_all(attended, "exp", split_axis=0, concat_axis=1, tiled=True)
    projected = jnp.dot(token_rows, full_proj, preferred_element_type=jnp.float32)
    stream = residual.astype(jnp.float32) + projected
    meansq = jnp.mean(stream * stream, axis=-1, keepdims=True)
    normed = (stream * lax.rsqrt(meansq + 1e-06) * norm_gain.astype(jnp.float32)).astype(
        jnp.bfloat16
    )
    capacity = max(2, tok_dev // 4)
    slot_count = EXPERTS * capacity
    flat_ids = expert_ids.reshape(-1)
    onehot = (flat_ids[:, None] == jnp.arange(EXPERTS, dtype=jnp.int32)[None, :]).astype(jnp.int32)
    slot_of = jnp.sum(onehot * (jnp.cumsum(onehot, axis=0) - 1), axis=1)
    dest = flat_ids * capacity + slot_of
    dest_hot = dest[:, None] == jnp.arange(slot_count, dtype=jnp.int32)[None, :]
    select = jnp.sum(dest_hot.reshape(tok_dev, TOPK, slot_count).astype(jnp.float32), axis=1)
    buffer = jnp.dot(
        select.T.astype(jnp.bfloat16), normed, preferred_element_type=jnp.float32
    ).astype(jnp.bfloat16).reshape(EXPERTS, capacity, normed.shape[1])
    exp_dev = w_gate.shape[0]
    received = lax.all_to_all(buffer, "exp", split_axis=0, concat_axis=0, tiled=True)
    slots = received.shape[1]
    width = received.shape[2]
    rows = jnp.swapaxes(received.reshape(exp_count, exp_dev, slots, width), 0, 1)
    expert_out = expert_ffn(rows.reshape(exp_dev, exp_count * slots, width), w_gate, w_up, w_down)
    expert_out = jnp.swapaxes(expert_out.reshape(exp_dev, exp_count, slots, width), 0, 1)
    returned = lax.all_to_all(
        expert_out.reshape(EXPERTS, slots, width),
        "exp",
        split_axis=0,
        concat_axis=0,
        tiled=True,
    )
    gates = expert_gates.astype(jnp.float32).reshape(tok_dev, TOPK, 1)
    weights = jnp.sum(dest_hot.reshape(tok_dev, TOPK, slot_count).astype(jnp.float32) * gates, axis=1)
    mixture = jnp.dot(
        weights.astype(jnp.bfloat16),
        returned.reshape(slot_count, received.shape[2]),
        preferred_element_type=jnp.float32,
    )
    return (stream + mixture).astype(jnp.bfloat16)


def solution(mesh):
    in_specs = (
        P("req", "exp"),
        P("req", "exp"),
        P("req", "exp"),
        P(None, "req", "exp"),
        P(None, "req", "exp"),
        P("req", None),
        P("req", None),
        P(("req", "exp"), None),
        P("exp", None),
        P(),
        P(("req", "exp"), None),
        P(("req", "exp"), None),
        P("exp", None, None),
        P("exp", None, None),
        P("exp", None, None),
    )
    out_specs = P(("req", "exp"), None)
    return jax.shard_map(
        per_device, mesh=mesh, in_specs=in_specs, out_specs=out_specs, check_vma=False
    )
```

```python
import math

import jax
import jax.numpy as jnp
from jax import lax
from jax.experimental import pallas as pl
from jax.experimental.pallas import tpu as pltpu
from jax.sharding import PartitionSpec as P

HEAD = 128
TOPK = 4
EXPERTS = 32
G = 4
RQ = 8
ROW_TOK = 1024


NEG = -1e30


def token_layout(lengths, groups):
    req_ends = jnp.cumsum(lengths, axis=-1)
    starts = req_ends - lengths
    position = jnp.arange(ROW_TOK, dtype=jnp.int32)
    request = jnp.sum((position[None, :, None] >= req_ends[:, None, :]).astype(jnp.int32), axis=-1)
    onehot = request[:, :, None] == jnp.arange(RQ, dtype=jnp.int32)[None, None, :]
    first_tok = jnp.sum(jnp.where(onehot, starts[:, None, :], 0), axis=-1)
    tok_group = jnp.sum(jnp.where(onehot, groups[:, None, :], 0), axis=-1)
    return (request, position[None, :] - first_tok, tok_group)


def split_blocks(row_count):
    if row_count % 1024 == 0 and row_count > 1024:
        return row_count // 1024
    return 1


def pack_parts(parts):
    return jnp.concatenate([parts[0], parts[1], parts[2]], axis=1)


def unpack_parts(packed, head_count):
    columns = head_count * HEAD
    return (
        packed[:, :columns],
        packed[:, columns : columns + head_count],
        packed[:, columns + head_count :],
    )


def attend_prefix(query_rows, query_group, prefix_k, prefix_v):
    row_count, columns = query_rows.shape
    head_count = columns // HEAD
    span = prefix_k.shape[1]
    key_grid = prefix_k.reshape(G, span, head_count, HEAD)
    val_grid = prefix_v.reshape(G, span, head_count, HEAD)
    blocks = split_blocks(row_count)
    block_len = row_count // blocks
    scaling = 1.0 / math.sqrt(HEAD)

    def per_block(pieces):
        block_q, block_g = pieces
        query_grid = block_q.reshape(block_len, head_count, HEAD)
        scores = (
            jnp.einsum("qhd,gkhd->hqgk", query_grid, key_grid, preferred_element_type=jnp.float32)
            * scaling
        )
        member = block_g[:, None] == jnp.arange(G, dtype=jnp.int32)[None, :]
        scores = jnp.where(member[None, :, :, None], scores, NEG)
        maxima = jnp.max(scores, axis=(2, 3))
        exp_terms = jnp.exp(scores - maxima[:, :, None, None])
        totals = jnp.sum(exp_terms, axis=(2, 3))
        weighted = jnp.einsum(
            "hqgk,gkhd->qhd",
            exp_terms.astype(jnp.bfloat16),
            val_grid,
            preferred_element_type=jnp.float32,
        )
        return (weighted.reshape(block_len, columns), maxima.T, totals.T)

    weighted, maxima, totals = lax.map(
        per_block,
        (query_rows.reshape(blocks, block_len, columns), query_group.reshape(blocks, block_len)),
    )
    return (
        weighted.reshape(row_count, columns),
        maxima.reshape(row_count, head_count),
        totals.reshape(row_count, head_count),
    )


QUERY_BLOCK = 64
KEY_BLOCK = 2048


def prefix_kernel(block_group_ref, q_ref, ka_ref, va_ref, kb_ref, vb_ref, acc_ref, m_ref, l_ref):
    scaling = 1.0 / math.sqrt(HEAD)
    q = q_ref[...]
    contract = (((1,), (1,)), ((), ()))
    s_a = lax.dot_general(q, ka_ref[0, 0], contract, preferred_element_type=jnp.float32) * scaling
    s_b = lax.dot_general(q, kb_ref[0, 0], contract, preferred_element_type=jnp.float32) * scaling
    m = jnp.maximum(jnp.max(s_a, axis=1, keepdims=True), jnp.max(s_b, axis=1, keepdims=True))
    p_a = jnp.exp(s_a - m)
    p_b = jnp.exp(s_b - m)
    acc_ref[...] = jnp.dot(
        p_a.astype(jnp.bfloat16), va_ref[0, 0], preferred_element_type=jnp.float32
    ) + jnp.dot(p_b.astype(jnp.bfloat16), vb_ref[0, 0], preferred_element_type=jnp.float32)
    m_ref[...] = jnp.broadcast_to(m, m_ref.shape)
    l_ref[...] = jnp.broadcast_to(
        jnp.sum(p_a, axis=1, keepdims=True) + jnp.sum(p_b, axis=1, keepdims=True), l_ref.shape
    )


def group_layout(query_group):
    row_count = query_group.shape[0]
    block_count = row_count // QUERY_BLOCK + G - 1
    member = query_group[:, None] == jnp.arange(G, dtype=jnp.int32)[None, :]
    counts = jnp.sum(member.astype(jnp.int32), axis=0)
    blocks = (counts + QUERY_BLOCK - 1) // QUERY_BLOCK
    first_block = jnp.cumsum(blocks) - blocks
    rank = jnp.sum(jnp.where(member, jnp.cumsum(member.astype(jnp.int32), axis=0) - 1, 0), axis=1)
    padded_index = jnp.sum(jnp.where(member, first_block[None, :], 0), axis=1) * QUERY_BLOCK + rank
    source = jnp.arange(block_count * QUERY_BLOCK, dtype=jnp.int32)[:, None] == padded_index[None, :]
    block_group = jnp.sum(
        (jnp.arange(block_count, dtype=jnp.int32)[:, None] >= first_block[None, 1:]).astype(jnp.int32),
        axis=1,
    )
    return padded_index, source, block_group


def attend_prefix_grouped(padded_rows, block_group, kv_a, kv_b):
    padded_count = padded_rows.shape[0]
    block_count = padded_count // QUERY_BLOCK
    row_spec = pl.BlockSpec((QUERY_BLOCK, HEAD), lambda b, bg: (b, 0))

    def piece_specs(kv):
        span = kv.shape[2]
        return [
            pl.BlockSpec((1, 1, span, HEAD), lambda b, bg: (0, bg[b], 0, 0)),
            pl.BlockSpec((1, 1, span, HEAD), lambda b, bg: (1, bg[b], 0, 0)),
        ]

    span = kv_a.shape[2] + kv_b.shape[2]
    out_shape = jax.ShapeDtypeStruct((padded_count, HEAD), jnp.float32)
    acc, maxima, totals = pl.pallas_call(
        prefix_kernel,
        grid_spec=pltpu.PrefetchScalarGridSpec(
            num_scalar_prefetch=1,
            grid=(block_count,),
            in_specs=[row_spec] + piece_specs(kv_a) + piece_specs(kv_b),
            out_specs=[row_spec] * 3,
        ),
        out_shape=[out_shape] * 3,
        compiler_params=pltpu.CompilerParams(dimension_semantics=("arbitrary",)),
        cost_estimate=pl.CostEstimate(
            flops=4 * padded_count * span * HEAD,
            transcendentals=padded_count * span,
            bytes_accessed=2 * G * span * HEAD * 2 + padded_count * HEAD * 14,
        ),
    )(block_group, padded_rows, kv_a, kv_a, kv_b, kv_b)
    return (acc, maxima[:, :1], totals[:, :1])


def expert_kernel(x_ref, wg_ref, wu_ref, wd_ref, o_ref, total):
    f = pl.program_id(1)

    @pl.when(f == 0)
    def _():
        total[...] = jnp.zeros_like(total)

    x_t = x_ref[0]
    gate_t = jnp.dot(wg_ref[0], x_t, preferred_element_type=jnp.float32)
    up_t = jnp.dot(wu_ref[0], x_t, preferred_element_type=jnp.float32)
    hidden = (gate_t / (1.0 + jnp.exp(-gate_t)) * up_t).T.astype(jnp.bfloat16)
    total[...] += jnp.dot(hidden, wd_ref[0], preferred_element_type=jnp.float32)

    @pl.when(f == pl.num_programs(1) - 1)
    def _():
        o_ref[0] = total[...].astype(o_ref.dtype)


FE_CHUNK = 176


def expert_ffn(rows, w_gate, w_up, w_down):
    exp_dev, row_count, width = rows.shape
    inner = w_gate.shape[2]
    chunk = FE_CHUNK if inner % FE_CHUNK == 0 else inner
    gate_t = jnp.swapaxes(w_gate, 1, 2)
    up_t = jnp.swapaxes(w_up, 1, 2)
    return pl.pallas_call(
        expert_kernel,
        grid=(exp_dev, inner // chunk),
        in_specs=[
            pl.BlockSpec((1, width, row_count), lambda e, f: (e, 0, 0)),
            pl.BlockSpec((1, chunk, width), lambda e, f: (e, f, 0)),
            pl.BlockSpec((1, chunk, width), lambda e, f: (e, f, 0)),
            pl.BlockSpec((1, chunk, width), lambda e, f: (e, f, 0)),
        ],
        out_specs=pl.BlockSpec((1, row_count, width), lambda e, f: (e, 0, 0)),
        out_shape=jax.ShapeDtypeStruct((exp_dev, row_count, width), jnp.bfloat16),
        scratch_shapes=[pltpu.VMEM((row_count, width), jnp.float32)],
        compiler_params=pltpu.CompilerParams(dimension_semantics=("arbitrary", "arbitrary")),
        cost_estimate=pl.CostEstimate(
            flops=6 * exp_dev * row_count * width * inner,
            transcendentals=exp_dev * row_count * inner,
            bytes_accessed=exp_dev * (3 * width * inner + 2 * row_count * width) * 2,
        ),
    )(jnp.swapaxes(rows, 1, 2), gate_t, up_t, w_down)


def attend_suffix(queries, keys, values, request, position):
    row_count, columns = queries.shape
    head_count = columns // HEAD
    blocks = split_blocks(row_count)
    block_len = row_count // blocks
    scaling = 1.0 / math.sqrt(HEAD)
    key_grid = keys.reshape(row_count, head_count, HEAD)
    val_grid = values.reshape(row_count, head_count, HEAD)

    def per_block(pieces):
        block_q, block_req, block_pos = pieces
        query_grid = block_q.reshape(block_len, head_count, HEAD)
        scores = (
            jnp.einsum("qhd,khd->hqk", query_grid, key_grid, preferred_element_type=jnp.float32)
            * scaling
        )
        allowed = (request[None, :] == block_req[:, None]) & (
            position[None, :] <= block_pos[:, None]
        )
        scores = jnp.where(allowed[None, :, :], scores, NEG)
        maxima = jnp.max(scores, axis=2)
        exp_terms = jnp.exp(scores - maxima[:, :, None])
        totals = jnp.sum(exp_terms, axis=2)
        weighted = jnp.einsum(
            "hqk,khd->qhd",
            exp_terms.astype(jnp.bfloat16),
            val_grid,
            preferred_element_type=jnp.float32,
        )
        return (weighted.reshape(block_len, columns), maxima.T, totals.T)

    weighted, maxima, totals = lax.map(
        per_block,
        (
            queries.reshape(blocks, block_len, columns),
            request.reshape(blocks, block_len),
            position.reshape(blocks, block_len),
        ),
    )
    return (
        weighted.reshape(row_count, columns),
        maxima.reshape(row_count, head_count),
        totals.reshape(row_count, head_count),
    )


def attend_suffix_rows(query_rows, query_req, query_pos, keys, values, request, position):
    scaling = 1.0 / math.sqrt(HEAD)
    scores = jnp.dot(query_rows, keys.T, preferred_element_type=jnp.float32) * scaling
    allowed = (request[None, :] == query_req[:, None]) & (position[None, :] <= query_pos[:, None])
    scores = jnp.where(allowed, scores, NEG)
    maxima = jnp.max(scores, axis=1, keepdims=True)
    exp_terms = jnp.exp(scores - maxima)
    totals = jnp.sum(exp_terms, axis=1, keepdims=True)
    weighted = jnp.dot(exp_terms.astype(jnp.bfloat16), values, preferred_element_type=jnp.float32)
    return (weighted, maxima, totals)


def combine(former, latter):
    weighted_a, maxima_a, totals_a = former
    weighted_b, maxima_b, totals_b = latter
    row_count, head_count = maxima_a.shape
    maxima = jnp.maximum(maxima_a, maxima_b)
    factor_a = jnp.exp(maxima_a - maxima)
    factor_b = jnp.exp(maxima_b - maxima)
    weighted = (
        weighted_a.reshape(row_count, head_count, HEAD) * factor_a[:, :, None]
        + weighted_b.reshape(row_count, head_count, HEAD) * factor_b[:, :, None]
    )
    return (
        weighted.reshape(row_count, head_count * HEAD),
        maxima,
        totals_a * factor_a + totals_b * factor_b,
    )


def per_device(
    queries,
    keys,
    values,
    prefix_keys,
    prefix_values,
    lengths,
    groups,
    residual,
    out_proj,
    norm_gain,
    expert_ids,
    expert_gates,
    w_gate,
    w_up,
    w_down,
):
    row_tok, columns = queries.shape
    head_count = columns // HEAD
    tok_dev = residual.shape[0]
    request, position, tok_group = token_layout(lengths, groups)
    request, position, tok_group = (request[0], position[0], tok_group[0])
    req_count = lax.axis_size("req")
    local_kv = jnp.stack([prefix_keys, prefix_values])
    partner = [(i, i ^ 1) for i in range(req_count)]
    partner_kv = lax.ppermute(local_kv, "req", partner)
    ring_parts = [
        lax.ppermute(local_kv, "req", [(i, (i + 2 * s) % req_count) for i in range(req_count)])
        for s in range(1, req_count // 2)
    ]
    padded_index, source, block_group = group_layout(tok_group)
    padded_rows = jnp.dot(
        source.astype(jnp.bfloat16), queries, preferred_element_type=jnp.float32
    ).astype(jnp.bfloat16)
    suffix_part = attend_suffix_rows(
        padded_rows,
        jnp.sum(jnp.where(source, request[None, :], 0), axis=1),
        jnp.sum(jnp.where(source, position[None, :], 0), axis=1),
        keys,
        values,
        request,
        position,
    )
    ring_parts, suffix_part = lax.optimization_barrier((ring_parts, suffix_part))
    ring_kv = jnp.concatenate(ring_parts, axis=2)
    forwarded_kv = lax.ppermute(ring_kv, "req", partner)
    prefix_part = combine(
        attend_prefix_grouped(padded_rows, block_group, local_kv, ring_kv),
        attend_prefix_grouped(padded_rows, block_group, partner_kv, forwarded_kv),
    )
    weighted, maxima, totals = combine(prefix_part, suffix_part)
    padded_attended = (weighted / totals).astype(jnp.bfloat16)
    back = (padded_index[:, None] == jnp.arange(padded_rows.shape[0], dtype=jnp.int32)[None, :])
    attended = jnp.dot(
        back.astype(jnp.bfloat16), padded_attended, preferred_element_type=jnp.float32
    ).astype(jnp.bfloat16)
    exp_count = lax.axis_size("exp")
    full_proj = lax.all_gather(out_proj, "exp", axis=0, tiled=True)
    token_rows = lax.all_to_all(attended, "exp", split_axis=0, concat_axis=1, tiled=True)
    projected = jnp.dot(token_rows, full_proj, preferred_element_type=jnp.float32)
    stream = residual.astype(jnp.float32) + projected
    meansq = jnp.mean(stream * stream, axis=-1, keepdims=True)
    normed = (stream * lax.rsqrt(meansq + 1e-06) * norm_gain.astype(jnp.float32)).astype(
        jnp.bfloat16
    )
    capacity = max(2, tok_dev // 4)
    slot_count = EXPERTS * capacity
    flat_ids = expert_ids.reshape(-1)
    onehot = (flat_ids[:, None] == jnp.arange(EXPERTS, dtype=jnp.int32)[None, :]).astype(jnp.int32)
    slot_of = jnp.sum(onehot * (jnp.cumsum(onehot, axis=0) - 1), axis=1)
    dest = flat_ids * capacity + slot_of
    dest_hot = dest[:, None] == jnp.arange(slot_count, dtype=jnp.int32)[None, :]
    select = jnp.sum(dest_hot.reshape(tok_dev, TOPK, slot_count).astype(jnp.float32), axis=1)
    buffer = jnp.dot(
        select.T.astype(jnp.bfloat16), normed, preferred_element_type=jnp.float32
    ).astype(jnp.bfloat16).reshape(EXPERTS, capacity, normed.shape[1])
    exp_dev = w_gate.shape[0]
    received = lax.all_to_all(buffer, "exp", split_axis=0, concat_axis=0, tiled=True)
    slots = received.shape[1]
    width = received.shape[2]
    rows = jnp.swapaxes(received.reshape(exp_count, exp_dev, slots, width), 0, 1)
    expert_out = expert_ffn(rows.reshape(exp_dev, exp_count * slots, width), w_gate, w_up, w_down)
    expert_out = jnp.swapaxes(expert_out.reshape(exp_dev, exp_count, slots, width), 0, 1)
    returned = lax.all_to_all(
        expert_out.reshape(EXPERTS, slots, width),
        "exp",
        split_axis=0,
        concat_axis=0,
        tiled=True,
    )
    gates = expert_gates.astype(jnp.float32).reshape(tok_dev, TOPK, 1)
    weights = jnp.sum(dest_hot.reshape(tok_dev, TOPK, slot_count).astype(jnp.float32) * gates, axis=1)
    mixture = jnp.dot(
        weights.astype(jnp.bfloat16),
        returned.reshape(slot_count, received.shape[2]),
        preferred_element_type=jnp.float32,
    )
    return (stream + mixture).astype(jnp.bfloat16)


def solution(mesh):
    in_specs = (
        P("req", "exp"),
        P("req", "exp"),
        P("req", "exp"),
        P(None, "req", "exp"),
        P(None, "req", "exp"),
        P("req", None),
        P("req", None),
        P(("req", "exp"), None),
        P("exp", None),
        P(),
        P(("req", "exp"), None),
        P(("req", "exp"), None),
        P("exp", None, None),
        P("exp", None, None),
        P("exp", None, None),
    )
    out_specs = P(("req", "exp"), None)
    return jax.shard_map(
        per_device, mesh=mesh, in_specs=in_specs, out_specs=out_specs, check_vma=False
    )
```

```python
import math

import jax
import jax.numpy as jnp
from jax import lax
from jax.experimental import pallas as pl
from jax.experimental.pallas import tpu as pltpu
from jax.sharding import PartitionSpec as P

HEAD = 128
TOPK = 4
EXPERTS = 32
G = 4
RQ = 8
ROW_TOK = 1024


NEG = -1e30


def token_layout(lengths, groups):
    req_ends = jnp.cumsum(lengths, axis=-1)
    starts = req_ends - lengths
    position = jnp.arange(ROW_TOK, dtype=jnp.int32)
    request = jnp.sum((position[None, :, None] >= req_ends[:, None, :]).astype(jnp.int32), axis=-1)
    onehot = request[:, :, None] == jnp.arange(RQ, dtype=jnp.int32)[None, None, :]
    first_tok = jnp.sum(jnp.where(onehot, starts[:, None, :], 0), axis=-1)
    tok_group = jnp.sum(jnp.where(onehot, groups[:, None, :], 0), axis=-1)
    return (request, position[None, :] - first_tok, tok_group)


def split_blocks(row_count):
    if row_count % 1024 == 0 and row_count > 1024:
        return row_count // 1024
    return 1


def pack_parts(parts):
    return jnp.concatenate([parts[0], parts[1], parts[2]], axis=1)


def unpack_parts(packed, head_count):
    columns = head_count * HEAD
    return (
        packed[:, :columns],
        packed[:, columns : columns + head_count],
        packed[:, columns + head_count :],
    )


def attend_prefix(query_rows, query_group, prefix_k, prefix_v):
    row_count, columns = query_rows.shape
    head_count = columns // HEAD
    span = prefix_k.shape[1]
    key_grid = prefix_k.reshape(G, span, head_count, HEAD)
    val_grid = prefix_v.reshape(G, span, head_count, HEAD)
    blocks = split_blocks(row_count)
    block_len = row_count // blocks
    scaling = 1.0 / math.sqrt(HEAD)

    def per_block(pieces):
        block_q, block_g = pieces
        query_grid = block_q.reshape(block_len, head_count, HEAD)
        scores = (
            jnp.einsum("qhd,gkhd->hqgk", query_grid, key_grid, preferred_element_type=jnp.float32)
            * scaling
        )
        member = block_g[:, None] == jnp.arange(G, dtype=jnp.int32)[None, :]
        scores = jnp.where(member[None, :, :, None], scores, NEG)
        maxima = jnp.max(scores, axis=(2, 3))
        exp_terms = jnp.exp(scores - maxima[:, :, None, None])
        totals = jnp.sum(exp_terms, axis=(2, 3))
        weighted = jnp.einsum(
            "hqgk,gkhd->qhd",
            exp_terms.astype(jnp.bfloat16),
            val_grid,
            preferred_element_type=jnp.float32,
        )
        return (weighted.reshape(block_len, columns), maxima.T, totals.T)

    weighted, maxima, totals = lax.map(
        per_block,
        (query_rows.reshape(blocks, block_len, columns), query_group.reshape(blocks, block_len)),
    )
    return (
        weighted.reshape(row_count, columns),
        maxima.reshape(row_count, head_count),
        totals.reshape(row_count, head_count),
    )


QUERY_BLOCK = 256
KEY_BLOCK = 2048


def prefix_kernel(block_group_ref, q_ref, ka_ref, va_ref, kb_ref, vb_ref, acc_ref, m_ref, l_ref):
    scaling = 1.0 / math.sqrt(HEAD)
    q = q_ref[...]
    contract = (((1,), (1,)), ((), ()))
    s_a = lax.dot_general(q, ka_ref[0, 0], contract, preferred_element_type=jnp.float32) * scaling
    s_b = lax.dot_general(q, kb_ref[0, 0], contract, preferred_element_type=jnp.float32) * scaling
    m = jnp.maximum(jnp.max(s_a, axis=1, keepdims=True), jnp.max(s_b, axis=1, keepdims=True))
    p_a = jnp.exp(s_a - m)
    p_b = jnp.exp(s_b - m)
    acc_ref[...] = jnp.dot(
        p_a.astype(jnp.bfloat16), va_ref[0, 0], preferred_element_type=jnp.float32
    ) + jnp.dot(p_b.astype(jnp.bfloat16), vb_ref[0, 0], preferred_element_type=jnp.float32)
    m_ref[...] = jnp.broadcast_to(m, m_ref.shape)
    l_ref[...] = jnp.broadcast_to(
        jnp.sum(p_a, axis=1, keepdims=True) + jnp.sum(p_b, axis=1, keepdims=True), l_ref.shape
    )


def group_layout(query_group):
    row_count = query_group.shape[0]
    block_count = row_count // QUERY_BLOCK + G - 1
    member = query_group[:, None] == jnp.arange(G, dtype=jnp.int32)[None, :]
    counts = jnp.sum(member.astype(jnp.int32), axis=0)
    blocks = (counts + QUERY_BLOCK - 1) // QUERY_BLOCK
    first_block = jnp.cumsum(blocks) - blocks
    rank = jnp.sum(jnp.where(member, jnp.cumsum(member.astype(jnp.int32), axis=0) - 1, 0), axis=1)
    padded_index = jnp.sum(jnp.where(member, first_block[None, :], 0), axis=1) * QUERY_BLOCK + rank
    source = jnp.arange(block_count * QUERY_BLOCK, dtype=jnp.int32)[:, None] == padded_index[None, :]
    block_group = jnp.sum(
        (jnp.arange(block_count, dtype=jnp.int32)[:, None] >= first_block[None, 1:]).astype(jnp.int32),
        axis=1,
    )
    return padded_index, source, block_group


def attend_prefix_grouped(padded_rows, block_group, kv_a, kv_b):
    padded_count = padded_rows.shape[0]
    block_count = padded_count // QUERY_BLOCK
    row_spec = pl.BlockSpec((QUERY_BLOCK, HEAD), lambda b, bg: (b, 0))

    def piece_specs(kv):
        span = kv.shape[2]
        return [
            pl.BlockSpec((1, 1, span, HEAD), lambda b, bg: (0, bg[b], 0, 0)),
            pl.BlockSpec((1, 1, span, HEAD), lambda b, bg: (1, bg[b], 0, 0)),
        ]

    span = kv_a.shape[2] + kv_b.shape[2]
    out_shape = jax.ShapeDtypeStruct((padded_count, HEAD), jnp.float32)
    acc, maxima, totals = pl.pallas_call(
        prefix_kernel,
        grid_spec=pltpu.PrefetchScalarGridSpec(
            num_scalar_prefetch=1,
            grid=(block_count,),
            in_specs=[row_spec] + piece_specs(kv_a) + piece_specs(kv_b),
            out_specs=[row_spec] * 3,
        ),
        out_shape=[out_shape] * 3,
        compiler_params=pltpu.CompilerParams(dimension_semantics=("arbitrary",)),
        cost_estimate=pl.CostEstimate(
            flops=4 * padded_count * span * HEAD,
            transcendentals=padded_count * span,
            bytes_accessed=2 * G * span * HEAD * 2 + padded_count * HEAD * 14,
        ),
    )(block_group, padded_rows, kv_a, kv_a, kv_b, kv_b)
    return (acc, maxima[:, :1], totals[:, :1])


def expert_kernel(x_ref, wg_ref, wu_ref, wd_ref, o_ref, total):
    f = pl.program_id(1)

    @pl.when(f == 0)
    def _():
        total[...] = jnp.zeros_like(total)

    x_t = x_ref[0]
    gate_t = jnp.dot(wg_ref[0], x_t, preferred_element_type=jnp.float32)
    up_t = jnp.dot(wu_ref[0], x_t, preferred_element_type=jnp.float32)
    hidden = (gate_t / (1.0 + jnp.exp(-gate_t)) * up_t).T.astype(jnp.bfloat16)
    total[...] += jnp.dot(hidden, wd_ref[0], preferred_element_type=jnp.float32)

    @pl.when(f == pl.num_programs(1) - 1)
    def _():
        o_ref[0] = total[...].astype(o_ref.dtype)


FE_CHUNK = 176


def expert_ffn(rows, w_gate, w_up, w_down):
    exp_dev, row_count, width = rows.shape
    inner = w_gate.shape[2]
    chunk = FE_CHUNK if inner % FE_CHUNK == 0 else inner
    gate_t = jnp.swapaxes(w_gate, 1, 2)
    up_t = jnp.swapaxes(w_up, 1, 2)
    return pl.pallas_call(
        expert_kernel,
        grid=(exp_dev, inner // chunk),
        in_specs=[
            pl.BlockSpec((1, width, row_count), lambda e, f: (e, 0, 0)),
            pl.BlockSpec((1, chunk, width), lambda e, f: (e, f, 0)),
            pl.BlockSpec((1, chunk, width), lambda e, f: (e, f, 0)),
            pl.BlockSpec((1, chunk, width), lambda e, f: (e, f, 0)),
        ],
        out_specs=pl.BlockSpec((1, row_count, width), lambda e, f: (e, 0, 0)),
        out_shape=jax.ShapeDtypeStruct((exp_dev, row_count, width), jnp.bfloat16),
        scratch_shapes=[pltpu.VMEM((row_count, width), jnp.float32)],
        compiler_params=pltpu.CompilerParams(dimension_semantics=("arbitrary", "arbitrary")),
        cost_estimate=pl.CostEstimate(
            flops=6 * exp_dev * row_count * width * inner,
            transcendentals=exp_dev * row_count * inner,
            bytes_accessed=exp_dev * (3 * width * inner + 2 * row_count * width) * 2,
        ),
    )(jnp.swapaxes(rows, 1, 2), gate_t, up_t, w_down)


def attend_suffix(queries, keys, values, request, position):
    row_count, columns = queries.shape
    head_count = columns // HEAD
    blocks = split_blocks(row_count)
    block_len = row_count // blocks
    scaling = 1.0 / math.sqrt(HEAD)
    key_grid = keys.reshape(row_count, head_count, HEAD)
    val_grid = values.reshape(row_count, head_count, HEAD)

    def per_block(pieces):
        block_q, block_req, block_pos = pieces
        query_grid = block_q.reshape(block_len, head_count, HEAD)
        scores = (
            jnp.einsum("qhd,khd->hqk", query_grid, key_grid, preferred_element_type=jnp.float32)
            * scaling
        )
        allowed = (request[None, :] == block_req[:, None]) & (
            position[None, :] <= block_pos[:, None]
        )
        scores = jnp.where(allowed[None, :, :], scores, NEG)
        maxima = jnp.max(scores, axis=2)
        exp_terms = jnp.exp(scores - maxima[:, :, None])
        totals = jnp.sum(exp_terms, axis=2)
        weighted = jnp.einsum(
            "hqk,khd->qhd",
            exp_terms.astype(jnp.bfloat16),
            val_grid,
            preferred_element_type=jnp.float32,
        )
        return (weighted.reshape(block_len, columns), maxima.T, totals.T)

    weighted, maxima, totals = lax.map(
        per_block,
        (
            queries.reshape(blocks, block_len, columns),
            request.reshape(blocks, block_len),
            position.reshape(blocks, block_len),
        ),
    )
    return (
        weighted.reshape(row_count, columns),
        maxima.reshape(row_count, head_count),
        totals.reshape(row_count, head_count),
    )


def attend_suffix_rows(query_rows, query_req, query_pos, keys, values, request, position):
    scaling = 1.0 / math.sqrt(HEAD)
    scores = jnp.dot(query_rows, keys.T, preferred_element_type=jnp.float32) * scaling
    allowed = (request[None, :] == query_req[:, None]) & (position[None, :] <= query_pos[:, None])
    scores = jnp.where(allowed, scores, NEG)
    maxima = jnp.max(scores, axis=1, keepdims=True)
    exp_terms = jnp.exp(scores - maxima)
    totals = jnp.sum(exp_terms, axis=1, keepdims=True)
    weighted = jnp.dot(exp_terms.astype(jnp.bfloat16), values, preferred_element_type=jnp.float32)
    return (weighted, maxima, totals)


def combine(former, latter):
    weighted_a, maxima_a, totals_a = former
    weighted_b, maxima_b, totals_b = latter
    row_count, head_count = maxima_a.shape
    maxima = jnp.maximum(maxima_a, maxima_b)
    factor_a = jnp.exp(maxima_a - maxima)
    factor_b = jnp.exp(maxima_b - maxima)
    weighted = (
        weighted_a.reshape(row_count, head_count, HEAD) * factor_a[:, :, None]
        + weighted_b.reshape(row_count, head_count, HEAD) * factor_b[:, :, None]
    )
    return (
        weighted.reshape(row_count, head_count * HEAD),
        maxima,
        totals_a * factor_a + totals_b * factor_b,
    )


def per_device(
    queries,
    keys,
    values,
    prefix_keys,
    prefix_values,
    lengths,
    groups,
    residual,
    out_proj,
    norm_gain,
    expert_ids,
    expert_gates,
    w_gate,
    w_up,
    w_down,
):
    row_tok, columns = queries.shape
    head_count = columns // HEAD
    tok_dev = residual.shape[0]
    request, position, tok_group = token_layout(lengths, groups)
    request, position, tok_group = (request[0], position[0], tok_group[0])
    req_count = lax.axis_size("req")
    local_kv = jnp.stack([prefix_keys, prefix_values])
    partner = [(i, i ^ 1) for i in range(req_count)]
    partner_kv = lax.ppermute(local_kv, "req", partner)
    ring_parts = [
        lax.ppermute(local_kv, "req", [(i, (i + 2 * s) % req_count) for i in range(req_count)])
        for s in range(1, req_count // 2)
    ]
    padded_index, source, block_group = group_layout(tok_group)
    padded_rows = jnp.dot(
        source.astype(jnp.bfloat16), queries, preferred_element_type=jnp.float32
    ).astype(jnp.bfloat16)
    suffix_part = attend_suffix_rows(
        padded_rows,
        jnp.sum(jnp.where(source, request[None, :], 0), axis=1),
        jnp.sum(jnp.where(source, position[None, :], 0), axis=1),
        keys,
        values,
        request,
        position,
    )
    ring_parts, suffix_part = lax.optimization_barrier((ring_parts, suffix_part))
    ring_kv = jnp.concatenate(ring_parts, axis=2)
    forwarded_kv = lax.ppermute(ring_kv, "req", partner)
    prefix_part = combine(
        attend_prefix_grouped(padded_rows, block_group, local_kv, ring_kv),
        attend_prefix_grouped(padded_rows, block_group, partner_kv, forwarded_kv),
    )
    weighted, maxima, totals = combine(prefix_part, suffix_part)
    padded_attended = (weighted / totals).astype(jnp.bfloat16)
    back = (padded_index[:, None] == jnp.arange(padded_rows.shape[0], dtype=jnp.int32)[None, :])
    attended = jnp.dot(
        back.astype(jnp.bfloat16), padded_attended, preferred_element_type=jnp.float32
    ).astype(jnp.bfloat16)
    exp_count = lax.axis_size("exp")
    full_proj = lax.all_gather(out_proj, "exp", axis=0, tiled=True)
    token_rows = lax.all_to_all(attended, "exp", split_axis=0, concat_axis=1, tiled=True)
    projected = jnp.dot(token_rows, full_proj, preferred_element_type=jnp.float32)
    stream = residual.astype(jnp.float32) + projected
    meansq = jnp.mean(stream * stream, axis=-1, keepdims=True)
    normed = (stream * lax.rsqrt(meansq + 1e-06) * norm_gain.astype(jnp.float32)).astype(
        jnp.bfloat16
    )
    capacity = max(2, tok_dev // 4)
    slot_count = EXPERTS * capacity
    flat_ids = expert_ids.reshape(-1)
    onehot = (flat_ids[:, None] == jnp.arange(EXPERTS, dtype=jnp.int32)[None, :]).astype(jnp.int32)
    slot_of = jnp.sum(onehot * (jnp.cumsum(onehot, axis=0) - 1), axis=1)
    dest = flat_ids * capacity + slot_of
    dest_hot = dest[:, None] == jnp.arange(slot_count, dtype=jnp.int32)[None, :]
    select = jnp.sum(dest_hot.reshape(tok_dev, TOPK, slot_count).astype(jnp.float32), axis=1)
    buffer = jnp.dot(
        select.T.astype(jnp.bfloat16), normed, preferred_element_type=jnp.float32
    ).astype(jnp.bfloat16).reshape(EXPERTS, capacity, normed.shape[1])
    exp_dev = w_gate.shape[0]
    received = lax.all_to_all(buffer, "exp", split_axis=0, concat_axis=0, tiled=True)
    slots = received.shape[1]
    width = received.shape[2]
    rows = jnp.swapaxes(received.reshape(exp_count, exp_dev, slots, width), 0, 1)
    expert_out = expert_ffn(rows.reshape(exp_dev, exp_count * slots, width), w_gate, w_up, w_down)
    expert_out = jnp.swapaxes(expert_out.reshape(exp_dev, exp_count, slots, width), 0, 1)
    returned = lax.all_to_all(
        expert_out.reshape(EXPERTS, slots, width),
        "exp",
        split_axis=0,
        concat_axis=0,
        tiled=True,
    )
    gates = expert_gates.astype(jnp.float32).reshape(tok_dev, TOPK, 1)
    weights = jnp.sum(dest_hot.reshape(tok_dev, TOPK, slot_count).astype(jnp.float32) * gates, axis=1)
    mixture = jnp.dot(
        weights.astype(jnp.bfloat16),
        returned.reshape(slot_count, received.shape[2]),
        preferred_element_type=jnp.float32,
    )
    return (stream + mixture).astype(jnp.bfloat16)


def solution(mesh):
    in_specs = (
        P("req", "exp"),
        P("req", "exp"),
        P("req", "exp"),
        P(None, "req", "exp"),
        P(None, "req", "exp"),
        P("req", None),
        P("req", None),
        P(("req", "exp"), None),
        P("exp", None),
        P(),
        P(("req", "exp"), None),
        P(("req", "exp"), None),
        P("exp", None, None),
        P("exp", None, None),
        P("exp", None, None),
    )
    out_specs = P(("req", "exp"), None)
    return jax.shard_map(
        per_device, mesh=mesh, in_specs=in_specs, out_specs=out_specs, check_vma=False
    )
```

```python
import math

import jax
import jax.numpy as jnp
from jax import lax
from jax.experimental import pallas as pl
from jax.experimental.pallas import tpu as pltpu
from jax.sharding import PartitionSpec as P

HEAD = 128
TOPK = 4
EXPERTS = 32
G = 4
RQ = 8
ROW_TOK = 1024


NEG = -1e30


def token_layout(lengths, groups):
    req_ends = jnp.cumsum(lengths, axis=-1)
    starts = req_ends - lengths
    position = jnp.arange(ROW_TOK, dtype=jnp.int32)
    request = jnp.sum((position[None, :, None] >= req_ends[:, None, :]).astype(jnp.int32), axis=-1)
    onehot = request[:, :, None] == jnp.arange(RQ, dtype=jnp.int32)[None, None, :]
    first_tok = jnp.sum(jnp.where(onehot, starts[:, None, :], 0), axis=-1)
    tok_group = jnp.sum(jnp.where(onehot, groups[:, None, :], 0), axis=-1)
    return (request, position[None, :] - first_tok, tok_group)


def split_blocks(row_count):
    if row_count % 1024 == 0 and row_count > 1024:
        return row_count // 1024
    return 1


def pack_parts(parts):
    return jnp.concatenate([parts[0], parts[1], parts[2]], axis=1)


def unpack_parts(packed, head_count):
    columns = head_count * HEAD
    return (
        packed[:, :columns],
        packed[:, columns : columns + head_count],
        packed[:, columns + head_count :],
    )


def attend_prefix(query_rows, query_group, prefix_k, prefix_v):
    row_count, columns = query_rows.shape
    head_count = columns // HEAD
    span = prefix_k.shape[1]
    key_grid = prefix_k.reshape(G, span, head_count, HEAD)
    val_grid = prefix_v.reshape(G, span, head_count, HEAD)
    blocks = split_blocks(row_count)
    block_len = row_count // blocks
    scaling = 1.0 / math.sqrt(HEAD)

    def per_block(pieces):
        block_q, block_g = pieces
        query_grid = block_q.reshape(block_len, head_count, HEAD)
        scores = (
            jnp.einsum("qhd,gkhd->hqgk", query_grid, key_grid, preferred_element_type=jnp.float32)
            * scaling
        )
        member = block_g[:, None] == jnp.arange(G, dtype=jnp.int32)[None, :]
        scores = jnp.where(member[None, :, :, None], scores, NEG)
        maxima = jnp.max(scores, axis=(2, 3))
        exp_terms = jnp.exp(scores - maxima[:, :, None, None])
        totals = jnp.sum(exp_terms, axis=(2, 3))
        weighted = jnp.einsum(
            "hqgk,gkhd->qhd",
            exp_terms.astype(jnp.bfloat16),
            val_grid,
            preferred_element_type=jnp.float32,
        )
        return (weighted.reshape(block_len, columns), maxima.T, totals.T)

    weighted, maxima, totals = lax.map(
        per_block,
        (query_rows.reshape(blocks, block_len, columns), query_group.reshape(blocks, block_len)),
    )
    return (
        weighted.reshape(row_count, columns),
        maxima.reshape(row_count, head_count),
        totals.reshape(row_count, head_count),
    )


QUERY_BLOCK = 256
KEY_BLOCK = 2048


def prefix_kernel(block_group_ref, q_ref, *refs):
    scaling = 1.0 / math.sqrt(HEAD)
    acc_ref, m_ref, l_ref = refs[-3:]
    pieces = refs[:-3]
    q = q_ref[...]
    contract = (((1,), (1,)), ((), ()))
    scores = [
        lax.dot_general(q, pieces[i][0, 0], contract, preferred_element_type=jnp.float32) * scaling
        for i in range(0, len(pieces), 2)
    ]
    m = scores[0].max(axis=1, keepdims=True)
    for s in scores[1:]:
        m = jnp.maximum(m, s.max(axis=1, keepdims=True))
    acc = None
    total = None
    for i, s in enumerate(scores):
        p = jnp.exp(s - m)
        term = jnp.dot(p.astype(jnp.bfloat16), pieces[2 * i + 1][0, 0], preferred_element_type=jnp.float32)
        acc = term if acc is None else acc + term
        row_sum = jnp.sum(p, axis=1, keepdims=True)
        total = row_sum if total is None else total + row_sum
    acc_ref[...] = acc
    m_ref[...] = jnp.broadcast_to(m, m_ref.shape)
    l_ref[...] = jnp.broadcast_to(total, l_ref.shape)


def group_layout(query_group):
    row_count = query_group.shape[0]
    block_count = row_count // QUERY_BLOCK + G - 1
    member = query_group[:, None] == jnp.arange(G, dtype=jnp.int32)[None, :]
    counts = jnp.sum(member.astype(jnp.int32), axis=0)
    blocks = (counts + QUERY_BLOCK - 1) // QUERY_BLOCK
    first_block = jnp.cumsum(blocks) - blocks
    rank = jnp.sum(jnp.where(member, jnp.cumsum(member.astype(jnp.int32), axis=0) - 1, 0), axis=1)
    padded_index = jnp.sum(jnp.where(member, first_block[None, :], 0), axis=1) * QUERY_BLOCK + rank
    source = jnp.arange(block_count * QUERY_BLOCK, dtype=jnp.int32)[:, None] == padded_index[None, :]
    block_group = jnp.sum(
        (jnp.arange(block_count, dtype=jnp.int32)[:, None] >= first_block[None, 1:]).astype(jnp.int32),
        axis=1,
    )
    return padded_index, source, block_group


def attend_prefix_grouped(padded_rows, block_group, *kv_list):
    padded_count = padded_rows.shape[0]
    block_count = padded_count // QUERY_BLOCK
    row_spec = pl.BlockSpec((QUERY_BLOCK, HEAD), lambda b, bg: (b, 0))

    def piece_specs(kv):
        span = kv.shape[2]
        return [
            pl.BlockSpec((1, 1, span, HEAD), lambda b, bg: (0, bg[b], 0, 0)),
            pl.BlockSpec((1, 1, span, HEAD), lambda b, bg: (1, bg[b], 0, 0)),
        ]

    span = sum(kv.shape[2] for kv in kv_list)
    out_shape = jax.ShapeDtypeStruct((padded_count, HEAD), jnp.float32)
    acc, maxima, totals = pl.pallas_call(
        prefix_kernel,
        grid_spec=pltpu.PrefetchScalarGridSpec(
            num_scalar_prefetch=1,
            grid=(block_count,),
            in_specs=[row_spec] + [spec for kv in kv_list for spec in piece_specs(kv)],
            out_specs=[row_spec] * 3,
        ),
        out_shape=[out_shape] * 3,
        compiler_params=pltpu.CompilerParams(dimension_semantics=("arbitrary",)),
        cost_estimate=pl.CostEstimate(
            flops=4 * padded_count * span * HEAD,
            transcendentals=padded_count * span,
            bytes_accessed=2 * G * span * HEAD * 2 + padded_count * HEAD * 14,
        ),
    )(block_group, padded_rows, *[kv for kv in kv_list for _ in range(2)])
    return (acc, maxima[:, :1], totals[:, :1])


def expert_kernel(x_ref, wg_ref, wu_ref, wd_ref, o_ref, total):
    f = pl.program_id(1)

    @pl.when(f == 0)
    def _():
        total[...] = jnp.zeros_like(total)

    x_t = x_ref[0]
    gate_t = jnp.dot(wg_ref[0], x_t, preferred_element_type=jnp.float32)
    up_t = jnp.dot(wu_ref[0], x_t, preferred_element_type=jnp.float32)
    hidden = (gate_t / (1.0 + jnp.exp(-gate_t)) * up_t).T.astype(jnp.bfloat16)
    total[...] += jnp.dot(hidden, wd_ref[0], preferred_element_type=jnp.float32)

    @pl.when(f == pl.num_programs(1) - 1)
    def _():
        o_ref[0] = total[...].astype(o_ref.dtype)


FE_CHUNK = 176


def expert_ffn(rows, w_gate, w_up, w_down):
    exp_dev, row_count, width = rows.shape
    inner = w_gate.shape[2]
    chunk = FE_CHUNK if inner % FE_CHUNK == 0 else inner
    gate_t = jnp.swapaxes(w_gate, 1, 2)
    up_t = jnp.swapaxes(w_up, 1, 2)
    return pl.pallas_call(
        expert_kernel,
        grid=(exp_dev, inner // chunk),
        in_specs=[
            pl.BlockSpec((1, width, row_count), lambda e, f: (e, 0, 0)),
            pl.BlockSpec((1, chunk, width), lambda e, f: (e, f, 0)),
            pl.BlockSpec((1, chunk, width), lambda e, f: (e, f, 0)),
            pl.BlockSpec((1, chunk, width), lambda e, f: (e, f, 0)),
        ],
        out_specs=pl.BlockSpec((1, row_count, width), lambda e, f: (e, 0, 0)),
        out_shape=jax.ShapeDtypeStruct((exp_dev, row_count, width), jnp.bfloat16),
        scratch_shapes=[pltpu.VMEM((row_count, width), jnp.float32)],
        compiler_params=pltpu.CompilerParams(dimension_semantics=("arbitrary", "arbitrary")),
        cost_estimate=pl.CostEstimate(
            flops=6 * exp_dev * row_count * width * inner,
            transcendentals=exp_dev * row_count * inner,
            bytes_accessed=exp_dev * (3 * width * inner + 2 * row_count * width) * 2,
        ),
    )(jnp.swapaxes(rows, 1, 2), gate_t, up_t, w_down)


def attend_suffix(queries, keys, values, request, position):
    row_count, columns = queries.shape
    head_count = columns // HEAD
    blocks = split_blocks(row_count)
    block_len = row_count // blocks
    scaling = 1.0 / math.sqrt(HEAD)
    key_grid = keys.reshape(row_count, head_count, HEAD)
    val_grid = values.reshape(row_count, head_count, HEAD)

    def per_block(pieces):
        block_q, block_req, block_pos = pieces
        query_grid = block_q.reshape(block_len, head_count, HEAD)
        scores = (
            jnp.einsum("qhd,khd->hqk", query_grid, key_grid, preferred_element_type=jnp.float32)
            * scaling
        )
        allowed = (request[None, :] == block_req[:, None]) & (
            position[None, :] <= block_pos[:, None]
        )
        scores = jnp.where(allowed[None, :, :], scores, NEG)
        maxima = jnp.max(scores, axis=2)
        exp_terms = jnp.exp(scores - maxima[:, :, None])
        totals = jnp.sum(exp_terms, axis=2)
        weighted = jnp.einsum(
            "hqk,khd->qhd",
            exp_terms.astype(jnp.bfloat16),
            val_grid,
            preferred_element_type=jnp.float32,
        )
        return (weighted.reshape(block_len, columns), maxima.T, totals.T)

    weighted, maxima, totals = lax.map(
        per_block,
        (
            queries.reshape(blocks, block_len, columns),
            request.reshape(blocks, block_len),
            position.reshape(blocks, block_len),
        ),
    )
    return (
        weighted.reshape(row_count, columns),
        maxima.reshape(row_count, head_count),
        totals.reshape(row_count, head_count),
    )


def attend_suffix_rows(query_rows, query_req, query_pos, keys, values, request, position):
    scaling = 1.0 / math.sqrt(HEAD)
    scores = jnp.dot(query_rows, keys.T, preferred_element_type=jnp.float32) * scaling
    allowed = (request[None, :] == query_req[:, None]) & (position[None, :] <= query_pos[:, None])
    scores = jnp.where(allowed, scores, NEG)
    maxima = jnp.max(scores, axis=1, keepdims=True)
    exp_terms = jnp.exp(scores - maxima)
    totals = jnp.sum(exp_terms, axis=1, keepdims=True)
    weighted = jnp.dot(exp_terms.astype(jnp.bfloat16), values, preferred_element_type=jnp.float32)
    return (weighted, maxima, totals)


def combine(former, latter):
    weighted_a, maxima_a, totals_a = former
    weighted_b, maxima_b, totals_b = latter
    row_count, head_count = maxima_a.shape
    maxima = jnp.maximum(maxima_a, maxima_b)
    factor_a = jnp.exp(maxima_a - maxima)
    factor_b = jnp.exp(maxima_b - maxima)
    weighted = (
        weighted_a.reshape(row_count, head_count, HEAD) * factor_a[:, :, None]
        + weighted_b.reshape(row_count, head_count, HEAD) * factor_b[:, :, None]
    )
    return (
        weighted.reshape(row_count, head_count * HEAD),
        maxima,
        totals_a * factor_a + totals_b * factor_b,
    )


def per_device(
    queries,
    keys,
    values,
    prefix_keys,
    prefix_values,
    lengths,
    groups,
    residual,
    out_proj,
    norm_gain,
    expert_ids,
    expert_gates,
    w_gate,
    w_up,
    w_down,
):
    row_tok, columns = queries.shape
    head_count = columns // HEAD
    tok_dev = residual.shape[0]
    request, position, tok_group = token_layout(lengths, groups)
    request, position, tok_group = (request[0], position[0], tok_group[0])
    req_count = lax.axis_size("req")
    local_kv = jnp.stack([prefix_keys, prefix_values])
    partner = [(i, i ^ 1) for i in range(req_count)]
    partner_kv = lax.ppermute(local_kv, "req", partner)
    ring_parts = [
        lax.ppermute(local_kv, "req", [(i, (i + 2 * s) % req_count) for i in range(req_count)])
        for s in range(1, req_count // 2)
    ]
    padded_index, source, block_group = group_layout(tok_group)
    padded_rows = jnp.dot(
        source.astype(jnp.bfloat16), queries, preferred_element_type=jnp.float32
    ).astype(jnp.bfloat16)
    suffix_part = attend_suffix_rows(
        padded_rows,
        jnp.sum(jnp.where(source, request[None, :], 0), axis=1),
        jnp.sum(jnp.where(source, position[None, :], 0), axis=1),
        keys,
        values,
        request,
        position,
    )
    ring_parts, suffix_part = lax.optimization_barrier((ring_parts, suffix_part))
    ring_kv = jnp.concatenate(ring_parts, axis=2)
    forwarded_kv = lax.ppermute(ring_kv, "req", partner)
    prefix_part = attend_prefix_grouped(
        padded_rows, block_group, local_kv, ring_kv, partner_kv, forwarded_kv
    )
    weighted, maxima, totals = combine(prefix_part, suffix_part)
    padded_attended = (weighted / totals).astype(jnp.bfloat16)
    back = (padded_index[:, None] == jnp.arange(padded_rows.shape[0], dtype=jnp.int32)[None, :])
    attended = jnp.dot(
        back.astype(jnp.bfloat16), padded_attended, preferred_element_type=jnp.float32
    ).astype(jnp.bfloat16)
    exp_count = lax.axis_size("exp")
    full_proj = lax.all_gather(out_proj, "exp", axis=0, tiled=True)
    token_rows = lax.all_to_all(attended, "exp", split_axis=0, concat_axis=1, tiled=True)
    projected = jnp.dot(token_rows, full_proj, preferred_element_type=jnp.float32)
    stream = residual.astype(jnp.float32) + projected
    meansq = jnp.mean(stream * stream, axis=-1, keepdims=True)
    normed = (stream * lax.rsqrt(meansq + 1e-06) * norm_gain.astype(jnp.float32)).astype(
        jnp.bfloat16
    )
    capacity = max(2, tok_dev // 4)
    slot_count = EXPERTS * capacity
    flat_ids = expert_ids.reshape(-1)
    onehot = (flat_ids[:, None] == jnp.arange(EXPERTS, dtype=jnp.int32)[None, :]).astype(jnp.int32)
    slot_of = jnp.sum(onehot * (jnp.cumsum(onehot, axis=0) - 1), axis=1)
    dest = flat_ids * capacity + slot_of
    dest_hot = dest[:, None] == jnp.arange(slot_count, dtype=jnp.int32)[None, :]
    select = jnp.sum(dest_hot.reshape(tok_dev, TOPK, slot_count).astype(jnp.float32), axis=1)
    buffer = jnp.dot(
        select.T.astype(jnp.bfloat16), normed, preferred_element_type=jnp.float32
    ).astype(jnp.bfloat16).reshape(EXPERTS, capacity, normed.shape[1])
    exp_dev = w_gate.shape[0]
    received = lax.all_to_all(buffer, "exp", split_axis=0, concat_axis=0, tiled=True)
    slots = received.shape[1]
    width = received.shape[2]
    rows = jnp.swapaxes(received.reshape(exp_count, exp_dev, slots, width), 0, 1)
    expert_out = expert_ffn(rows.reshape(exp_dev, exp_count * slots, width), w_gate, w_up, w_down)
    expert_out = jnp.swapaxes(expert_out.reshape(exp_dev, exp_count, slots, width), 0, 1)
    returned = lax.all_to_all(
        expert_out.reshape(EXPERTS, slots, width),
        "exp",
        split_axis=0,
        concat_axis=0,
        tiled=True,
    )
    gates = expert_gates.astype(jnp.float32).reshape(tok_dev, TOPK, 1)
    weights = jnp.sum(dest_hot.reshape(tok_dev, TOPK, slot_count).astype(jnp.float32) * gates, axis=1)
    mixture = jnp.dot(
        weights.astype(jnp.bfloat16),
        returned.reshape(slot_count, received.shape[2]),
        preferred_element_type=jnp.float32,
    )
    return (stream + mixture).astype(jnp.bfloat16)


def solution(mesh):
    in_specs = (
        P("req", "exp"),
        P("req", "exp"),
        P("req", "exp"),
        P(None, "req", "exp"),
        P(None, "req", "exp"),
        P("req", None),
        P("req", None),
        P(("req", "exp"), None),
        P("exp", None),
        P(),
        P(("req", "exp"), None),
        P(("req", "exp"), None),
        P("exp", None, None),
        P("exp", None, None),
        P("exp", None, None),
    )
    out_specs = P(("req", "exp"), None)
    return jax.shard_map(
        per_device, mesh=mesh, in_specs=in_specs, out_specs=out_specs, check_vma=False
    )
```

```python
import math

import jax
import jax.numpy as jnp
from jax import lax
from jax.experimental import pallas as pl
from jax.experimental.pallas import tpu as pltpu
from jax.sharding import PartitionSpec as P

HEAD = 128
TOPK = 4
EXPERTS = 32
G = 4
RQ = 8
ROW_TOK = 1024


NEG = -1e30


def token_layout(lengths, groups):
    req_ends = jnp.cumsum(lengths, axis=-1)
    starts = req_ends - lengths
    position = jnp.arange(ROW_TOK, dtype=jnp.int32)
    request = jnp.sum((position[None, :, None] >= req_ends[:, None, :]).astype(jnp.int32), axis=-1)
    onehot = request[:, :, None] == jnp.arange(RQ, dtype=jnp.int32)[None, None, :]
    first_tok = jnp.sum(jnp.where(onehot, starts[:, None, :], 0), axis=-1)
    tok_group = jnp.sum(jnp.where(onehot, groups[:, None, :], 0), axis=-1)
    return (request, position[None, :] - first_tok, tok_group)


def split_blocks(row_count):
    if row_count % 1024 == 0 and row_count > 1024:
        return row_count // 1024
    return 1


def pack_parts(parts):
    return jnp.concatenate([parts[0], parts[1], parts[2]], axis=1)


def unpack_parts(packed, head_count):
    columns = head_count * HEAD
    return (
        packed[:, :columns],
        packed[:, columns : columns + head_count],
        packed[:, columns + head_count :],
    )


def attend_prefix(query_rows, query_group, prefix_k, prefix_v):
    row_count, columns = query_rows.shape
    head_count = columns // HEAD
    span = prefix_k.shape[1]
    key_grid = prefix_k.reshape(G, span, head_count, HEAD)
    val_grid = prefix_v.reshape(G, span, head_count, HEAD)
    blocks = split_blocks(row_count)
    block_len = row_count // blocks
    scaling = 1.0 / math.sqrt(HEAD)

    def per_block(pieces):
        block_q, block_g = pieces
        query_grid = block_q.reshape(block_len, head_count, HEAD)
        scores = (
            jnp.einsum("qhd,gkhd->hqgk", query_grid, key_grid, preferred_element_type=jnp.float32)
            * scaling
        )
        member = block_g[:, None] == jnp.arange(G, dtype=jnp.int32)[None, :]
        scores = jnp.where(member[None, :, :, None], scores, NEG)
        maxima = jnp.max(scores, axis=(2, 3))
        exp_terms = jnp.exp(scores - maxima[:, :, None, None])
        totals = jnp.sum(exp_terms, axis=(2, 3))
        weighted = jnp.einsum(
            "hqgk,gkhd->qhd",
            exp_terms.astype(jnp.bfloat16),
            val_grid,
            preferred_element_type=jnp.float32,
        )
        return (weighted.reshape(block_len, columns), maxima.T, totals.T)

    weighted, maxima, totals = lax.map(
        per_block,
        (query_rows.reshape(blocks, block_len, columns), query_group.reshape(blocks, block_len)),
    )
    return (
        weighted.reshape(row_count, columns),
        maxima.reshape(row_count, head_count),
        totals.reshape(row_count, head_count),
    )


QUERY_BLOCK = 256
KEY_BLOCK = 2048


def prefix_kernel(block_group_ref, q_ref, *refs):
    scaling = 1.0 / math.sqrt(HEAD)
    acc_ref, m_ref, l_ref = refs[-3:]
    pieces = refs[:-3]
    q = q_ref[...]
    contract = (((1,), (1,)), ((), ()))
    scores = [
        lax.dot_general(q, pieces[i][0, 0], contract, preferred_element_type=jnp.float32) * scaling
        for i in range(0, len(pieces), 2)
    ]
    m = scores[0].max(axis=1, keepdims=True)
    for s in scores[1:]:
        m = jnp.maximum(m, s.max(axis=1, keepdims=True))
    acc = None
    total = None
    for i, s in enumerate(scores):
        p = jnp.exp(s - m)
        term = jnp.dot(p.astype(jnp.bfloat16), pieces[2 * i + 1][0, 0], preferred_element_type=jnp.float32)
        acc = term if acc is None else acc + term
        row_sum = jnp.sum(p, axis=1, keepdims=True)
        total = row_sum if total is None else total + row_sum
    acc_ref[...] = acc
    m_ref[...] = jnp.broadcast_to(m, m_ref.shape)
    l_ref[...] = jnp.broadcast_to(total, l_ref.shape)


def group_layout(query_group):
    row_count = query_group.shape[0]
    block_count = row_count // QUERY_BLOCK + G - 1
    member = query_group[:, None] == jnp.arange(G, dtype=jnp.int32)[None, :]
    counts = jnp.sum(member.astype(jnp.int32), axis=0)
    blocks = (counts + QUERY_BLOCK - 1) // QUERY_BLOCK
    first_block = jnp.cumsum(blocks) - blocks
    rank = jnp.sum(jnp.where(member, jnp.cumsum(member.astype(jnp.int32), axis=0) - 1, 0), axis=1)
    padded_index = jnp.sum(jnp.where(member, first_block[None, :], 0), axis=1) * QUERY_BLOCK + rank
    source = jnp.arange(block_count * QUERY_BLOCK, dtype=jnp.int32)[:, None] == padded_index[None, :]
    block_group = jnp.sum(
        (jnp.arange(block_count, dtype=jnp.int32)[:, None] >= first_block[None, 1:]).astype(jnp.int32),
        axis=1,
    )
    return padded_index, source, block_group


def attend_prefix_grouped(padded_rows, block_group, *kv_list):
    padded_count = padded_rows.shape[0]
    block_count = padded_count // QUERY_BLOCK
    row_spec = pl.BlockSpec((QUERY_BLOCK, HEAD), lambda b, bg: (b, 0))

    def piece_specs(kv):
        span = kv.shape[2]
        return [
            pl.BlockSpec((1, 1, span, HEAD), lambda b, bg: (0, bg[b], 0, 0)),
            pl.BlockSpec((1, 1, span, HEAD), lambda b, bg: (1, bg[b], 0, 0)),
        ]

    span = sum(kv.shape[2] for kv in kv_list)
    out_shape = jax.ShapeDtypeStruct((padded_count, HEAD), jnp.float32)
    acc, maxima, totals = pl.pallas_call(
        prefix_kernel,
        grid_spec=pltpu.PrefetchScalarGridSpec(
            num_scalar_prefetch=1,
            grid=(block_count,),
            in_specs=[row_spec] + [spec for kv in kv_list for spec in piece_specs(kv)],
            out_specs=[row_spec] * 3,
        ),
        out_shape=[out_shape] * 3,
        compiler_params=pltpu.CompilerParams(dimension_semantics=("arbitrary",)),
        cost_estimate=pl.CostEstimate(
            flops=4 * padded_count * span * HEAD,
            transcendentals=padded_count * span,
            bytes_accessed=2 * G * span * HEAD * 2 + padded_count * HEAD * 14,
        ),
    )(block_group, padded_rows, *[kv for kv in kv_list for _ in range(2)])
    return (acc, maxima[:, :1], totals[:, :1])


def expert_kernel(x_ref, wg_ref, wu_ref, wd_ref, o_ref, total):
    f = pl.program_id(1)

    @pl.when(f == 0)
    def _():
        total[...] = jnp.zeros_like(total)

    x_t = x_ref[0]
    gate_t = jnp.dot(wg_ref[0], x_t, preferred_element_type=jnp.float32)
    up_t = jnp.dot(wu_ref[0], x_t, preferred_element_type=jnp.float32)
    hidden = (gate_t / (1.0 + jnp.exp(-gate_t)) * up_t).T.astype(jnp.bfloat16)
    total[...] += jnp.dot(hidden, wd_ref[0], preferred_element_type=jnp.float32)

    @pl.when(f == pl.num_programs(1) - 1)
    def _():
        o_ref[0] = total[...].astype(o_ref.dtype)


FE_CHUNK = 176


def expert_ffn(rows, w_gate, w_up, w_down):
    exp_dev, row_count, width = rows.shape
    inner = w_gate.shape[2]
    chunk = FE_CHUNK if inner % FE_CHUNK == 0 else inner
    gate_t = jnp.swapaxes(w_gate, 1, 2)
    up_t = jnp.swapaxes(w_up, 1, 2)
    return pl.pallas_call(
        expert_kernel,
        grid=(exp_dev, inner // chunk),
        in_specs=[
            pl.BlockSpec((1, width, row_count), lambda e, f: (e, 0, 0)),
            pl.BlockSpec((1, chunk, width), lambda e, f: (e, f, 0)),
            pl.BlockSpec((1, chunk, width), lambda e, f: (e, f, 0)),
            pl.BlockSpec((1, chunk, width), lambda e, f: (e, f, 0)),
        ],
        out_specs=pl.BlockSpec((1, row_count, width), lambda e, f: (e, 0, 0)),
        out_shape=jax.ShapeDtypeStruct((exp_dev, row_count, width), jnp.bfloat16),
        scratch_shapes=[pltpu.VMEM((row_count, width), jnp.float32)],
        compiler_params=pltpu.CompilerParams(dimension_semantics=("arbitrary", "arbitrary")),
        cost_estimate=pl.CostEstimate(
            flops=6 * exp_dev * row_count * width * inner,
            transcendentals=exp_dev * row_count * inner,
            bytes_accessed=exp_dev * (3 * width * inner + 2 * row_count * width) * 2,
        ),
    )(jnp.swapaxes(rows, 1, 2), gate_t, up_t, w_down)


def attend_suffix(queries, keys, values, request, position):
    row_count, columns = queries.shape
    head_count = columns // HEAD
    blocks = split_blocks(row_count)
    block_len = row_count // blocks
    scaling = 1.0 / math.sqrt(HEAD)
    key_grid = keys.reshape(row_count, head_count, HEAD)
    val_grid = values.reshape(row_count, head_count, HEAD)

    def per_block(pieces):
        block_q, block_req, block_pos = pieces
        query_grid = block_q.reshape(block_len, head_count, HEAD)
        scores = (
            jnp.einsum("qhd,khd->hqk", query_grid, key_grid, preferred_element_type=jnp.float32)
            * scaling
        )
        allowed = (request[None, :] == block_req[:, None]) & (
            position[None, :] <= block_pos[:, None]
        )
        scores = jnp.where(allowed[None, :, :], scores, NEG)
        maxima = jnp.max(scores, axis=2)
        exp_terms = jnp.exp(scores - maxima[:, :, None])
        totals = jnp.sum(exp_terms, axis=2)
        weighted = jnp.einsum(
            "hqk,khd->qhd",
            exp_terms.astype(jnp.bfloat16),
            val_grid,
            preferred_element_type=jnp.float32,
        )
        return (weighted.reshape(block_len, columns), maxima.T, totals.T)

    weighted, maxima, totals = lax.map(
        per_block,
        (
            queries.reshape(blocks, block_len, columns),
            request.reshape(blocks, block_len),
            position.reshape(blocks, block_len),
        ),
    )
    return (
        weighted.reshape(row_count, columns),
        maxima.reshape(row_count, head_count),
        totals.reshape(row_count, head_count),
    )


def attend_suffix_rows(query_rows, query_req, query_pos, keys, values, request, position):
    scaling = 1.0 / math.sqrt(HEAD)
    scores = jnp.dot(query_rows, keys.T, preferred_element_type=jnp.float32) * scaling
    allowed = (request[None, :] == query_req[:, None]) & (position[None, :] <= query_pos[:, None])
    scores = jnp.where(allowed, scores, NEG)
    maxima = jnp.max(scores, axis=1, keepdims=True)
    exp_terms = jnp.exp(scores - maxima)
    totals = jnp.sum(exp_terms, axis=1, keepdims=True)
    weighted = jnp.dot(exp_terms.astype(jnp.bfloat16), values, preferred_element_type=jnp.float32)
    return (weighted, maxima, totals)


def combine(former, latter):
    weighted_a, maxima_a, totals_a = former
    weighted_b, maxima_b, totals_b = latter
    row_count, head_count = maxima_a.shape
    maxima = jnp.maximum(maxima_a, maxima_b)
    factor_a = jnp.exp(maxima_a - maxima)
    factor_b = jnp.exp(maxima_b - maxima)
    weighted = (
        weighted_a.reshape(row_count, head_count, HEAD) * factor_a[:, :, None]
        + weighted_b.reshape(row_count, head_count, HEAD) * factor_b[:, :, None]
    )
    return (
        weighted.reshape(row_count, head_count * HEAD),
        maxima,
        totals_a * factor_a + totals_b * factor_b,
    )


def per_device(
    queries,
    keys,
    values,
    prefix_keys,
    prefix_values,
    lengths,
    groups,
    residual,
    out_proj,
    norm_gain,
    expert_ids,
    expert_gates,
    w_gate,
    w_up,
    w_down,
):
    row_tok, columns = queries.shape
    head_count = columns // HEAD
    tok_dev = residual.shape[0]
    request, position, tok_group = token_layout(lengths, groups)
    request, position, tok_group = (request[0], position[0], tok_group[0])
    req_count = lax.axis_size("req")
    local_kv = jnp.stack([prefix_keys, prefix_values])
    partner = [(i, i ^ 1) for i in range(req_count)]
    partner_kv = lax.ppermute(local_kv, "req", partner)
    ring_parts = [
        lax.ppermute(local_kv, "req", [(i, (i + 2 * s) % req_count) for i in range(req_count)])
        for s in range(1, req_count // 2)
    ]
    padded_index, source, block_group = group_layout(tok_group)
    padded_rows = jnp.dot(
        source.astype(jnp.bfloat16), queries, preferred_element_type=jnp.float32
    ).astype(jnp.bfloat16)
    suffix_part = attend_suffix_rows(
        padded_rows,
        jnp.sum(jnp.where(source, request[None, :], 0), axis=1),
        jnp.sum(jnp.where(source, position[None, :], 0), axis=1),
        keys,
        values,
        request,
        position,
    )
    ring_parts, suffix_part = lax.optimization_barrier((ring_parts, suffix_part))
    forwarded_parts = [lax.ppermute(part, "req", partner) for part in ring_parts]
    prefix_part = attend_prefix_grouped(
        padded_rows, block_group, local_kv, *ring_parts, partner_kv, *forwarded_parts
    )
    weighted, maxima, totals = combine(prefix_part, suffix_part)
    padded_attended = (weighted / totals).astype(jnp.bfloat16)
    back = (padded_index[:, None] == jnp.arange(padded_rows.shape[0], dtype=jnp.int32)[None, :])
    attended = jnp.dot(
        back.astype(jnp.bfloat16), padded_attended, preferred_element_type=jnp.float32
    ).astype(jnp.bfloat16)
    exp_count = lax.axis_size("exp")
    full_proj = lax.all_gather(out_proj, "exp", axis=0, tiled=True)
    token_rows = lax.all_to_all(attended, "exp", split_axis=0, concat_axis=1, tiled=True)
    projected = jnp.dot(token_rows, full_proj, preferred_element_type=jnp.float32)
    stream = residual.astype(jnp.float32) + projected
    meansq = jnp.mean(stream * stream, axis=-1, keepdims=True)
    normed = (stream * lax.rsqrt(meansq + 1e-06) * norm_gain.astype(jnp.float32)).astype(
        jnp.bfloat16
    )
    capacity = max(2, tok_dev // 4)
    slot_count = EXPERTS * capacity
    flat_ids = expert_ids.reshape(-1)
    onehot = (flat_ids[:, None] == jnp.arange(EXPERTS, dtype=jnp.int32)[None, :]).astype(jnp.int32)
    slot_of = jnp.sum(onehot * (jnp.cumsum(onehot, axis=0) - 1), axis=1)
    dest = flat_ids * capacity + slot_of
    dest_hot = dest[:, None] == jnp.arange(slot_count, dtype=jnp.int32)[None, :]
    select = jnp.sum(dest_hot.reshape(tok_dev, TOPK, slot_count).astype(jnp.float32), axis=1)
    buffer = jnp.dot(
        select.T.astype(jnp.bfloat16), normed, preferred_element_type=jnp.float32
    ).astype(jnp.bfloat16).reshape(EXPERTS, capacity, normed.shape[1])
    exp_dev = w_gate.shape[0]
    received = lax.all_to_all(buffer, "exp", split_axis=0, concat_axis=0, tiled=True)
    slots = received.shape[1]
    width = received.shape[2]
    rows = jnp.swapaxes(received.reshape(exp_count, exp_dev, slots, width), 0, 1)
    expert_out = expert_ffn(rows.reshape(exp_dev, exp_count * slots, width), w_gate, w_up, w_down)
    expert_out = jnp.swapaxes(expert_out.reshape(exp_dev, exp_count, slots, width), 0, 1)
    returned = lax.all_to_all(
        expert_out.reshape(EXPERTS, slots, width),
        "exp",
        split_axis=0,
        concat_axis=0,
        tiled=True,
    )
    gates = expert_gates.astype(jnp.float32).reshape(tok_dev, TOPK, 1)
    weights = jnp.sum(dest_hot.reshape(tok_dev, TOPK, slot_count).astype(jnp.float32) * gates, axis=1)
    mixture = jnp.dot(
        weights.astype(jnp.bfloat16),
        returned.reshape(slot_count, received.shape[2]),
        preferred_element_type=jnp.float32,
    )
    return (stream + mixture).astype(jnp.bfloat16)


def solution(mesh):
    in_specs = (
        P("req", "exp"),
        P("req", "exp"),
        P("req", "exp"),
        P(None, "req", "exp"),
        P(None, "req", "exp"),
        P("req", None),
        P("req", None),
        P(("req", "exp"), None),
        P("exp", None),
        P(),
        P(("req", "exp"), None),
        P(("req", "exp"), None),
        P("exp", None, None),
        P("exp", None, None),
        P("exp", None, None),
    )
    out_specs = P(("req", "exp"), None)
    return jax.shard_map(
        per_device, mesh=mesh, in_specs=in_specs, out_specs=out_specs, check_vma=False
    )
```
